32 devices in a mesh: rep: 4 (over x, core), fsdp: 8 (over z, y).
Axes of the slice: x: 2, y: 2, z: 4, core: 2. Of those that a mesh axis runs over, the one named last changes fastest.
Arguments:
- hidden_in: bfloat16 [16384, 1024], P(('rep', 'fsdp')), may hold values from -6 to 6
- seg_ids: int32 [16384], P(('rep', 'fsdp')), may hold values from 0 to 127, never falling along the last dimension, each value on 1 to 4096 neighbouring positions
- attn_gain: bfloat16 [1024], P('fsdp'), may hold values from 0.5 to 1.5
- qkv_weight: bfloat16 [1024, 3072], P('fsdp'), may hold values from -0.1875 to 0.1875
- beta_weight: bfloat16 [1024, 8], P('fsdp'), may hold values from -0.1875 to 0.1875
- gate_weight: bfloat16 [1024, 1024], P('fsdp'), may hold values from -0.1875 to 0.1875
- conv_taps: bfloat16 [4, 3072], P(None, 'fsdp'), may hold values from -3 to 3
- out_gain: bfloat16 [128], P('fsdp'), may hold values from 0.5 to 1.5
- out_weight: bfloat16 [1024, 1024], P('fsdp'), may hold values from -0.375 to 0.375
- ffn_gain: bfloat16 [1024], P('fsdp'), may hold values from 0.5 to 1.5
- ffn_gate: bfloat16 [1024, 2816], P('fsdp'), may hold values from -0.1875 to 0.1875
- ffn_up: bfloat16 [1024, 2816], P('fsdp'), may hold values from -0.1875 to 0.1875
- ffn_down: bfloat16 [2816, 1024], P('fsdp'), may hold values from -0.109375 to 0.109375
- cotangent: bfloat16 [16384, 1024], P(('rep', 'fsdp')), may hold values from -6 to 6
Outputs:
- output: bfloat16 [16384, 1024], P(('rep', 'fsdp'))
- input_grad: bfloat16 [16384, 1024], P(('rep', 'fsdp'))
- attngain_grad: float32 [1024], P('fsdp')
- qkv_grad: float32 [1024, 3072], P('fsdp')
- beta_grad: float32 [1024, 8], P('fsdp')
- gate_grad: float32 [1024, 1024], P('fsdp')
- taps_grad: float32 [4, 3072], P(None, 'fsdp')
- outgain_grad: float32 [128], P('fsdp')
- outproj_grad: float32 [1024, 1024], P('fsdp')
- ffngain_grad: float32 [1024], P('fsdp')
- hidgate_grad: float32 [1024, 2816], P('fsdp')
- hidup_grad: float32 [1024, 2816], P('fsdp')
- down_grad: float32 [2816, 1024], P('fsdp')
The draws below stay inside these ranges and needn't reach their ends.
Inputs may be any that keep to these rules, and one draw needn't show every extreme that they name: `seg_ids`: segment ids never fall along the array; each segment covers 1 to 4096 consecutive positions and one covers exactly 4096.
All inputs are finite; a program needn't handle non-finite values.
Results may differ from the reference program's by a relative error of at most 0.022.
Values may be sent and summed in bfloat16 or wider, within the bound.
No kernel may reach another device: no remote copies, remote signals or barrier semaphores. Data moves between devices by JAX's collectives and lax.ppermute only.
A program may use at most 256 MiB of HBM per device.

```python
import math
from functools import partial
import jax
import jax.numpy as jnp
import numpy as np
from jax import lax

D = 1024
H = 8
DK = 128
FF = 2816
SPAN = 64
GROUP_TOK = 4096
TOKENS = 16384
DOC_MOST = 4096
DOC_COUNT = 128
N_REP = 4


def block_scale(own_key, extent, cuts, least, high):
    level = 1.0
    for axis_at, parts in cuts:
        draws = jax.random.uniform(jax.random.fold_in(jax.random.fold_in(own_key, 6), axis_at), (parts,), jnp.float32, least / len(cuts), high / len(cuts))
        level = level * jnp.repeat(jnp.exp(draws), extent[axis_at] // parts).reshape((-1,) + (1,) * (len(extent) - 1 - axis_at))
    return level


def length_profile(count, total, most, skew):
    weights = [(1 << 20) // math.isqrt(grade ** skew) + 1 for grade in range(2, count + 1)]
    spare, holding = total - most - (count - 1), [1] * (count - 1)
    while spare > 0:
        free = [i for i in range(count - 1) if holding[i] < most]
        whole, budget = sum([weights[i] for i in free]), spare
        for i in free:
            addition = min(most - holding[i], max(1, budget * weights[i] // whole), spare)
            holding[i] = holding[i] + addition
            spare = spare - addition
    return np.array([most] + holding)


def uneven_parts(rng, amount, total, most, slope):
    if amount == 2:
        one = jax.random.randint(rng, (), max(1, total - most), min(most, total - 1) + 1)
        return jnp.stack([one, total - one])
    sizes = jnp.asarray(length_profile(amount, total, most, slope), jnp.int32)
    twos = (amount - 1) // 2
    donor, receiver = sizes[1:1 + 2 * twos:2], sizes[2:2 + 2 * twos:2]
    slack = jnp.minimum(donor - 1, most - receiver)
    moved = jax.random.randint(jax.random.fold_in(rng, 1), (twos,), 0, 1 << 20) % (slack + 1)
    sizes = sizes.at[1:1 + 2 * twos:2].set(donor - moved).at[2:2 + 2 * twos:2].set(receiver + moved)
    return sizes[jax.random.permutation(jax.random.fold_in(rng, 2), amount)]


def noise(key, shape, scale, bound, split=(), held_as=jnp.bfloat16):
    entries = jax.random.normal(key, shape, jnp.float32) * scale
    if len(split) > 0:
        entries = block_scale(key, shape, split, -0.22, 0.18) * entries
    return jnp.clip(entries, min=-bound, max=bound).astype(held_as)


def setup_inputs(seed: int = 0) -> dict:
    splits = jax.random.split(jax.random.key(seed), 15)
    hidden_in = noise(splits[0], (TOKENS, D), 1.0, 6.0, ((0, 32),))
    seg_ids = jnp.searchsorted(jnp.cumsum(uneven_parts(splits[1], DOC_COUNT, TOKENS, DOC_MOST, 2)), jnp.arange(TOKENS), side="right").astype(jnp.int32)
    attn_gain = jnp.clip(1.0 + 0.1 * jax.random.normal(splits[2], (D,), jnp.float32), 0.5, 1.5).astype(jnp.bfloat16)
    qkv_weight = noise(splits[3], (D, 3 * D), D ** -0.5, 0.1875, ((0, 8),))
    beta_weight = noise(splits[4], (D, H), D ** -0.5, 0.1875, ((0, 8),))
    gate_weight = noise(splits[5], (D, D), D ** -0.5, 0.1875, ((0, 8),))
    conv_taps = noise(splits[6], (4, 3 * D), 4 ** -0.5, 3.0, ((1, 8),))
    out_gain = jnp.clip(1.0 + 0.1 * jax.random.normal(splits[7], (DK,), jnp.float32), 0.5, 1.5).astype(jnp.bfloat16)
    out_weight = noise(splits[8], (D, D), (D // 4) ** -0.5, 0.375, ((0, 8),))
    ffn_gain = jnp.clip(1.0 + 0.1 * jax.random.normal(splits[9], (D,), jnp.float32), 0.5, 1.5).astype(jnp.bfloat16)
    ffn_gate = noise(splits[10], (D, FF), D ** -0.5, 0.1875, ((0, 8),))
    ffn_up = noise(splits[11], (D, FF), D ** -0.5, 0.1875, ((0, 8),))
    ffn_down = noise(splits[12], (FF, D), FF ** -0.5, 0.109375, ((0, 8),))
    cotangent = noise(splits[13], (TOKENS, D), 1.0, 6.0, ((0, 32),))
    return dict(hidden_in=hidden_in, seg_ids=seg_ids, attn_gain=attn_gain, qkv_weight=qkv_weight, beta_weight=beta_weight, gate_weight=gate_weight, conv_taps=conv_taps, out_gain=out_gain, out_weight=out_weight, ffn_gain=ffn_gain, ffn_gate=ffn_gate, ffn_up=ffn_up, ffn_down=ffn_down, cotangent=cotangent)


EPSILON = 1e-06
HIGH = lax.Precision.HIGHEST

@jax.custom_vjp
def low(v):
    return lax.optimization_barrier(v.astype(jnp.bfloat16)).astype(jnp.float32)

@jax.custom_vjp
def low_back(v):
    return v

def low_keep(v):
    return (low(v), None)

def low_pass(kept, grad):
    return (grad,)

def back_keep(v):
    return (v, None)

def back_low(kept, grad):
    return (low(grad),)
low.defvjp(low_keep, low_pass)
low_back.defvjp(back_keep, back_low)

def hi_einsum(form, left, right):
    return jnp.einsum(form, left, right, precision=HIGH, preferred_element_type=jnp.float32)

def matmul_hi(left, right):
    return jnp.dot(left, right, precision=HIGH, preferred_element_type=jnp.float32)

def rms_norm(values, gain):
    return values * lax.rsqrt(lax.optimization_barrier(jnp.mean(values * values, axis=-1, keepdims=True)) + EPSILON) * gain

def span_step(carried, pieces):
    queries, key_unit, values, rates, starts = pieces
    queries = queries.astype(jnp.float32)
    key_unit = key_unit.astype(jnp.float32)
    values = values.astype(jnp.float32)
    block_len = starts.shape[-1]
    row_ids = lax.broadcasted_iota(jnp.int32, (block_len, block_len), 0)
    col_ids = lax.broadcasted_iota(jnp.int32, (block_len, block_len), 1)
    causal = (row_ids >= col_ids).astype(jnp.float32)
    strict = (row_ids > col_ids).astype(jnp.float32)
    doc_index = hi_einsum('...s,ts->...t', starts, causal)
    first_doc = (doc_index < 0.5).astype(jnp.float32)
    last_doc = (doc_index > doc_index[..., -1:] - 0.5).astype(jnp.float32)
    same_doc = (jnp.abs(doc_index[..., :, None] - doc_index[..., None, :]) < 0.5).astype(jnp.float32)
    keep_state = first_doc[..., -1]
    query_heads = jnp.swapaxes(queries, -2, -3)
    key_heads = jnp.swapaxes(key_unit, -2, -3)
    value_heads = jnp.swapaxes(values, -2, -3)
    rate_heads = jnp.swapaxes(rates, -1, -2)[..., None]
    lower = (strict * same_doc)[..., None, :, :]
    mixing = hi_einsum('...td,...sd->...ts', key_heads * rate_heads, key_heads) * lower
    unit_matrix = jnp.eye(block_len, dtype=jnp.float32)
    inverse = unit_matrix - mixing
    powered = mixing
    for level in range(block_len.bit_length() - 2):
        powered = hi_einsum('...ts,...su->...tu', powered, powered)
        inverse = hi_einsum('...ts,...su->...tu', inverse, unit_matrix + powered)
    key_mix = low(hi_einsum('...ts,...sd->...td', inverse, key_heads * rate_heads))
    value_mix = low(hi_einsum('...ts,...sd->...td', inverse, value_heads * rate_heads))
    carried_low = low(carried)
    head_first = first_doc[..., None, :, None]
    fresh_values = low(value_mix - head_first * hi_einsum('...td,...de->...te', key_mix, carried_low))
    carried_next = keep_state[..., None, None, None] * carried + hi_einsum('...td,...te->...de', key_heads * last_doc[..., None, :, None], fresh_values)
    visible = (causal * same_doc)[..., None, :, :]
    scores = low(hi_einsum('...td,...sd->...ts', query_heads, key_heads) * visible)
    outputs = head_first * hi_einsum('...td,...de->...te', query_heads, carried_low) + hi_einsum('...ts,...se->...te', scores, fresh_values)
    return (carried_next, jnp.swapaxes(outputs, -2, -3))

def delta_rule(queries, key_unit, values, rates, starts):
    blocks = GROUP_TOK // SPAN

    def to_blocks(array):
        shaped = array.reshape((N_REP, blocks, SPAN) + array.shape[1:])
        return jnp.swapaxes(shaped, 0, 1)
    pieces = (to_blocks(queries), to_blocks(key_unit), to_blocks(values), to_blocks(rates), to_blocks(starts))
    carried = jnp.zeros((N_REP, H, DK, DK), jnp.float32)
    final_state, outputs = lax.scan(jax.checkpoint(span_step), carried, pieces)
    return jnp.swapaxes(outputs, 0, 1).reshape(TOKENS, H, DK)

def forward(hidden, attn_gain, qkv_weight, beta_weight, gate_weight, conv_taps, out_gain, out_weight, ffn_gain, ffn_gate, ffn_up, ffn_down, starts, masks):
    normed = low(rms_norm(hidden, attn_gain))
    mixed_pre = low_back(matmul_hi(normed, qkv_weight))
    beta_pre = low_back(matmul_hi(normed, beta_weight))
    gate_pre = low_back(matmul_hi(normed, gate_weight))
    mixed = conv_taps[0] * mixed_pre * masks[0]
    for offset in range(1, 4):
        shifted = jnp.concatenate([jnp.zeros((offset, 3 * D), jnp.float32), mixed_pre[:TOKENS - offset]], axis=0)
        mixed = mixed + conv_taps[offset] * shifted * masks[offset]
    active = jax.nn.silu(mixed)
    queries = low(active[:, :D] * DK ** (-0.5)).reshape(TOKENS, H, DK)
    key_raw = active[:, D:2 * D].reshape(TOKENS, H, DK)
    key_unit = low(key_raw * lax.rsqrt(lax.optimization_barrier(jnp.sum(key_raw * key_raw, axis=-1, keepdims=True)) + EPSILON))
    values = low(active[:, 2 * D:]).reshape(TOKENS, H, DK)
    rates = jax.nn.sigmoid(beta_pre)
    attn_heads = delta_rule(queries, key_unit, values, rates, starts)
    gated = low(rms_norm(attn_heads, out_gain).reshape(TOKENS, D) * jax.nn.silu(gate_pre))
    middle = hidden + low_back(matmul_hi(gated, out_weight))
    normed_two = low(rms_norm(middle, ffn_gain))
    up_gate = low_back(matmul_hi(normed_two, ffn_gate))
    up_lin = low_back(matmul_hi(normed_two, ffn_up))
    hidden_ff = low(jax.nn.silu(up_gate) * up_lin)
    return middle + low_back(matmul_hi(hidden_ff, ffn_down))

def reference(hidden_in, seg_ids, attn_gain, qkv_weight, beta_weight, gate_weight, conv_taps, out_gain, out_weight, ffn_gain, ffn_gate, ffn_up, ffn_down, cotangent):
    positions = jnp.arange(TOKENS, dtype=jnp.int32)
    previous = jnp.concatenate([seg_ids[:1], seg_ids[:-1]])
    start_flags = jnp.logical_or(positions % GROUP_TOK == 0, seg_ids != previous)
    doc_number = jnp.cumsum(start_flags.astype(jnp.int32)).astype(jnp.int32)
    masks = []
    for offset in range(4):
        earlier = jnp.concatenate([jnp.full((offset,), -1, jnp.int32), doc_number[:TOKENS - offset]])
        masks.append((earlier == doc_number).astype(jnp.float32)[:, None])
    starts = start_flags.astype(jnp.float32)
    flow = partial(forward, starts=starts, masks=masks)
    result, backward = jax.vjp(flow, hidden_in.astype(jnp.float32), attn_gain.astype(jnp.float32), qkv_weight.astype(jnp.float32), beta_weight.astype(jnp.float32), gate_weight.astype(jnp.float32), conv_taps.astype(jnp.float32), out_gain.astype(jnp.float32), out_weight.astype(jnp.float32), ffn_gain.astype(jnp.float32), ffn_gate.astype(jnp.float32), ffn_up.astype(jnp.float32), ffn_down.astype(jnp.float32))
    grads = backward(cotangent.astype(jnp.float32))
    return (result.astype(jnp.bfloat16), grads[0].astype(jnp.bfloat16), grads[1], grads[2], grads[3], grads[4], grads[5], grads[6], grads[7], grads[8], grads[9], grads[10], grads[11])
```

```python
from functools import partial

import jax
import jax.numpy as jnp
from jax import lax
from jax.experimental import pallas as pl
from jax.experimental.pallas import tpu as pltpu
from jax.sharding import PartitionSpec as P

SPAN = 64
EPSILON = 1e-06
BF = jnp.bfloat16
F32 = jnp.float32


def nn(a, b):
    return lax.dot_general(a, b, (((1,), (0,)), ((), ())), preferred_element_type=F32)


def nt(a, b):
    return lax.dot_general(a, b, (((1,), (1,)), ((), ())), preferred_element_type=F32)


def tn(a, b):
    return lax.dot_general(a, b, (((0,), (0,)), ((), ())), preferred_element_type=F32)


def block_masks(cols_ref, rows_ref, heads):
    n = SPAN
    row = lax.broadcasted_iota(jnp.int32, (n, n), 0)
    col = lax.broadcasted_iota(jnp.int32, (n, n), 1)
    ids = cols_ref[:, heads : heads + 1]
    ids_row = rows_ref[0, heads : heads + 1, :]
    before = rows_ref[0, heads + 1 : heads + 2, :]
    end = ids_row[:, n - 1 : n]
    same = ids == ids_row
    first = (ids == before[:, :1]).astype(F32)
    last = (ids == end).astype(F32)
    keep = (end == before[:, :1]).astype(F32)
    return row, col, same, first, last, keep


def summary_kernel(heads, q_dim, k_ref, v_ref, cols_ref, rows_ref, w_ref, u_ref, a_ref, x_ref, state):
    n, d = SPAN, q_dim
    block = pl.program_id(0)

    @pl.when(block == 0)
    def _():
        r = lax.broadcasted_iota(jnp.int32, (d, 2 * d), 0)
        c = lax.broadcasted_iota(jnp.int32, (d, 2 * d), 1)
        unit = (r + d == c).astype(F32)
        for h in range(heads):
            state[h] = unit

    row, col, same, first, last, keep = block_masks(cols_ref, rows_ref, heads)
    lower = jnp.logical_and(same, row > col)
    unit = (row == col).astype(F32)
    pair = jnp.logical_and(row == col + 1, (row & 1) == 1)
    keys = [k_ref[:, h * d : (h + 1) * d] for h in range(heads)]
    mixing = []
    inverse = []
    for h in range(heads):
        m = jnp.where(lower, nt(keys[h], keys[h]) * cols_ref[:, h : h + 1], 0.0)
        mixing.append(m)
        inverse.append((unit - jnp.where(pair, m, 0.0)).astype(BF))
    size = 2
    while size < n:
        level = jnp.logical_and(
            (row // (2 * size)) == (col // (2 * size)),
            jnp.logical_and(((row // size) & 1) == 1, ((col // size) & 1) == 0),
        )
        inner = [nn(jnp.where(level, mixing[h], 0.0).astype(BF), inverse[h]).astype(BF) for h in range(heads)]
        for h in range(heads):
            inverse[h] = inverse[h] - jnp.where(level, nn(inverse[h], inner[h]), 0.0).astype(BF)
        size *= 2
    first_low = first
    for h in range(heads):
        cut = slice(h * d, (h + 1) * d)
        a_ref[h] = inverse[h]
        scaled = (inverse[h].astype(F32) * rows_ref[0, h : h + 1, :]).astype(BF)
        both = nn(scaled, jnp.concatenate([keys[h], v_ref[:, cut]], axis=1))
        w = both[:, :d].astype(BF)
        u = both[:, d:].astype(BF)
        w_ref[:, cut] = w
        u_ref[:, cut] = u
        held = state[h]
        moved = nn(w, held.astype(BF)) * first_low
        fresh = (jnp.concatenate([u.astype(F32), jnp.zeros((n, d), F32)], axis=1) - moved).astype(BF)
        key_last = (keys[h].astype(F32) * last).astype(BF)
        state[h] = keep * held + tn(key_last, fresh)

    @pl.when(block == pl.num_programs(0) - 1)
    def _():
        x_ref[...] = state[...].astype(BF)


def forward_kernel(
    heads, d, q_ref, k_ref, w_ref, u_ref, cols_ref, rows_ref, s_ref, gate_ref, gain_ref,
    y_ref, o_ref, e_ref, kept_ref, state,
):
    n = SPAN
    block = pl.program_id(0)

    @pl.when(block == 0)
    def _():
        state[...] = s_ref[...].astype(F32)

    row, col, same, first, last, keep = block_masks(cols_ref, rows_ref, heads)
    visible = jnp.logical_and(same, row >= col)
    for h in range(heads):
        cut = slice(h * d, (h + 1) * d)
        q, k, w = q_ref[:, cut], k_ref[:, cut], w_ref[:, cut]
        held = state[h]
        held_low = held.astype(BF)
        kept_ref[0, h] = held_low
        both = nn(jnp.concatenate([w, q], axis=0), held_low)
        fresh = (u_ref[:, cut].astype(F32) - first * both[:n]).astype(BF)
        e_ref[:, cut] = fresh
        scores = jnp.where(visible, nt(q, k), 0.0).astype(BF)
        out = first * both[n:] + nn(scores, fresh)
        key_last = (k.astype(F32) * last).astype(BF)
        state[h] = keep * held + tn(key_last, fresh)
        o_ref[:, cut] = out
        g = gate_ref[:, cut]
        root = lax.rsqrt(jnp.mean(out * out, axis=1, keepdims=True) + EPSILON)
        y_ref[:, cut] = (out * root * gain_ref[...] * (g / (1.0 + jnp.exp(-g)))).astype(BF)


def adjoint_kernel(
    heads, d, q_ref, k_ref, w_ref, cols_ref, rows_ref, dy_ref, o_ref, gate_ref, gain_ref,
    do_ref, dgate_ref, dgain_ref, ds_ref, state,
):
    n = SPAN
    step = pl.program_id(0)

    @pl.when(step == 0)
    def _():
        state[...] = jnp.zeros_like(state)
        dgain_ref[...] = jnp.zeros_like(dgain_ref)

    row, col, same, first, last, keep = block_masks(cols_ref, rows_ref, heads)
    visible = jnp.logical_and(same, row >= col)
    gain = gain_ref[...]
    gain_sum = jnp.zeros((1, d), F32)
    for h in range(heads):
        cut = slice(h * d, (h + 1) * d)
        q, k, w = q_ref[:, cut], k_ref[:, cut], w_ref[:, cut]
        o, g, dy = o_ref[:, cut], gate_ref[:, cut], dy_ref[:, cut]
        root = lax.rsqrt(jnp.mean(o * o, axis=1, keepdims=True) + EPSILON)
        unit = o * root
        sig = 1.0 / (1.0 + jnp.exp(-g))
        m = g * sig
        t = dy * m
        gain_sum = gain_sum + jnp.sum(t * unit, axis=0, keepdims=True)
        tg = t * gain
        do = root * (tg - unit * jnp.mean(tg * unit, axis=1, keepdims=True))
        dgate_ref[:, cut] = (dy * gain * unit * (sig * (1.0 + g * (1.0 - sig)))).astype(BF)
        do_low = do.astype(BF)
        do_ref[:, cut] = do_low
        scores = jnp.where(visible, nt(q, k), 0.0).astype(BF)
        later = state[h]
        de = last * nn(k, later.astype(BF)) + tn(scores, do_low)
        left = jnp.concatenate([q.astype(F32) * first, w.astype(F32) * (-first)], axis=0).astype(BF)
        right = jnp.concatenate([do_low, de.astype(BF)], axis=0)
        state[h] = keep * later + tn(left, right)
    dgain_ref[...] += gain_sum

    @pl.when(step == pl.num_programs(0) - 1)
    def _():
        ds_ref[...] = state[...].astype(BF)


def backward_kernel(
    heads, d, q_ref, k_ref, v_ref, w_ref, u_ref, a_ref, e_ref, kept_ref, do_ref, cols_ref, rows_ref, s_ref,
    dq_ref, dk_ref, dv_ref, dr_ref, state,
):
    n = SPAN
    step = pl.program_id(0)

    @pl.when(step == 0)
    def _():
        state[...] = s_ref[...].astype(F32)

    row, col, same, first, last, keep = block_masks(cols_ref, rows_ref, heads)
    visible = jnp.logical_and(same, row >= col)
    lower = jnp.logical_and(same, row > col)
    lane = lax.broadcasted_iota(jnp.int32, (n, d), 1)
    rate_grads = jnp.zeros((n, d), F32)
    for h in range(heads):
        cut = slice(h * d, (h + 1) * d)
        q, k, v, w, u = q_ref[:, cut], k_ref[:, cut], v_ref[:, cut], w_ref[:, cut], u_ref[:, cut]
        do, e, held = do_ref[:, cut], e_ref[:, cut], kept_ref[0, h]
        rate = cols_ref[:, h : h + 1]
        later = state[h]
        later_low = later.astype(BF)
        scores = jnp.where(visible, nt(q, k), 0.0).astype(BF)
        de = last * nn(k, later_low) + tn(scores, do)
        de_low = de.astype(BF)
        dscores = jnp.where(visible, nt(do, e), 0.0).astype(BF)
        both = nt(jnp.concatenate([do, de_low], axis=0), held)
        dq_ref[:, cut] = first * both[:n] + nn(dscores, k)
        dw = -first * both[n:]
        dk = tn(dscores, q) + last * nt(e, later_low)
        pg = tn(a_ref[h], jnp.concatenate([dw.astype(BF), de_low], axis=1))
        p, g = pg[:, :d], pg[:, d:]
        dmix = jnp.where(lower, -nt(pg.astype(BF), jnp.concatenate([w, u], axis=1)), 0.0).astype(BF)
        kf = k.astype(F32)
        drk = p + nn(dmix, k)
        dk_ref[:, cut] = dk + tn(dmix, (kf * rate).astype(BF)) + rate * drk
        dv_ref[:, cut] = rate * g
        dr = jnp.sum(drk * kf + g * v.astype(F32), axis=1, keepdims=True)
        rate_grads = jnp.where(lane == h, dr, rate_grads)
        left = jnp.concatenate([q.astype(F32) * first, w.astype(F32) * (-first)], axis=0).astype(BF)
        right = jnp.concatenate([do, de_low], axis=0)
        state[h] = keep * later + tn(left, right)
    dr_ref[...] = rate_grads


def prefix_kernel(peers, x_ref, out_ref):
    cols = out_ref.shape[2]
    held = jnp.zeros(out_ref.shape[1:], F32)
    for i in range(peers):
        out_ref[i] = held.astype(BF)
        held = nn(x_ref[i, :, cols:], held.astype(BF)) + x_ref[i, :, :cols].astype(F32)


def suffix_kernel(peers, t_ref, g_ref, out_ref):
    held = jnp.zeros(out_ref.shape[1:], F32)
    cols = out_ref.shape[2]
    for i in reversed(range(peers)):
        out_ref[i] = held.astype(BF)
        held = tn(t_ref[i, :, cols:], held.astype(BF)) + g_ref[i].astype(F32)


VMEM_LIMIT = 48 * 1024 * 1024


def params():
    return pltpu.CompilerParams(dimension_semantics=("arbitrary",), vmem_limit_bytes=VMEM_LIMIT)


def specs(blocks, heads, d, flip):
    at = (lambda b: blocks - 1 - b) if flip else (lambda b: b)
    wide = pl.BlockSpec((SPAN, heads * d), lambda b: (at(b), 0))
    cols = pl.BlockSpec((SPAN, 2 * heads), lambda b: (at(b), 0))
    rows = pl.BlockSpec((1, 2 * heads, SPAN), lambda b: (at(b), 0, 0))
    state = pl.BlockSpec((heads, d, d), lambda b: (0, 0, 0))
    mix = pl.BlockSpec((heads, SPAN, SPAN), lambda b: (0, at(b), 0))
    kept = pl.BlockSpec((1, heads, d, d), lambda b: (at(b), 0, 0, 0))
    gain = pl.BlockSpec((1, d), lambda b: (0, 0))
    return wide, cols, rows, state, mix, kept, gain


def shape(dims, kind):
    return jax.ShapeDtypeStruct(dims, kind)


def delta_summary(k, v, cols, rows, heads):
    count, width = k.shape
    d, blocks = width // heads, count // SPAN
    wide, c, r, state, mix, kept, gain = specs(blocks, heads, d, False)
    return pl.pallas_call(
        partial(summary_kernel, heads, d),
        grid=(blocks,),
        in_specs=[wide, wide, c, r],
        out_specs=[wide, wide, mix, pl.BlockSpec((heads, d, 2 * d), lambda b: (0, 0, 0))],
        out_shape=[
            shape((count, width), BF),
            shape((count, width), BF),
            shape((heads, count, SPAN), BF),
            shape((heads, d, 2 * d), BF),
        ],
        scratch_shapes=[pltpu.VMEM((heads, d, 2 * d), F32)],
        compiler_params=params(),
        name="delta_summary",
    )(k, v, cols, rows)


def delta_forward(q, k, w, u, cols, rows, entry, gate, gain_full, heads):
    count, width = k.shape
    d, blocks = width // heads, count // SPAN
    wide, c, r, state, mix, kept, gain = specs(blocks, heads, d, False)
    return pl.pallas_call(
        partial(forward_kernel, heads, d),
        grid=(blocks,),
        in_specs=[wide, wide, wide, wide, c, r, state, wide, gain],
        out_specs=[wide, wide, wide, kept],
        out_shape=[
            shape((count, width), BF),
            shape((count, width), F32),
            shape((count, width), BF),
            shape((blocks, heads, d, d), BF),
        ],
        scratch_shapes=[pltpu.VMEM((heads, d, d), F32)],
        compiler_params=params(),
        name="delta_forward",
    )(q, k, w, u, cols, rows, entry, gate, gain_full)


def delta_adjoint(q, k, w, cols, rows, dy, o, gate, gain_full, heads):
    count, width = k.shape
    d, blocks = width // heads, count // SPAN
    wide, c, r, state, mix, kept, gain = specs(blocks, heads, d, True)
    return pl.pallas_call(
        partial(adjoint_kernel, heads, d),
        grid=(blocks,),
        in_specs=[wide, wide, wide, c, r, wide, wide, wide, gain],
        out_specs=[wide, wide, gain, state],
        out_shape=[
            shape((count, width), BF),
            shape((count, width), BF),
            shape((1, d), F32),
            shape((heads, d, d), BF),
        ],
        scratch_shapes=[pltpu.VMEM((heads, d, d), F32)],
        compiler_params=params(),
        name="delta_adjoint",
    )(q, k, w, cols, rows, dy, o, gate, gain_full)


def delta_backward(q, k, v, w, u, a, e, kept_states, do, cols, rows, later, heads):
    count, width = k.shape
    d, blocks = width // heads, count // SPAN
    wide, c, r, state, mix, kept, gain = specs(blocks, heads, d, True)
    return pl.pallas_call(
        partial(backward_kernel, heads, d),
        grid=(blocks,),
        in_specs=[wide, wide, wide, wide, wide, mix, wide, kept, wide, c, r, state],
        out_specs=[wide, wide, wide, pl.BlockSpec((SPAN, d), lambda b: (blocks - 1 - b, 0))],
        out_shape=[
            shape((count, width), F32),
            shape((count, width), F32),
            shape((count, width), F32),
            shape((count, d), F32),
        ],
        scratch_shapes=[pltpu.VMEM((heads, d, d), F32)],
        compiler_params=params(),
        name="delta_backward",
    )(q, k, v, w, u, a, e, kept_states, do, cols, rows, later)


def scan_states(x):
    peers, d, width = x.shape
    return pl.pallas_call(
        partial(prefix_kernel, peers),
        out_shape=shape((peers, d, width - d), BF),
        name="state_prefix",
    )(x)


def scan_grads(x, g):
    peers, d, width = g.shape
    return pl.pallas_call(
        partial(suffix_kernel, peers),
        out_shape=shape((peers, d, width), BF),
        name="state_suffix",
    )(x, g)


class Place:
    def __init__(self):
        self.nf, self.nr = lax.axis_size("fsdp"), lax.axis_size("rep")
        self.ny = 2 if self.nf <= 8 else self.nf // 4
        self.nz = self.nf // self.ny
        self.nc = 2 if self.nr % 2 == 0 else 1
        self.nx = self.nr // self.nc
        self.f, self.r = lax.axis_index("fsdp"), lax.axis_index("rep")
        self.z, self.y = self.f // self.ny, self.f % self.ny
        self.x, self.c = self.r // self.nc, self.r % self.nc

    def send(self, value, way, steps):
        if way == "z":
            pairs = [
                (z * self.ny + y, (z + steps) % self.nz * self.ny + y)
                for z in range(self.nz)
                for y in range(self.ny)
            ]
            return lax.ppermute(value, "fsdp", pairs)
        if way == "y":
            pairs = [
                (z * self.ny + y, z * self.ny + (y + steps) % self.ny)
                for z in range(self.nz)
                for y in range(self.ny)
            ]
            return lax.ppermute(value, "fsdp", pairs)
        if way == "x":
            pairs = [
                (x * self.nc + c, (x + steps) % self.nx * self.nc + c)
                for x in range(self.nx)
                for c in range(self.nc)
            ]
            return lax.ppermute(value, "rep", pairs)
        pairs = [
            (x * self.nc + c, x * self.nc + (c + steps) % self.nc)
            for x in range(self.nx)
            for c in range(self.nc)
        ]
        return lax.ppermute(value, "rep", pairs)

    def size(self, way):
        return {"z": self.nz, "y": self.ny, "x": self.nx, "c": self.nc}[way]

    def at(self, way):
        return {"z": self.z, "y": self.y, "x": self.x, "c": self.c}[way]


def place_kernel(count, rows, each, by_rows, widths, offs_ref, own_ref, *refs):
    stacks, outs, sems = refs[: len(count)], refs[len(count) : -1], refs[-1]
    copies = []

    def put(src, row, height, col, width_of):
        start = 0
        for out, width in zip(outs, widths):
            copy = pltpu.make_async_copy(
                src(start, width), out.at[pl.ds(row, height), col(width)], sems.at[len(copies)]
            )
            copy.start()
            copies.append(copy)
            start += width

    top = pl.multiple_of(offs_ref[0], rows)
    put(lambda s, w: own_ref.at[:, pl.ds(s, w)], top, rows, lambda w: pl.ds(0, w), None)
    at = 1
    for stack, number in zip(stacks, count):
        for j in range(number):
            if by_rows:
                row = pl.multiple_of(offs_ref[at], each)
                put(lambda s, w, j=j: stack.at[j, :, pl.ds(s, w)], row, each, lambda w: pl.ds(0, w), None)
            else:
                row = pl.multiple_of(offs_ref[at], rows)
                column = pl.multiple_of(offs_ref[at + 1], each)
                put(lambda s, w, j=j: stack.at[j], row, rows, lambda w: pl.ds(column, each), None)
            at += 1 if by_rows else 2
    for copy in copies:
        copy.wait()


def gather_weights(here, shard, widths, deep, by_rows=True):
    rows, total = shard.shape
    parts = here.nr if deep else here.nc
    extent = rows if by_rows else total
    each = extent // parts
    if extent % parts or each % (32 if by_rows else 128) or rows % 32:
        whole = lax.all_gather(shard, "fsdp", axis=0, tiled=True)
        starts = [sum(widths[:i]) for i in range(len(widths))]
        return [whole[:, s : s + w] for s, w in zip(starts, widths)]
    part = here.r if deep else here.c
    piece = lax.dynamic_slice_in_dim(shard, part * each, each, 0 if by_rows else 1)
    near = [(s, 0, here.send(piece, "z", s)) for s in range(1, here.nz)]
    far = [(0, s, here.send(piece, "y", s)) for s in range(1, here.ny)]
    far += [(sz, s, here.send(a, "y", s)) for sz, zero, a in near for s in range(1, here.ny)]
    pieces = near + far
    stack = jnp.stack([a for sz, sy, a in pieces])
    stacks = [(0, 0, stack)]
    if deep:
        stacks += [(s, 0, here.send(stack, "x", s)) for s in range(1, here.nx)]
    stacks += [(sx, s, here.send(a, "c", s)) for sx, zero, a in stacks for s in range(1, here.nc)]
    offsets = [here.f * rows]
    for sx, sc, a in stacks:
        x, c = (here.x - sx) % here.nx, (here.c - sc) % here.nc
        inside = (x * here.nc + c if deep else c) * each
        for sz, sy, unused in pieces:
            source = (here.z - sz) % here.nz * here.ny + (here.y - sy) % here.ny
            if by_rows:
                offsets.append(source * rows + inside)
            else:
                offsets += [source * rows, inside]
    offsets = jnp.stack(offsets).astype(jnp.int32)
    count = [len(pieces)] * len(stacks)
    any_space = pl.BlockSpec(memory_space=pl.ANY)
    outs = pl.pallas_call(
        partial(place_kernel, count, rows, each, by_rows, widths),
        grid_spec=pltpu.PrefetchScalarGridSpec(
            num_scalar_prefetch=1,
            grid=(1,),
            in_specs=[any_space] * (1 + len(stacks)),
            out_specs=[pl.BlockSpec((here.nf * rows, w), lambda i, o: (0, 0)) for w in widths],
            scratch_shapes=[pltpu.SemaphoreType.DMA(((1 + sum(count)) * len(widths),))],
        ),
        out_shape=[jax.ShapeDtypeStruct((here.nf * rows, w), shard.dtype) for w in widths],
        compiler_params=pltpu.CompilerParams(vmem_limit_bytes=VMEM_LIMIT),
        name="place_weights",
    )(offsets, shard, *[a for sx, sc, a in stacks])
    return outs


def scatter_way(here, array, way, axis):
    number, mine = here.size(way), here.at(way)
    total = lax.dynamic_index_in_dim(array, mine, axis, keepdims=False).astype(F32)
    for s in range(1, number):
        out = lax.dynamic_index_in_dim(array, (mine + s) % number, axis, keepdims=False)
        total = total + here.send(out, way, s).astype(F32)
    return total.astype(BF)


def join_way(here, array, way, axis):
    number, mine = here.size(way), here.at(way)
    got = [array] + [here.send(array, way, s) for s in range(1, number)]
    if number == 2:
        ahead = jnp.concatenate(got, axis=axis)
        behind = jnp.concatenate(got[::-1], axis=axis)
        return jnp.where(mine == 0, ahead, behind)
    stack = jnp.stack(got)
    order = (mine - jnp.arange(number)) % number
    stack = jnp.take(stack, order, axis=0)
    return jnp.concatenate([stack[i] for i in range(number)], axis=axis)


def reduce_grad(here, left, right, order):
    width = right.shape[1]
    half = width // here.nc
    if here.nc == 2:
        theirs = lax.dynamic_slice_in_dim(right, (1 - here.c) * half, half, 1)
        mine = lax.dynamic_slice_in_dim(right, here.c * half, half, 1)
        away = contract(left, theirs, 0, 0).astype(BF)
        came = here.send(away, "c", 1)
        part = (contract(left, mine, 0, 0) + came.astype(F32)).astype(BF)
    else:
        part = contract(left, right, 0, 0).astype(BF)
    rows = part.shape[0] // here.nf
    part = part.reshape(here.nz, here.ny, rows, half)
    split = False
    have = {"z": 0, "y": 1}
    for way in order:
        if way == "x":
            if len(have) == 2:
                lead = part.shape[:2]
                part = part.reshape(lead + (here.nx, rows // here.nx, half))
                part = scatter_way(here, part, "x", 2)
                split = True
            elif len(have) == 0:
                total = part.astype(F32)
                for s in range(1, here.nx):
                    total = total + here.send(part, "x", s).astype(F32)
                part = total.astype(BF)
            else:
                part = part.reshape((part.shape[0], here.nx, rows // here.nx, half))
                part = scatter_way(here, part, "x", 1)
                split = True
        else:
            axis = 1 if (way == "y" and "z" in have) else 0
            part = scatter_way(here, part, way, axis)
            have.pop(way)
    if split:
        part = join_way(here, part, "x", 0)
    if here.nc == 2:
        part = join_way(here, part, "c", 1)
    return part.astype(F32)


def sum_all(here, array):
    for way in ("c", "x", "y", "z"):
        low = array.astype(BF)
        total = low.astype(F32)
        got = [here.send(low, way, s).astype(F32) for s in range(1, here.size(way))]
        array = total
        for g in got:
            array = array + g
    return array


def contract(left, right, left_dim, right_dim):
    return lax.dot_general(
        left, right, (((left_dim,), (right_dim,)), ((), ())), preferred_element_type=F32
    )


def rms_norm(values, gain):
    return values * lax.rsqrt(jnp.mean(values * values, axis=-1, keepdims=True) + EPSILON) * gain


def make_features(extended, taps, beta_pre, masks, head_count):
    row_count = beta_pre.shape[0]
    lead = extended.shape[0] - row_count
    mixed = taps[0] * extended[lead:] * masks[0]
    for offset in range(1, 4):
        mixed = mixed + taps[offset] * extended[lead - offset : lead - offset + row_count] * masks[offset]
    active = jax.nn.silu(mixed)
    model_width = active.shape[1] // 3
    head_dim = model_width // head_count
    queries = active[:, :model_width] * head_dim ** (-0.5)
    key_raw = active[:, model_width : 2 * model_width].reshape(row_count, head_count, head_dim)
    key_unit = key_raw * lax.rsqrt(jnp.sum(key_raw * key_raw, axis=-1, keepdims=True) + EPSILON)
    values = active[:, 2 * model_width :]
    return (queries, key_unit.reshape(row_count, model_width), values, jax.nn.sigmoid(beta_pre))


def swiglu(up_gate, up_lin):
    return jax.nn.silu(up_gate) * up_lin


def from_behind(value, steps):
    count = lax.axis_size("fsdp")
    first, last = (max(0, -steps), min(count, count - steps))
    return lax.ppermute(value, "fsdp", [(source, source + steps) for source in range(first, last)])


def to_owners(parts, fanout):
    heads, d, width = parts.shape
    cut = parts.reshape(heads, d, fanout, width // fanout)
    return jnp.swapaxes(cut, 1, 2).reshape(heads * fanout, d, width // fanout)


def to_heads(parts, fanout):
    owners, d, width = parts.shape
    cut = parts.reshape(owners // fanout, fanout, d, width)
    return jnp.swapaxes(cut, 1, 2).reshape(owners // fanout, d, width * fanout)


def swap(value):
    return lax.all_to_all(value, "fsdp", 0, 0, tiled=True)


def gather_small(here, arrays):
    flat = jnp.concatenate([a.reshape(-1) for a in arrays])
    near = [(s, 0, here.send(flat, "z", s)) for s in range(1, here.nz)]
    far = [(sz, s, here.send(a, "y", s)) for sz, zero, a in [(0, 0, flat)] + near for s in range(1, here.ny)]
    pieces = [(0, 0, flat)] + near + far
    stack = jnp.stack([a for sz, sy, a in pieces])
    source = jnp.stack(
        [(here.z - sz) % here.nz * here.ny + (here.y - sy) % here.ny for sz, sy, a in pieces]
    )
    pick = (lax.broadcasted_iota(jnp.int32, (here.nf, here.nf), 0) == source[None, :]).astype(BF)
    whole = contract(pick, stack, 1, 0)
    outs, at = [], 0
    for a in arrays:
        outs.append(whole[:, at : at + a.size].reshape((here.nf,) + a.shape))
        at += a.size
    return outs


def on_device(
    hidden_in,
    seg_ids,
    attn_gain,
    qkv_weight,
    beta_weight,
    gate_weight,
    conv_taps,
    out_gain,
    out_weight,
    ffn_gain,
    ffn_gate,
    ffn_up,
    ffn_down,
    cotangent,
):
    here = Place()
    row_count, width = hidden_in.shape
    heads = beta_weight.shape[1]
    head_dim = width // heads
    blocks = row_count // SPAN
    rim = 8

    rim_rows = from_behind(hidden_in[row_count - rim :], 1)
    numbers = seg_ids + 1
    rim_ids = from_behind(numbers[row_count - rim :], 1)
    attn_s, outgain_s, ffngain_s, taps_s = gather_small(
        here, (attn_gain, out_gain, ffn_gain, conv_taps)
    )
    attn_scale = attn_s.reshape(-1)
    outgain_scale = outgain_s.reshape(1, -1)
    ffngain_scale = ffngain_s.reshape(-1)
    taps_scale = jnp.swapaxes(taps_s, 0, 1).reshape(conv_taps.shape[0], -1)

    (qkv_full,) = gather_weights(here, qkv_weight, [3 * width], True)
    lanes = 128
    beta_wide = jnp.pad(beta_weight, ((0, 0), (0, lanes - heads)))
    gate_full, outw_full, beta_full = gather_weights(
        here,
        jnp.concatenate([gate_weight, out_weight, beta_wide], axis=1),
        [width, width, lanes],
        False,
    )
    hidden_units = ffn_gate.shape[1]
    hidgate_full, hidup_full = gather_weights(
        here, jnp.concatenate([ffn_gate, ffn_up], axis=1), [hidden_units, hidden_units], True
    )
    (down_full,) = gather_weights(here, ffn_down, [width], False, by_rows=False)

    residual = hidden_in.astype(F32)
    extended_in = jnp.concatenate([rim_rows, hidden_in]).astype(F32)
    normed_ext = rms_norm(extended_in, attn_scale).astype(BF)
    normed_low = normed_ext[rim:]
    mixed_pre = jnp.dot(normed_ext, qkv_full, preferred_element_type=F32)
    beta_pre = jnp.dot(normed_low, beta_full, preferred_element_type=F32)[:, :heads]
    gate_pre = jnp.dot(normed_low, gate_full, preferred_element_type=F32)
    ids = jnp.concatenate([rim_ids, numbers]).astype(F32)
    masks = jnp.stack(
        [
            (ids[rim - offset : rim - offset + row_count] == ids[rim:]).astype(F32)
            for offset in range(4)
        ]
    )[:, :, None]
    features, feature_back = jax.vjp(
        partial(make_features, masks=masks, head_count=heads), mixed_pre, taps_scale, beta_pre
    )
    queries, key_unit, values, rates = features
    query_low, key_low, value_low = queries.astype(BF), key_unit.astype(BF), values.astype(BF)
    own_ids = ids[rim:]
    before = ids[rim - 1 : rim - 1 + row_count : SPAN]
    cols = jnp.concatenate([rates, own_ids[:, None], jnp.zeros((row_count, heads - 1), F32)], 1)
    rows = jnp.concatenate(
        [
            jnp.swapaxes(rates.reshape(blocks, SPAN, heads), 1, 2),
            own_ids.reshape(blocks, 1, SPAN),
            jnp.broadcast_to(before[:, None, None], (blocks, 1, SPAN)),
            jnp.zeros((blocks, heads - 2, SPAN), F32),
        ],
        1,
    )
    w, u, a, moves = delta_summary(key_low, value_low, cols, rows, heads)
    fanout = here.nf // heads
    if fanout > 1:
        moves = jnp.concatenate(
            [
                to_owners(moves[:, :, :head_dim], fanout),
                jnp.repeat(moves[:, :, head_dim:], fanout, axis=0),
            ],
            axis=2,
        )
    owned = swap(moves)
    entry = swap(scan_states(owned))
    if fanout > 1:
        entry = to_heads(entry, fanout)
    gated_low, attn_heads, fresh, kept = delta_forward(
        query_low, key_low, w, u, cols, rows, entry, gate_pre, outgain_scale, heads
    )
    middle = residual + jnp.dot(gated_low, outw_full, preferred_element_type=F32)
    normed_two, norm_two_back = jax.vjp(rms_norm, middle, ffngain_scale)
    normed_two_low = normed_two.astype(BF)
    up_gate = jnp.dot(normed_two_low, hidgate_full, preferred_element_type=F32)
    up_lin = jnp.dot(normed_two_low, hidup_full, preferred_element_type=F32)
    hidden_ff, swiglu_back = jax.vjp(swiglu, up_gate, up_lin)
    hidden_low = hidden_ff.astype(BF)
    output = (middle + jnp.dot(hidden_low, down_full, preferred_element_type=F32)).astype(BF)

    top_grad = cotangent.astype(F32)
    down_total = reduce_grad(here, hidden_low, cotangent, "yzx")
    hidden_grad = contract(cotangent, down_full, 1, 1)
    upgate_grad, uplin_grad = swiglu_back(hidden_grad)
    upgate_low, uplin_low = upgate_grad.astype(BF), uplin_grad.astype(BF)
    hidgate_total = reduce_grad(here, normed_two_low, upgate_low, "xyz")
    hidup_total = reduce_grad(here, normed_two_low, uplin_low, "xyz")
    normed_two_grad = contract(upgate_low, hidgate_full, 1, 1) + contract(uplin_low, hidup_full, 1, 1)
    middle_back, ffngain_grad = norm_two_back(normed_two_grad)
    middle_grad = top_grad + middle_back
    middle_low = middle_grad.astype(BF)
    outproj_total = reduce_grad(here, gated_low, middle_low, "yzx")
    gated_grad = contract(middle_low, outw_full, 1, 1)
    heads_grad, gatepre_low, outgain_grad, local_later = delta_adjoint(
        query_low, key_low, w, cols, rows, gated_grad, attn_heads, gate_pre, outgain_scale, heads
    )
    if fanout > 1:
        local_later = to_owners(local_later, fanout)
    later = swap(scan_grads(owned, swap(local_later)))
    if fanout > 1:
        later = to_heads(later, fanout)
    gate_total = reduce_grad(here, normed_low, gatepre_low, "yzx")
    query_grad, key_grad, value_grad, rate_grad = delta_backward(
        query_low, key_low, value_low, w, u, a, fresh, kept, heads_grad, cols, rows, later, heads
    )
    ext_grad, taps_grad, betapre_grad = feature_back(
        (query_grad, key_grad, value_grad, rate_grad[:, :heads])
    )
    mixed_low = ext_grad.astype(BF)
    betapre_low = betapre_grad.astype(BF)
    parts = [
        reduce_grad(here, normed_ext, mixed_low[:, i * width : (i + 1) * width], order)
        for i, order in enumerate(("xyz", "yzx", "zyx"))
    ]
    qkv_total = jnp.concatenate(parts, axis=1)
    beta_grad = contract(normed_low, betapre_low, 0, 0)
    wide_grad = contract(mixed_low, qkv_full, 1, 1)
    rim_grad = from_behind(wide_grad[:rim].astype(BF), -1).astype(F32)
    normed_grad = (
        wide_grad[rim:]
        + jnp.pad(rim_grad, ((row_count - rim, 0), (0, 0)))
        + contract(betapre_low, beta_full[:, :heads], 1, 1)
        + contract(gatepre_low, gate_full, 1, 1)
    )
    input_back, attngain_grad = jax.vjp(rms_norm, residual, attn_scale)[1](normed_grad)
    input_grad = (middle_grad + input_back).astype(BF)

    small = (
        attngain_grad.reshape(here.nf, -1),
        beta_grad.reshape(here.nf, -1),
        jnp.swapaxes(taps_grad.reshape(taps_grad.shape[0], here.nf, -1), 0, 1).reshape(here.nf, -1),
        outgain_grad.reshape(here.nf, -1),
        ffngain_grad.reshape(here.nf, -1),
    )
    summed = sum_all(here, jnp.concatenate(small, axis=1))
    mine = lax.dynamic_index_in_dim(summed, here.f, 0, keepdims=False)
    ends = [0]
    for s in small:
        ends.append(ends[-1] + s.shape[1])
    cut = [mine[ends[i] : ends[i + 1]] for i in range(len(small))]
    return (
        output,
        input_grad,
        cut[0],
        qkv_total,
        cut[1].reshape(-1, heads),
        gate_total,
        cut[2].reshape(conv_taps.shape),
        cut[3],
        outproj_total,
        cut[4],
        hidgate_total,
        hidup_total,
        down_total,
    )


def solution(mesh):
    placed = (
        P(("rep", "fsdp"), None),
        P(("rep", "fsdp")),
        P("fsdp"),
        P("fsdp", None),
        P("fsdp", None),
        P("fsdp", None),
        P(None, "fsdp"),
        P("fsdp"),
        P("fsdp", None),
        P("fsdp"),
        P("fsdp", None),
        P("fsdp", None),
        P("fsdp", None),
        P(("rep", "fsdp"), None),
    )
    return jax.shard_map(
        on_device,
        mesh=mesh,
        in_specs=placed,
        out_specs=(
            P(("rep", "fsdp"), None),
            P(("rep", "fsdp"), None),
            P("fsdp"),
            P("fsdp", None),
            P("fsdp", None),
            P("fsdp", None),
            P(None, "fsdp"),
            P("fsdp"),
            P("fsdp", None),
            P("fsdp"),
            P("fsdp", None),
            P("fsdp", None),
            P("fsdp", None),
        ),
        check_vma=False,
    )
```

```python
from functools import partial

import jax
import jax.numpy as jnp
from jax import lax
from jax.experimental import pallas as pl
from jax.experimental.pallas import tpu as pltpu
from jax.sharding import PartitionSpec as P

SPAN = 64
EPSILON = 1e-06
BF = jnp.bfloat16
F32 = jnp.float32


def nn(a, b):
    return lax.dot_general(a, b, (((1,), (0,)), ((), ())), preferred_element_type=F32)


def nt(a, b):
    return lax.dot_general(a, b, (((1,), (1,)), ((), ())), preferred_element_type=F32)


def tn(a, b):
    return lax.dot_general(a, b, (((0,), (0,)), ((), ())), preferred_element_type=F32)


def block_masks(cols_ref, rows_ref, heads):
    n = SPAN
    row = lax.broadcasted_iota(jnp.int32, (n, n), 0)
    col = lax.broadcasted_iota(jnp.int32, (n, n), 1)
    ids = cols_ref[:, heads : heads + 1]
    ids_row = rows_ref[0, heads : heads + 1, :]
    before = rows_ref[0, heads + 1 : heads + 2, :]
    end = ids_row[:, n - 1 : n]
    same = ids == ids_row
    first = (ids == before[:, :1]).astype(F32)
    last = (ids == end).astype(F32)
    keep = (end == before[:, :1]).astype(F32)
    return row, col, same, first, last, keep


def sigmoid(z):
    return 0.5 * jnp.tanh(0.5 * z) + 0.5


def shifted_rows(x, prev, masks):
    both = jnp.concatenate([prev, x], axis=0)
    lead = prev.shape[0]
    return [x] + [both[lead - j : lead - j + x.shape[0]] * masks[j - 1] for j in (1, 2, 3)]


def mix_rows(rows, taps):
    mixed = rows[0] * taps[0:1]
    for j in (1, 2, 3):
        mixed = mixed + rows[j] * taps[j : j + 1]
    return mixed


def lag_masks(cols_ref, heads):
    return [cols_ref[:, heads + j : heads + j + 1] for j in (1, 2, 3)]


def kv_at(heads, d, h):
    half = heads // 2
    start = (h // half) * 2 * half * d + (h % half) * d
    return slice(start, start + d), slice(start + half * d, start + half * d + d)


def summary_kernel(
    heads, d, pre_ref, prev_ref, taps_ref, cols_ref, rows_ref,
    k_ref, v_ref, w_ref, u_ref, a_ref, x_ref, state,
):
    n = SPAN
    block = pl.program_id(0)

    @pl.when(block == 0)
    def _():
        r = lax.broadcasted_iota(jnp.int32, (d, 2 * d), 0)
        c = lax.broadcasted_iota(jnp.int32, (d, 2 * d), 1)
        unit = (r + d == c).astype(F32)
        for h in range(heads):
            state[h] = unit

    row, col, same, first, last, keep = block_masks(cols_ref, rows_ref, heads)
    lower = jnp.logical_and(same, row > col)
    unit = (row == col).astype(F32)
    pair = jnp.logical_and(row == col + 1, (row & 1) == 1)
    masks = lag_masks(cols_ref, heads)
    keys = []
    mixing = []
    inverse = []
    for h in range(heads):
        cut = slice(h * d, (h + 1) * d)
        at_k, at_v = kv_at(heads, d, h)
        z = mix_rows(shifted_rows(pre_ref[:, at_k], prev_ref[:, at_k], masks), taps_ref[:, at_k])
        act = z * sigmoid(z)
        root = lax.rsqrt(jnp.sum(act * act, axis=1, keepdims=True) + EPSILON)
        keys.append((act * root).astype(BF))
        k_ref[:, cut] = keys[h]
        z = mix_rows(shifted_rows(pre_ref[:, at_v], prev_ref[:, at_v], masks), taps_ref[:, at_v])
        v_ref[:, cut] = (z * sigmoid(z)).astype(BF)
        m = jnp.where(lower, nt(keys[h], keys[h]) * cols_ref[:, h : h + 1], 0.0)
        mixing.append(m)
        inverse.append((unit - jnp.where(pair, m, 0.0)).astype(BF))
    size = 2
    while size < n:
        level = jnp.logical_and(
            (row // (2 * size)) == (col // (2 * size)),
            jnp.logical_and(((row // size) & 1) == 1, ((col // size) & 1) == 0),
        )
        inner = [nn(jnp.where(level, mixing[h], 0.0).astype(BF), inverse[h]).astype(BF) for h in range(heads)]
        for h in range(heads):
            inverse[h] = inverse[h] - jnp.where(level, nn(inverse[h], inner[h]), 0.0).astype(BF)
        size *= 2
    for h in range(heads):
        cut = slice(h * d, (h + 1) * d)
        a_ref[h] = inverse[h]
        scaled = (inverse[h].astype(F32) * rows_ref[0, h : h + 1, :]).astype(BF)
        both = nn(scaled, jnp.concatenate([keys[h], v_ref[:, cut]], axis=1))
        w = both[:, :d].astype(BF)
        u = both[:, d:].astype(BF)
        w_ref[:, cut] = w
        u_ref[:, cut] = u
        held = state[h]
        moved = nn(w, held.astype(BF)) * first
        fresh = (jnp.concatenate([u.astype(F32), jnp.zeros((n, d), F32)], axis=1) - moved).astype(BF)
        key_last = (keys[h].astype(F32) * last).astype(BF)
        state[h] = keep * held + tn(key_last, fresh)

    @pl.when(block == pl.num_programs(0) - 1)
    def _():
        x_ref[...] = state[...].astype(BF)


def forward_kernel(
    heads, d, pre_ref, prev_ref, taps_ref, k_ref, w_ref, u_ref, cols_ref, rows_ref, s_ref, gate_ref, gain_ref,
    q_ref, y_ref, o_ref, e_ref, kept_ref, state,
):
    n = SPAN
    block = pl.program_id(0)

    @pl.when(block == 0)
    def _():
        state[...] = s_ref[...].astype(F32)

    row, col, same, first, last, keep = block_masks(cols_ref, rows_ref, heads)
    visible = jnp.logical_and(same, row >= col)
    masks = lag_masks(cols_ref, heads)
    for h in range(heads):
        cut = slice(h * d, (h + 1) * d)
        z = mix_rows(shifted_rows(pre_ref[:, cut], prev_ref[:, cut], masks), taps_ref[:, cut])
        q = (z * sigmoid(z) * d ** (-0.5)).astype(BF)
        q_ref[:, cut] = q
        k, w = k_ref[:, cut], w_ref[:, cut]
        held = state[h]
        held_low = held.astype(BF)
        kept_ref[0, h] = held_low
        both = nn(jnp.concatenate([w, q], axis=0), held_low)
        fresh = (u_ref[:, cut].astype(F32) - first * both[:n]).astype(BF)
        e_ref[:, cut] = fresh
        scores = jnp.where(visible, nt(q, k), 0.0).astype(BF)
        out = first * both[n:] + nn(scores, fresh)
        key_last = (k.astype(F32) * last).astype(BF)
        state[h] = keep * held + tn(key_last, fresh)
        o_ref[:, cut] = out
        g = gate_ref[:, cut]
        root = lax.rsqrt(jnp.mean(out * out, axis=1, keepdims=True) + EPSILON)
        y_ref[:, cut] = (out * root * gain_ref[...] * (g * sigmoid(g))).astype(BF)


def adjoint_kernel(
    heads, d, q_ref, k_ref, w_ref, cols_ref, rows_ref, dy_ref, o_ref, gate_ref, gain_ref,
    do_ref, dgate_ref, dgain_ref, ds_ref, state,
):
    n = SPAN
    step = pl.program_id(0)

    @pl.when(step == 0)
    def _():
        state[...] = jnp.zeros_like(state)
        dgain_ref[...] = jnp.zeros_like(dgain_ref)

    row, col, same, first, last, keep = block_masks(cols_ref, rows_ref, heads)
    visible = jnp.logical_and(same, row >= col)
    gain = gain_ref[...]
    gain_sum = jnp.zeros((1, d), F32)
    for h in range(heads):
        cut = slice(h * d, (h + 1) * d)
        q, k, w = q_ref[:, cut], k_ref[:, cut], w_ref[:, cut]
        o, g, dy = o_ref[:, cut], gate_ref[:, cut], dy_ref[:, cut]
        root = lax.rsqrt(jnp.mean(o * o, axis=1, keepdims=True) + EPSILON)
        unit = o * root
        sig = sigmoid(g)
        m = g * sig
        t = dy * m
        gain_sum = gain_sum + jnp.sum(t * unit, axis=0, keepdims=True)
        tg = t * gain
        do = root * (tg - unit * jnp.mean(tg * unit, axis=1, keepdims=True))
        dgate_ref[:, cut] = (dy * gain * unit * (sig * (1.0 + g * (1.0 - sig)))).astype(BF)
        do_low = do.astype(BF)
        do_ref[:, cut] = do_low
        scores = jnp.where(visible, nt(q, k), 0.0).astype(BF)
        later = state[h]
        de = last * nn(k, later.astype(BF)) + tn(scores, do_low)
        left = jnp.concatenate([q.astype(F32) * first, w.astype(F32) * (-first)], axis=0).astype(BF)
        right = jnp.concatenate([do_low, de.astype(BF)], axis=0)
        state[h] = keep * later + tn(left, right)
    dgain_ref[...] += gain_sum

    @pl.when(step == pl.num_programs(0) - 1)
    def _():
        ds_ref[...] = state[...].astype(BF)


def backward_kernel(
    heads, part, d, q_ref, k_ref, v_ref, w_ref, u_ref, a_ref, e_ref, kept_ref, do_ref, cols_ref, rows_ref, s_ref,
    qpre_ref, qprev_ref, qtaps_ref, kvpre_ref, kvprev_ref, kvtaps_ref,
    dpre_ref, dbeta_ref, dtaps_ref, state, carry,
):
    n = SPAN
    step = pl.program_id(0)
    number = heads // 2

    @pl.when(step == 0)
    def _():
        state[...] = s_ref[...].astype(F32)
        carry[...] = jnp.zeros_like(carry)
        dtaps_ref[...] = jnp.zeros_like(dtaps_ref)

    @pl.when(step < pl.num_programs(0) - 1)
    def _():
        row, col, same, first, last, keep = block_masks(cols_ref, rows_ref, heads)
        visible = jnp.logical_and(same, row >= col)
        lower = jnp.logical_and(same, row > col)
        lane = lax.broadcasted_iota(jnp.int32, (n, d), 1)
        masks = lag_masks(cols_ref, heads)
        rate_grads = jnp.zeros((n, d), F32)

        def conv_back(dact, z, sig, rows, taps, at):
            dconv = dact * (sig * (1.0 + z * (1.0 - sig)))
            here = slice(at, at + d)
            dtaps_ref[:, here] += jnp.concatenate(
                [jnp.sum(dconv * r, axis=0, keepdims=True) for r in rows], axis=0
            )
            dpre = dconv * taps[0:1]
            for j in (1, 2, 3):
                masked = dconv * masks[j - 1]
                both = jnp.concatenate([masked, carry[j - 1, :, here]], axis=0)
                dpre = dpre + both[j : n + j] * taps[j : j + 1]
                carry[j - 1, :, here] = masked[:8]
            dpre_ref[:, here] = dpre.astype(BF)

        for h in range(number):
            cut = slice(h * d, (h + 1) * d)
            cut_v = slice((number + h) * d, (number + h + 1) * d)
            q, k, v, w, u = q_ref[:, cut], k_ref[:, cut], v_ref[:, cut], w_ref[:, cut], u_ref[:, cut]
            do, e, held = do_ref[:, cut], e_ref[:, cut], kept_ref[0, h]
            at = part * number + h
            rate = cols_ref[:, at : at + 1]
            later = state[h]
            later_low = later.astype(BF)
            scores = jnp.where(visible, nt(q, k), 0.0).astype(BF)
            de = last * nn(k, later_low) + tn(scores, do)
            de_low = de.astype(BF)
            dscores = jnp.where(visible, nt(do, e), 0.0).astype(BF)
            both = nt(jnp.concatenate([do, de_low], axis=0), held)
            dq = first * both[:n] + nn(dscores, k)
            dw = -first * both[n:]
            dk = tn(dscores, q) + last * nt(e, later_low)
            pg = tn(a_ref[h], jnp.concatenate([dw.astype(BF), de_low], axis=1))
            p, g = pg[:, :d], pg[:, d:]
            dmix = jnp.where(lower, -nt(pg.astype(BF), jnp.concatenate([w, u], axis=1)), 0.0).astype(BF)
            kf = k.astype(F32)
            drk = p + nn(dmix, k)
            dk = dk + tn(dmix, (kf * rate).astype(BF)) + rate * drk
            dr = jnp.sum(drk * kf + g * v.astype(F32), axis=1, keepdims=True)
            rate_grads = jnp.where(lane == at, dr * rate * (1.0 - rate), rate_grads)
            left = jnp.concatenate([q.astype(F32) * first, w.astype(F32) * (-first)], axis=0).astype(BF)
            right = jnp.concatenate([do, de_low], axis=0)
            state[h] = keep * later + tn(left, right)

            taps = qtaps_ref[:, cut]
            rows = shifted_rows(qpre_ref[:, cut], qprev_ref[:, cut], masks)
            z = mix_rows(rows, taps)
            conv_back(dq * d ** (-0.5), z, sigmoid(z), rows, taps, h * d)
            taps = kvtaps_ref[:, cut]
            rows = shifted_rows(kvpre_ref[:, cut], kvprev_ref[:, cut], masks)
            z = mix_rows(rows, taps)
            sig = sigmoid(z)
            act = z * sig
            root = lax.rsqrt(jnp.sum(act * act, axis=1, keepdims=True) + EPSILON)
            unit = act * root
            dact = root * (dk - unit * jnp.sum(unit * dk, axis=1, keepdims=True))
            conv_back(dact, z, sig, rows, taps, (number + h) * d)
            taps = kvtaps_ref[:, cut_v]
            rows = shifted_rows(kvpre_ref[:, cut_v], kvprev_ref[:, cut_v], masks)
            z = mix_rows(rows, taps)
            conv_back(rate * g, z, sigmoid(z), rows, taps, (2 * number + h) * d)
        dbeta_ref[...] = rate_grads

    @pl.when(step == pl.num_programs(0) - 1)
    def _():
        wide = number * d
        for i, taps_ref, at in ((0, qtaps_ref, 0), (1, kvtaps_ref, 0), (2, kvtaps_ref, wide)):
            here = slice(i * wide, (i + 1) * wide)
            dpre = jnp.zeros((8, wide), F32)
            for j in (1, 2, 3):
                held = carry[j - 1, :, here]
                both = jnp.concatenate([jnp.zeros_like(held), held], axis=0)
                dpre = dpre + both[j : 8 + j] * taps_ref[j : j + 1, at : at + wide]
            dpre_ref[0:8, here] = dpre.astype(BF)


def prefix_kernel(peers, x_ref, out_ref):
    cols = out_ref.shape[2]
    held = jnp.zeros(out_ref.shape[1:], F32)
    for i in range(peers):
        out_ref[i] = held.astype(BF)
        held = nn(x_ref[i, :, cols:], held.astype(BF)) + x_ref[i, :, :cols].astype(F32)


def suffix_kernel(peers, t_ref, g_ref, out_ref):
    held = jnp.zeros(out_ref.shape[1:], F32)
    cols = out_ref.shape[2]
    for i in reversed(range(peers)):
        out_ref[i] = held.astype(BF)
        held = tn(t_ref[i, :, cols:], held.astype(BF)) + g_ref[i].astype(F32)


VMEM_LIMIT = 16 * 1024 * 1024


def params():
    return pltpu.CompilerParams(dimension_semantics=("arbitrary",), vmem_limit_bytes=VMEM_LIMIT)


def cost(microseconds):
    return pl.CostEstimate(
        flops=int(microseconds * 1e9), bytes_accessed=int(microseconds * 3e6), transcendentals=0
    )


def specs(blocks, heads, d, flip):
    at = (lambda b: blocks - 1 - b) if flip else (lambda b: b)
    wide = pl.BlockSpec((SPAN, heads * d), lambda b: (at(b), 0))
    cols = pl.BlockSpec((SPAN, 2 * heads), lambda b: (at(b), 0))
    rows = pl.BlockSpec((1, 2 * heads, SPAN), lambda b: (at(b), 0, 0))
    state = pl.BlockSpec((heads, d, d), lambda b: (0, 0, 0))
    mix = pl.BlockSpec((heads, SPAN, SPAN), lambda b: (0, at(b), 0))
    kept = pl.BlockSpec((1, heads, d, d), lambda b: (at(b), 0, 0, 0))
    gain = pl.BlockSpec((1, d), lambda b: (0, 0))
    return wide, cols, rows, state, mix, kept, gain


def shape(dims, kind):
    return jax.ShapeDtypeStruct(dims, kind)


def before_block(blocks, rim, flip, size, column):
    def index(step):
        b = blocks - 1 - jnp.minimum(step, blocks - 1) if flip else step
        per = SPAN // rim
        return jnp.where(b == 0, blocks * per, b * per - 1), column

    return pl.BlockSpec((rim, size), index)


def delta_summary(pre, taps, cols, rows, heads):
    count, width = cols.shape[0], pre.shape[1] // 2
    d, blocks = width // heads, count // SPAN
    rim = pre.shape[0] - count
    wide, c, r, state, mix, kept, gain = specs(blocks, heads, d, False)
    return pl.pallas_call(
        partial(summary_kernel, heads, d),
        grid=(blocks,),
        in_specs=[
            pl.BlockSpec((SPAN, 2 * width), lambda b: (b, 0)),
            before_block(blocks, rim, False, 2 * width, 0),
            pl.BlockSpec((4, 2 * width), lambda b: (0, 0)),
            c,
            r,
        ],
        out_specs=[wide, wide, wide, wide, mix, pl.BlockSpec((heads, d, 2 * d), lambda b: (0, 0, 0))],
        out_shape=[
            shape((count, width), BF),
            shape((count, width), BF),
            shape((count, width), BF),
            shape((count, width), BF),
            shape((heads, count, SPAN), BF),
            shape((heads, d, 2 * d), BF),
        ],
        scratch_shapes=[pltpu.VMEM((heads, d, 2 * d), F32)],
        compiler_params=params(),
        cost_estimate=cost(24),
        name="delta_summary",
    )(pre, pre, taps, cols, rows)


def delta_forward(pre, taps, k, w, u, cols, rows, entry, gain_full, heads):
    count, width = k.shape
    d, blocks = width // heads, count // SPAN
    rim = pre.shape[0] - count
    wide, c, r, state, mix, kept, gain = specs(blocks, heads, d, False)
    return pl.pallas_call(
        partial(forward_kernel, heads, d),
        grid=(blocks,),
        in_specs=[
            wide,
            before_block(blocks, rim, False, width, 0),
            pl.BlockSpec((4, width), lambda b: (0, 0)),
            wide,
            wide,
            wide,
            c,
            r,
            state,
            pl.BlockSpec((SPAN, width), lambda b: (b, 1)),
            gain,
        ],
        out_specs=[wide, wide, wide, wide, kept],
        out_shape=[
            shape((count, width), BF),
            shape((count, width), BF),
            shape((count, width), F32),
            shape((count, width), BF),
            shape((blocks, heads, d, d), BF),
        ],
        scratch_shapes=[pltpu.VMEM((heads, d, d), F32)],
        compiler_params=params(),
        cost_estimate=cost(16),
        name="delta_forward",
    )(pre, pre, taps, k, w, u, cols, rows, entry, pre, gain_full)


def delta_adjoint(q, k, w, cols, rows, dy, o, gate, gain_full, heads):
    count, width = k.shape
    d, blocks = width // heads, count // SPAN
    wide, c, r, state, mix, kept, gain = specs(blocks, heads, d, True)
    return pl.pallas_call(
        partial(adjoint_kernel, heads, d),
        grid=(blocks,),
        in_specs=[
            wide,
            wide,
            wide,
            c,
            r,
            wide,
            wide,
            pl.BlockSpec((SPAN, width), lambda b: (blocks - 1 - b, 1)),
            gain,
        ],
        out_specs=[wide, wide, gain, state],
        out_shape=[
            shape((count, width), BF),
            shape((count, width), BF),
            shape((1, d), F32),
            shape((heads, d, d), BF),
        ],
        scratch_shapes=[pltpu.VMEM((heads, d, d), F32)],
        compiler_params=params(),
        cost_estimate=cost(15),
        name="delta_adjoint",
    )(q, k, w, cols, rows, dy, o, gate, gain_full)


def delta_backward(part, q, k, v, w, u, a, e, kept_states, do, cols, rows, later, qg_pre, qtaps, kv_pre, kvtaps, heads):
    count, width = k.shape
    d, blocks = width // heads, count // SPAN
    rim = kv_pre.shape[0] - count
    number = heads // 2
    size = number * d

    def at(step):
        return blocks - 1 - jnp.minimum(step, blocks - 1)

    wide = pl.BlockSpec((SPAN, size), lambda b: (at(b), part))
    in_specs = [
        wide,
        wide,
        wide,
        wide,
        wide,
        pl.BlockSpec((number, SPAN, SPAN), lambda b: (part, at(b), 0)),
        wide,
        pl.BlockSpec((1, number, d, d), lambda b: (at(b), part, 0, 0)),
        wide,
        pl.BlockSpec((SPAN, 2 * heads), lambda b: (at(b), 0)),
        pl.BlockSpec((1, 2 * heads, SPAN), lambda b: (at(b), 0, 0)),
        pl.BlockSpec((number, d, d), lambda b: (part, 0, 0)),
        wide,
        before_block(blocks, rim, True, size, part),
        pl.BlockSpec((4, size), lambda b: (0, part)),
        pl.BlockSpec((SPAN, 2 * size), lambda b: (at(b), part)),
        before_block(blocks, rim, True, 2 * size, part),
        pl.BlockSpec((4, 2 * size), lambda b: (0, part)),
    ]
    return pl.pallas_call(
        partial(backward_kernel, heads, part, d),
        grid=(blocks + 1,),
        in_specs=in_specs,
        out_specs=[
            pl.BlockSpec((SPAN, 3 * size), lambda b: (jnp.where(b < blocks, blocks - 1 - b, blocks), 0)),
            pl.BlockSpec((SPAN, d), lambda b: (at(b), 0)),
            pl.BlockSpec((4, 3 * size), lambda b: (0, 0)),
        ],
        out_shape=[
            shape((count + rim, 3 * size), BF),
            shape((count, d), F32),
            shape((4, 3 * size), F32),
        ],
        scratch_shapes=[pltpu.VMEM((number, d, d), F32), pltpu.VMEM((3, rim, 3 * size), F32)],
        compiler_params=params(),
        cost_estimate=cost(32),
        name="delta_backward",
    )(q, k, v, w, u, a, e, kept_states, do, cols, rows, later, qg_pre, qg_pre, qtaps, kv_pre, kv_pre, kvtaps)


def scan_states(x):
    peers, d, width = x.shape
    return pl.pallas_call(
        partial(prefix_kernel, peers),
        out_shape=shape((peers, d, width - d), BF),
        cost_estimate=cost(3),
        name="state_prefix",
    )(x)


def scan_grads(x, g):
    peers, d, width = g.shape
    return pl.pallas_call(
        partial(suffix_kernel, peers),
        out_shape=shape((peers, d, width), BF),
        cost_estimate=cost(3),
        name="state_suffix",
    )(x, g)


def hold(value, *after):
    return lax.optimization_barrier((value, after))[0]


class Place:
    def __init__(self):
        self.nf, self.nr = lax.axis_size("fsdp"), lax.axis_size("rep")
        self.ny = self.nf // 4
        self.nx = self.nr // 2
        self.f, self.r = lax.axis_index("fsdp"), lax.axis_index("rep")
        z = self.f // self.ny
        self.mine = {"v": z // 2, "w": z % 2, "y": self.f % self.ny, "x": self.r // 2, "c": self.r % 2}
        self.number = {"v": 2, "w": 2, "y": self.ny, "x": self.nx, "c": 2}
        self.stride = {"v": 2 * self.ny, "w": self.ny, "y": 1, "x": 2, "c": 1}

    def send(self, value, way, steps=1):
        axis = "rep" if way in "xc" else "fsdp"
        total = self.nr if way in "xc" else self.nf
        number, stride = self.number[way], self.stride[way]
        pairs = []
        for i in range(total):
            at = i // stride % number
            pairs.append((i, i + ((at + steps) % number - at) * stride))
        return lax.ppermute(value, axis, pairs)


def place_kernel(count, rows, each, by_rows, widths, offs_ref, own_ref, *refs):
    stacks, outs, sems = refs[: len(count)], refs[len(count) : -1], refs[-1]
    copies = []

    def put(src, row, height, column, out):
        copy = pltpu.make_async_copy(src, out.at[pl.ds(row, height), column], sems.at[len(copies)])
        copy.start()
        copies.append(copy)

    starts = [sum(widths[:i]) for i in range(len(widths))]
    top = pl.multiple_of(offs_ref[0], rows)
    for start, width, out in zip(starts, widths, outs):
        put(own_ref.at[:, pl.ds(start, width)], top, rows, pl.ds(0, width), out)
    at = 1
    for stack, number in zip(stacks, count):
        for j in range(number):
            row = pl.multiple_of(offs_ref[at], each if by_rows else rows)
            if by_rows:
                for start, width, out in zip(starts, widths, outs):
                    put(stack.at[j, :, pl.ds(start, width)], row, each, pl.ds(0, width), out)
                at += 1
            else:
                column = pl.multiple_of(offs_ref[at + 1], each)
                put(stack.at[j], row, rows, pl.ds(column, each), outs[0])
                at += 2
    for copy in copies:
        copy.wait()


class Gather:
    def __init__(self, here, shard, widths, deep, by_rows=True):
        self.here, self.shard, self.widths, self.deep, self.by_rows = here, shard, widths, deep, by_rows
        rows, total = shard.shape
        parts = here.nr if deep else 2
        extent = rows if by_rows else total
        self.each = extent // parts
        self.plain = bool(extent % parts or self.each % (32 if by_rows else 128) or rows % 32)
        self.plain = self.plain or here.ny != 2 or here.nx != 2
        self.have = {}
        if self.plain:
            return
        part = here.r if deep else here.mine["c"]
        self.have[""] = lax.dynamic_slice_in_dim(shard, part * self.each, self.each, 0 if by_rows else 1)

    def got(self, *names):
        return [] if self.plain else [self.have[name] for name in names]

    def move(self, *names, after=()):
        if not self.plain:
            for name in names:
                self.have[name] = self.here.send(hold(self.have[name[:-1]], *after), name[-1])

    def pile(self):
        if not self.plain:
            self.have["z"] = jnp.stack([self.have[name] for name in ("", "w", "v", "vw")])

    def place(self):
        here, shard, widths = self.here, self.shard, self.widths
        rows, each = shard.shape[0], self.each
        if self.plain:
            whole = lax.all_gather(shard, "fsdp", axis=0, tiled=True)
            starts = [sum(widths[:i]) for i in range(len(widths))]
            return [whole[:, s : s + w] for s, w in zip(starts, widths)]
        mine = here.mine
        offsets = [here.f * rows]
        names = [name for name in self.have if name.startswith("z")]
        for name in names:
            x, c, y = ((mine[way] + (way in name)) % 2 for way in "xcy")
            inside = (x * 2 + c if self.deep else c) * each
            for j in range(4):
                v = (mine["v"] + j // 2) % 2
                w = (mine["w"] + j % 2) % 2
                source = (v * 2 + w) * here.ny + y
                offsets += [source * rows + inside] if self.by_rows else [source * rows, inside]
        offsets = jnp.stack(offsets).astype(jnp.int32)
        stacks = [self.have[name] for name in names]
        count = [4] * len(stacks)
        any_space = pl.BlockSpec(memory_space=pl.ANY)
        size = here.nf * rows
        return pl.pallas_call(
            partial(place_kernel, count, rows, each, self.by_rows, widths),
            grid_spec=pltpu.PrefetchScalarGridSpec(
                num_scalar_prefetch=1,
                grid=(1,),
                in_specs=[any_space] * (1 + len(stacks)),
                out_specs=[pl.BlockSpec((size, w), lambda i, o: (0, 0)) for w in widths],
                scratch_shapes=[pltpu.SemaphoreType.DMA(((1 + sum(count)) * len(widths),))],
            ),
            out_shape=[jax.ShapeDtypeStruct((size, w), shard.dtype) for w in widths],
            compiler_params=pltpu.CompilerParams(
                vmem_limit_bytes=2 * size * sum(widths) * 2 + (1 << 20)
            ),
            cost_estimate=cost(6),
            name="place_weights",
        )(offsets, shard, *stacks)


class Reduce:
    def __init__(self, here):
        self.here = here
        self.split = False

    def swap(self, away):
        self.came = self.here.send(away.astype(BF), "c")

    def take(self, part):
        self.begin(part + self.came.astype(F32))

    def begin(self, part):
        part = part.astype(BF)
        here = self.here
        rows = part.shape[0] // here.nf
        self.part = part.reshape(2, 2, here.ny, rows, part.shape[1])
        self.axes = ["v", "w", "y"]

    def step(self, way, *after):
        here = self.here
        part = hold(self.part, *after)
        number, mine = here.number[way], here.mine[way]
        if way in "xc" and not self.axes:
            total = part.astype(F32)
            for s in range(1, number):
                total = total + here.send(part, way, s).astype(F32)
            self.part = total.astype(BF)
            return
        if way == "x":
            axis = len(self.axes)
            shape = part.shape
            part = part.reshape(shape[:axis] + (number, shape[axis] // number) + shape[axis + 1 :])
            self.split = True
        else:
            axis = self.axes.index(way)
            self.axes.pop(axis)
        total = lax.dynamic_index_in_dim(part, mine, axis, keepdims=False).astype(F32)
        for s in range(1, number):
            out = lax.dynamic_index_in_dim(part, (mine + s) % number, axis, keepdims=False)
            total = total + here.send(out, way, s).astype(F32)
        self.part = total.astype(BF)

    def rows(self):
        if self.split:
            self.part = join_way(self.here, self.part, "x", 0)

    def other(self):
        return self.here.send(self.part, "c")


def join_way(here, array, way, axis):
    number, mine = here.number[way], here.mine[way]
    got = [array] + [here.send(array, way, s) for s in range(1, number)]
    if number == 2:
        ahead = jnp.concatenate(got, axis=axis)
        behind = jnp.concatenate(got[::-1], axis=axis)
        return jnp.where(mine == 0, ahead, behind)
    stack = jnp.stack(got)
    order = (mine - jnp.arange(number)) % number
    stack = jnp.take(stack, order, axis=0)
    return jnp.concatenate([stack[i] for i in range(number)], axis=axis)


def contract(left, right, left_dim, right_dim):
    return lax.dot_general(
        left, right, (((left_dim,), (right_dim,)), ((), ())), preferred_element_type=F32
    )


def rms_norm(values, gain):
    return values * lax.rsqrt(jnp.mean(values * values, axis=-1, keepdims=True) + EPSILON) * gain


def swiglu(pair):
    half = pair.shape[1] // 2
    return jax.nn.silu(pair[:, :half]) * pair[:, half:]


def kv_order(array):
    half = array.shape[1] // 6
    return [array[:, i * half : (i + 1) * half] for i in (2, 4, 3, 5)]


def from_behind(value, steps):
    count = lax.axis_size("fsdp")
    first, last = (max(0, -steps), min(count, count - steps))
    return lax.ppermute(value, "fsdp", [(source, source + steps) for source in range(first, last)])


def to_owners(parts, fanout):
    heads, d, width = parts.shape
    cut = parts.reshape(heads, d, fanout, width // fanout)
    return jnp.swapaxes(cut, 1, 2).reshape(heads * fanout, d, width // fanout)


def to_heads(parts, fanout):
    owners, d, width = parts.shape
    cut = parts.reshape(owners // fanout, fanout, d, width)
    return jnp.swapaxes(cut, 1, 2).reshape(owners // fanout, d, width * fanout)


def swap(value):
    return lax.all_to_all(value, "fsdp", 0, 0, tiled=True)


def by_core(here, for_zero, for_one):
    return jnp.where(here.mine["c"] == 0, for_zero, for_one)


def on_device(
    hidden_in,
    seg_ids,
    attn_gain,
    qkv_weight,
    beta_weight,
    gate_weight,
    conv_taps,
    out_gain,
    out_weight,
    ffn_gain,
    ffn_gate,
    ffn_up,
    ffn_down,
    cotangent,
):
    here = Place()
    row_count, width = hidden_in.shape
    heads = beta_weight.shape[1]
    head_dim = width // heads
    blocks = row_count // SPAN
    rim = 8
    lanes = 128
    hidden_units = ffn_gate.shape[1]

    rim_rows = from_behind(hidden_in[row_count - rim :], 1)
    numbers = seg_ids + 1
    rim_ids = from_behind(numbers[row_count - rim :], 1)

    small = [attn_gain, out_gain, ffn_gain, conv_taps]
    shard_rows = qkv_weight.shape[0]
    flat = jnp.concatenate([a.reshape(-1) for a in small])
    columns = -(-flat.size // shard_rows)
    flat = jnp.pad(flat, (0, columns * shard_rows - flat.size)).reshape(shard_rows, columns)
    extra = jnp.concatenate(
        [beta_weight, flat, jnp.zeros((shard_rows, lanes - heads - columns), BF)], axis=1
    )
    first = Gather(
        here,
        jnp.concatenate(kv_order(qkv_weight) + [extra], axis=1),
        [2 * width, lanes],
        True,
    )
    second = Gather(
        here,
        jnp.concatenate([qkv_weight[:, :width], gate_weight, out_weight], axis=1),
        [2 * width, width],
        False,
    )
    third = Gather(here, jnp.concatenate([ffn_gate, ffn_up], axis=1), [2 * hidden_units], True)
    fourth = Gather(here, ffn_down, [width], False, by_rows=False)
    first.move("v", "w")
    first.move("vw")
    first.pile()
    first.move("zy", "zx", "zc")
    first.move("zyx", "zyc", "zxc")
    second.move("v", "w", after=first.got("vw"))
    first.move("zyxc", after=second.got("v", "w"))
    second.move("vw")
    second.pile()
    kv_full, extra_full = first.place()

    small_full = extra_full[:, heads : heads + columns].reshape(here.nf, -1)
    cuts, at = [], 0
    for array in small:
        cuts.append(small_full[:, at : at + array.size].astype(F32))
        at += array.size
    attn_scale = cuts[0].reshape(-1)
    outgain_scale = cuts[1].reshape(1, -1)
    ffngain_scale = cuts[2].reshape(-1)
    taps_count = conv_taps.shape[0]
    taps_scale = jnp.swapaxes(cuts[3].reshape(here.nf, taps_count, -1), 0, 1).reshape(taps_count, -1)
    query_taps = taps_scale[:, :width]
    kv_taps = jnp.concatenate(kv_order(taps_scale), axis=1)
    residual = hidden_in.astype(F32)
    extended_in = jnp.concatenate([hidden_in, rim_rows]).astype(F32)
    normed_ext = rms_norm(extended_in, attn_scale).astype(BF)
    normed_low = normed_ext[:row_count]
    second.move("zy")
    kv_full = hold(kv_full, second.got("z"))
    kv_pre = jnp.dot(normed_ext, kv_full, preferred_element_type=F32)
    third.move("v", "w", after=[kv_pre])
    beta_pre = jnp.dot(normed_low, extra_full, preferred_element_type=F32)[:, :heads]
    rates = jax.nn.sigmoid(beta_pre)
    ids = jnp.concatenate([rim_ids, numbers]).astype(F32)
    own_ids = numbers.astype(F32)
    before = ids[rim - 1 : rim - 1 + row_count : SPAN]
    cols = jnp.concatenate(
        [rates, own_ids[:, None]]
        + [(ids[rim - j : rim - j + row_count] == own_ids).astype(F32)[:, None] for j in (1, 2, 3)]
        + [jnp.zeros((row_count, heads - 4), F32)],
        1,
    )
    rows = jnp.concatenate(
        [
            jnp.swapaxes(rates.reshape(blocks, SPAN, heads), 1, 2),
            own_ids.reshape(blocks, 1, SPAN),
            jnp.broadcast_to(before[:, None, None], (blocks, 1, SPAN)),
            jnp.zeros((blocks, heads - 2, SPAN), F32),
        ],
        1,
    )
    second.move("zc", after=[cols])
    key_low, value_low, w, u, a, moves = delta_summary(kv_pre, kv_taps, cols, rows, heads)
    moves = hold(moves, second.got("zy"), third.got("v", "w"))
    second.move("zyc", after=[moves])
    third.move("vw", after=[moves])
    fourth.move("v", "w", after=[moves])
    third.pile()
    third.move("zy", "zx")
    fanout = here.nf // heads
    if fanout > 1:
        moves = jnp.concatenate(
            [
                to_owners(moves[:, :, :head_dim], fanout),
                jnp.repeat(moves[:, :, head_dim:], fanout, axis=0),
            ],
            axis=2,
        )
    owned = swap(moves)
    qg_full, outw_full = second.place()
    qg_pre = jnp.dot(normed_ext, qg_full, preferred_element_type=F32)
    fourth.move("vw", after=[owned])
    fourth.pile()
    third.move("zyx", after=[owned])
    third.move("zc", "zxc", "zyc", after=[owned])
    entry = swap(scan_states(owned))
    if fanout > 1:
        entry = to_heads(entry, fanout)
    fourth.move("zy", after=[entry] + third.got("zy"))
    fourth.move("zc", after=[entry])
    query_low, gated_low, attn_heads, fresh, kept = delta_forward(
        qg_pre, query_taps, key_low, w, u, cols, rows, entry, outgain_scale, heads
    )
    third.move("zyxc", after=[gated_low])
    fourth.move("zyc", after=[gated_low])
    middle = residual + jnp.dot(gated_low, outw_full, preferred_element_type=F32)
    normed_two, norm_two_back = jax.vjp(rms_norm, middle, ffngain_scale)
    normed_two_low = normed_two.astype(BF)
    (pair_full,) = third.place()
    pair_pre = jnp.dot(normed_two_low, pair_full, preferred_element_type=F32)
    hidden_ff, swiglu_back = jax.vjp(swiglu, pair_pre)
    hidden_low = hidden_ff.astype(BF)
    (down_full,) = fourth.place()

    c = here.mine["c"]

    def shares(array, start, size):
        half = size // 2
        cut = [lax.dynamic_slice_in_dim(array, start + at * half, half, 1) for at in (1 - c, c)]
        return cut

    hidden_grad = contract(cotangent, down_full, 1, 1)
    theirs, ours = shares(cotangent, 0, width)
    down_sum = Reduce(here)
    down_sum.swap(contract(hidden_low, theirs, 0, 0))
    (pair_grad,) = swiglu_back(hidden_grad)
    pair_low = pair_grad.astype(BF)
    hidden_sums = [Reduce(here), Reduce(here)]
    quarter = hidden_units // 2
    nears = []
    for i, one in enumerate(hidden_sums):
        away = lax.dynamic_slice_in_dim(pair_low, (1 - c) * hidden_units + i * quarter, quarter, 1)
        nears.append(lax.dynamic_slice_in_dim(pair_low, c * hidden_units + i * quarter, quarter, 1))
        one.swap(contract(normed_two_low, away, 0, 0))
    hidden_a, hidden_b = hidden_sums
    down_sum.take(contract(hidden_low, hold(ours, pair_low), 0, 0))
    top_grad = cotangent.astype(F32)
    normed_two_grad = contract(pair_low, pair_full, 1, 1)
    middle_back, ffngain_grad = norm_two_back(normed_two_grad)
    middle_grad = top_grad + middle_back
    middle_low = middle_grad.astype(BF)
    gated_grad = contract(middle_low, outw_full, 1, 1)
    gated_grad = hold(gated_grad, down_sum.part, hidden_a.came, hidden_b.came)
    down_sum.step("y")
    heads_grad, gatepre_low, outgain_grad, local_later = delta_adjoint(
        query_low, key_low, w, cols, rows, gated_grad, attn_heads, qg_pre, outgain_scale, heads
    )
    local_later = hold(local_later, down_sum.part)
    if fanout > 1:
        local_later = to_owners(local_later, fanout)
    came_later = swap(local_later)

    near_a, near_b = hold(tuple(nears), local_later)
    hidden_a.take(contract(normed_two_low, near_a, 0, 0))
    hidden_b.take(contract(normed_two_low, near_b, 0, 0))
    down_sum.step("w", local_later)
    came_later = hold(came_later, hidden_a.part, hidden_b.part)
    hidden_a.step("x")
    hidden_b.step("y")
    later = swap(scan_grads(owned, came_later))
    if fanout > 1:
        later = to_heads(later, fanout)
    hidden_held, middle_held, gatepre_held = hold((hidden_low, middle_low, gatepre_low), came_later)
    output = (middle + jnp.dot(hidden_held, down_full, preferred_element_type=F32)).astype(BF)
    out_grad = contract(gated_low, middle_held, 0, 0)
    gate_grad = contract(normed_low, gatepre_held, 0, 0)
    other_sum = Reduce(here)
    other_sum.swap(by_core(here, gate_grad, out_grad))
    later = hold(later, down_sum.part, output, hidden_a.part, hidden_b.part, other_sum.came)
    other_sum.take(by_core(here, out_grad, gate_grad))
    later = hold(later, other_sum.part)
    down_sum.step("v")
    hidden_a.step("y")
    hidden_b.step("w")
    other_sum.step("x")
    state = (query_low, key_low, value_low, w, u, a, fresh, kept, heads_grad, cols, rows)
    mixed_a, beta_a, taps_a = delta_backward(
        0, *state, later, qg_pre, query_taps, kv_pre, kv_taps, heads
    )
    mixed_a = hold(mixed_a, down_sum.part, hidden_a.part, hidden_b.part, other_sum.part)
    a_sum = Reduce(here)
    size = 3 * width // 2
    theirs, ours = shares(mixed_a, 0, size)
    a_sum.swap(contract(normed_ext, theirs, 0, 0))
    a_sum.take(contract(normed_ext, ours, 0, 0))
    later = hold(later, a_sum.part)
    a_sum.step("x")
    hidden_a.step("w", mixed_a)
    hidden_b.step("v", mixed_a)
    other_sum.step("y", mixed_a)
    mixed_b, beta_b, taps_b = delta_backward(
        1, *state, later, qg_pre, query_taps, kv_pre, kv_taps, heads
    )
    mixed_b = hold(mixed_b, hidden_a.part, hidden_b.part, other_sum.part, a_sum.part)
    b_sum = Reduce(here)
    theirs, ours = shares(mixed_b, 0, size)
    b_sum.swap(contract(normed_ext, theirs, 0, 0))
    b_sum.take(contract(normed_ext, ours, 0, 0))
    mixed_b = hold(mixed_b, b_sum.part)
    b_sum.step("x")
    a_sum.step("y", mixed_b)
    hidden_a.step("v", mixed_b)
    other_sum.step("w", mixed_b)
    betapre_low = (beta_a + beta_b).astype(BF)
    beta_grad = contract(normed_low, betapre_low, 0, 0)[:, :heads]
    eighth = width // 2
    wide_grad = (
        contract(mixed_a[:, eighth:], kv_full[:, :width], 1, 1)
        + contract(mixed_b[:, eighth:], kv_full[:, width:], 1, 1)
        + contract(mixed_a[:, :eighth], qg_full[:, :eighth], 1, 1)
        + contract(mixed_b[:, :eighth], qg_full[:, eighth:width], 1, 1)
    )
    rim_grad = from_behind(wide_grad[row_count:].astype(BF), -1).astype(F32)
    normed_grad = hold(
        wide_grad[:row_count]
        + jnp.pad(rim_grad, ((row_count - rim, 0), (0, 0)))
        + contract(betapre_low, extra_full, 1, 1)
        + contract(gatepre_low, qg_full[:, width:], 1, 1),
        a_sum.part,
    )
    input_back, attngain_grad = jax.vjp(rms_norm, residual, attn_scale)[1](normed_grad)
    input_grad = (middle_grad + input_back).astype(BF)

    def by_kind(first_heads, other_heads):
        cut = [slice(i * eighth, (i + 1) * eighth) for i in range(3)]
        both = [array[:, s] for s in cut for array in (first_heads, other_heads)]
        return jnp.concatenate(both, axis=1)

    taps_grad = by_kind(taps_a, taps_b)
    parts = (
        attngain_grad.reshape(here.nf, -1),
        outgain_grad.reshape(here.nf, -1),
        ffngain_grad.reshape(here.nf, -1),
        jnp.swapaxes(taps_grad.reshape(taps_count, here.nf, -1), 0, 1).reshape(here.nf, -1),
    )
    flat = jnp.concatenate(parts, axis=1)
    flat = jnp.pad(flat, ((0, 0), (0, columns * shard_rows - flat.shape[1])))
    extra = jnp.concatenate(
        [
            beta_grad,
            flat.reshape(width, columns),
            jnp.zeros((width, lanes - heads - columns), F32),
        ],
        axis=1,
    )
    small_sum = Reduce(here)
    small_sum.begin(extra)
    first_tail = (b_sum.part, hidden_a.part, other_sum.part, a_sum.part)
    b_sum.step("y", *first_tail)
    a_sum.step("w", *first_tail)
    other_sum.step("v", *first_tail)
    down_sum.step("x", *first_tail)
    small_sum.step("y", b_sum.part)
    second_tail = (b_sum.part, a_sum.part, other_sum.part, down_sum.part)
    b_sum.step("w", *second_tail)
    a_sum.step("v", *second_tail)
    hidden_b.step("x", *second_tail)
    small_sum.step("w", b_sum.part)
    b_sum.step("v", a_sum.part, hidden_b.part)
    small_sum.step("v", b_sum.part)
    small_sum.step("x")
    small_sum.step("c")
    for done in (hidden_a, other_sum, a_sum, b_sum):
        done.rows()
    hidden = jnp.concatenate([hidden_a.part, hidden_b.part], axis=1)
    other = here.send(hidden, "c")
    hidgate_total = by_core(here, hidden, other).astype(F32)
    hidup_total = by_core(here, other, hidden).astype(F32)
    other = other_sum.other()
    outproj_total = by_core(here, other_sum.part, other).astype(F32)
    gate_total = by_core(here, other, other_sum.part).astype(F32)
    down_total = join_way(here, down_sum.part, "c", 1).astype(F32)
    qkv_total = by_kind(
        join_way(here, a_sum.part, "c", 1), join_way(here, b_sum.part, "c", 1)
    ).astype(F32)
    extra = small_sum.part.astype(F32)
    flat = extra[:, heads : heads + columns].reshape(-1)
    cut, at = [], 0
    for part in parts:
        cut.append(flat[at : at + part.shape[1]])
        at += part.shape[1]
    return (
        output,
        input_grad,
        cut[0],
        qkv_total,
        extra[:, :heads],
        gate_total,
        cut[3].reshape(conv_taps.shape),
        cut[1],
        outproj_total,
        cut[2],
        hidgate_total,
        hidup_total,
        down_total,
    )


def solution(mesh):
    placed = (
        P(("rep", "fsdp"), None),
        P(("rep", "fsdp")),
        P("fsdp"),
        P("fsdp", None),
        P("fsdp", None),
        P("fsdp", None),
        P(None, "fsdp"),
        P("fsdp"),
        P("fsdp", None),
        P("fsdp"),
        P("fsdp", None),
        P("fsdp", None),
        P("fsdp", None),
        P(("rep", "fsdp"), None),
    )
    return jax.shard_map(
        on_device,
        mesh=mesh,
        in_specs=placed,
        out_specs=(
            P(("rep", "fsdp"), None),
            P(("rep", "fsdp"), None),
            P("fsdp"),
            P("fsdp", None),
            P("fsdp", None),
            P("fsdp", None),
            P(None, "fsdp"),
            P("fsdp"),
            P("fsdp", None),
            P("fsdp"),
            P("fsdp", None),
            P("fsdp", None),
            P("fsdp", None),
        ),
        check_vma=False,
    )
```

```python
from functools import partial

import jax
import jax.numpy as jnp
from jax import lax
from jax.experimental import pallas as pl
from jax.experimental.pallas import tpu as pltpu
from jax.sharding import PartitionSpec as P

SPAN = 64
EPSILON = 1e-06
BF = jnp.bfloat16
F32 = jnp.float32


def nn(a, b):
    return lax.dot_general(a, b, (((1,), (0,)), ((), ())), preferred_element_type=F32)


def nt(a, b):
    return lax.dot_general(a, b, (((1,), (1,)), ((), ())), preferred_element_type=F32)


def tn(a, b):
    return lax.dot_general(a, b, (((0,), (0,)), ((), ())), preferred_element_type=F32)


def block_masks(cols_ref, rows_ref, heads):
    n = SPAN
    row = lax.broadcasted_iota(jnp.int32, (n, n), 0)
    col = lax.broadcasted_iota(jnp.int32, (n, n), 1)
    ids = cols_ref[:, heads : heads + 1]
    ids_row = rows_ref[0, heads : heads + 1, :]
    before = rows_ref[0, heads + 1 : heads + 2, :]
    end = ids_row[:, n - 1 : n]
    same = ids == ids_row
    first = (ids == before[:, :1]).astype(F32)
    last = (ids == end).astype(F32)
    keep = (end == before[:, :1]).astype(F32)
    return row, col, same, first, last, keep


def sigmoid(z):
    return 0.5 * jnp.tanh(0.5 * z) + 0.5


def shifted_rows(x, prev, masks):
    both = jnp.concatenate([prev, x], axis=0)
    lead = prev.shape[0]
    return [x] + [both[lead - j : lead - j + x.shape[0]] * masks[j - 1] for j in (1, 2, 3)]


def mix_rows(rows, taps):
    mixed = rows[0] * taps[0:1]
    for j in (1, 2, 3):
        mixed = mixed + rows[j] * taps[j : j + 1]
    return mixed


def lag_masks(cols_ref, heads):
    return [cols_ref[:, heads + j : heads + j + 1] for j in (1, 2, 3)]


def kv_at(heads, d, h):
    half = heads // 2
    start = (h // half) * 2 * half * d + (h % half) * d
    return slice(start, start + d), slice(start + half * d, start + half * d + d)


def summary_kernel(
    heads, d, pre_ref, prev_ref, taps_ref, cols_ref, rows_ref,
    k_ref, v_ref, w_ref, u_ref, a_ref, x_ref, state,
):
    n = SPAN
    block = pl.program_id(0)

    @pl.when(block == 0)
    def _():
        r = lax.broadcasted_iota(jnp.int32, (d, 2 * d), 0)
        c = lax.broadcasted_iota(jnp.int32, (d, 2 * d), 1)
        unit = (r + d == c).astype(F32)
        for h in range(heads):
            state[h] = unit

    row, col, same, first, last, keep = block_masks(cols_ref, rows_ref, heads)
    lower = jnp.logical_and(same, row > col)
    unit = (row == col).astype(F32)
    pair = jnp.logical_and(row == col + 1, (row & 1) == 1)
    masks = lag_masks(cols_ref, heads)
    keys = []
    mixing = []
    inverse = []
    for h in range(heads):
        cut = slice(h * d, (h + 1) * d)
        at_k, at_v = kv_at(heads, d, h)
        z = mix_rows(shifted_rows(pre_ref[:, at_k], prev_ref[:, at_k], masks), taps_ref[:, at_k])
        act = z * sigmoid(z)
        root = lax.rsqrt(jnp.sum(act * act, axis=1, keepdims=True) + EPSILON)
        keys.append((act * root).astype(BF))
        k_ref[:, cut] = keys[h]
        z = mix_rows(shifted_rows(pre_ref[:, at_v], prev_ref[:, at_v], masks), taps_ref[:, at_v])
        v_ref[:, cut] = (z * sigmoid(z)).astype(BF)
        m = jnp.where(lower, nt(keys[h], keys[h]) * cols_ref[:, h : h + 1], 0.0)
        mixing.append(m)
        inverse.append((unit - jnp.where(pair, m, 0.0)).astype(BF))
    size = 2
    while size < n:
        level = jnp.logical_and(
            (row // (2 * size)) == (col // (2 * size)),
            jnp.logical_and(((row // size) & 1) == 1, ((col // size) & 1) == 0),
        )
        inner = [nn(jnp.where(level, mixing[h], 0.0).astype(BF), inverse[h]).astype(BF) for h in range(heads)]
        for h in range(heads):
            inverse[h] = inverse[h] - jnp.where(level, nn(inverse[h], inner[h]), 0.0).astype(BF)
        size *= 2
    for h in range(heads):
        cut = slice(h * d, (h + 1) * d)
        a_ref[h] = inverse[h]
        scaled = (inverse[h].astype(F32) * rows_ref[0, h : h + 1, :]).astype(BF)
        both = nn(scaled, jnp.concatenate([keys[h], v_ref[:, cut]], axis=1))
        w = both[:, :d].astype(BF)
        u = both[:, d:].astype(BF)
        w_ref[:, cut] = w
        u_ref[:, cut] = u
        held = state[h]
        moved = nn(w, held.astype(BF)) * first
        fresh = (jnp.concatenate([u.astype(F32), jnp.zeros((n, d), F32)], axis=1) - moved).astype(BF)
        key_last = (keys[h].astype(F32) * last).astype(BF)
        state[h] = keep * held + tn(key_last, fresh)

    @pl.when(block == pl.num_programs(0) - 1)
    def _():
        x_ref[...] = state[...].astype(BF)


def forward_kernel(
    heads, d, pre_ref, prev_ref, taps_ref, k_ref, w_ref, u_ref, cols_ref, rows_ref, s_ref, gate_ref, gain_ref,
    q_ref, y_ref, o_ref, e_ref, kept_ref, state,
):
    n = SPAN
    block = pl.program_id(0)

    @pl.when(block == 0)
    def _():
        state[...] = s_ref[...].astype(F32)

    row, col, same, first, last, keep = block_masks(cols_ref, rows_ref, heads)
    visible = jnp.logical_and(same, row >= col)
    masks = lag_masks(cols_ref, heads)
    for h in range(heads):
        cut = slice(h * d, (h + 1) * d)
        z = mix_rows(shifted_rows(pre_ref[:, cut], prev_ref[:, cut], masks), taps_ref[:, cut])
        q = (z * sigmoid(z) * d ** (-0.5)).astype(BF)
        q_ref[:, cut] = q
        k, w = k_ref[:, cut], w_ref[:, cut]
        held = state[h]
        held_low = held.astype(BF)
        kept_ref[0, h] = held_low
        both = nn(jnp.concatenate([w, q], axis=0), held_low)
        fresh = (u_ref[:, cut].astype(F32) - first * both[:n]).astype(BF)
        e_ref[:, cut] = fresh
        scores = jnp.where(visible, nt(q, k), 0.0).astype(BF)
        out = first * both[n:] + nn(scores, fresh)
        key_last = (k.astype(F32) * last).astype(BF)
        state[h] = keep * held + tn(key_last, fresh)
        o_ref[:, cut] = out
        g = gate_ref[:, cut]
        root = lax.rsqrt(jnp.mean(out * out, axis=1, keepdims=True) + EPSILON)
        y_ref[:, cut] = (out * root * gain_ref[...] * (g * sigmoid(g))).astype(BF)


def adjoint_kernel(
    heads, d, q_ref, k_ref, w_ref, cols_ref, rows_ref, dy_ref, o_ref, gate_ref, gain_ref,
    do_ref, dgate_ref, dgain_ref, ds_ref, state,
):
    n = SPAN
    step = pl.program_id(0)

    @pl.when(step == 0)
    def _():
        state[...] = jnp.zeros_like(state)
        dgain_ref[...] = jnp.zeros_like(dgain_ref)

    row, col, same, first, last, keep = block_masks(cols_ref, rows_ref, heads)
    visible = jnp.logical_and(same, row >= col)
    gain = gain_ref[...]
    gain_sum = jnp.zeros((1, d), F32)
    for h in range(heads):
        cut = slice(h * d, (h + 1) * d)
        q, k, w = q_ref[:, cut], k_ref[:, cut], w_ref[:, cut]
        o, g, dy = o_ref[:, cut], gate_ref[:, cut], dy_ref[:, cut]
        root = lax.rsqrt(jnp.mean(o * o, axis=1, keepdims=True) + EPSILON)
        unit = o * root
        sig = sigmoid(g)
        m = g * sig
        t = dy * m
        gain_sum = gain_sum + jnp.sum(t * unit, axis=0, keepdims=True)
        tg = t * gain
        do = root * (tg - unit * jnp.mean(tg * unit, axis=1, keepdims=True))
        dgate_ref[:, cut] = (dy * gain * unit * (sig * (1.0 + g * (1.0 - sig)))).astype(BF)
        do_low = do.astype(BF)
        do_ref[:, cut] = do_low
        scores = jnp.where(visible, nt(q, k), 0.0).astype(BF)
        later = state[h]
        de = last * nn(k, later.astype(BF)) + tn(scores, do_low)
        left = jnp.concatenate([q.astype(F32) * first, w.astype(F32) * (-first)], axis=0).astype(BF)
        right = jnp.concatenate([do_low, de.astype(BF)], axis=0)
        state[h] = keep * later + tn(left, right)
    dgain_ref[...] += gain_sum

    @pl.when(step == pl.num_programs(0) - 1)
    def _():
        ds_ref[...] = state[...].astype(BF)


def backward_kernel(
    heads, part, d, q_ref, k_ref, v_ref, w_ref, u_ref, a_ref, e_ref, kept_ref, do_ref, cols_ref, rows_ref, s_ref,
    qpre_ref, qprev_ref, qtaps_ref, kvpre_ref, kvprev_ref, kvtaps_ref,
    dpre_ref, dbeta_ref, dtaps_ref, state, carry,
):
    n = SPAN
    step = pl.program_id(0)
    number = heads // 2

    @pl.when(step == 0)
    def _():
        state[...] = s_ref[...].astype(F32)
        carry[...] = jnp.zeros_like(carry)
        dtaps_ref[...] = jnp.zeros_like(dtaps_ref)

    @pl.when(step < pl.num_programs(0) - 1)
    def _():
        row, col, same, first, last, keep = block_masks(cols_ref, rows_ref, heads)
        visible = jnp.logical_and(same, row >= col)
        lower = jnp.logical_and(same, row > col)
        lane = lax.broadcasted_iota(jnp.int32, (n, d), 1)
        masks = lag_masks(cols_ref, heads)
        rate_grads = jnp.zeros((n, d), F32)

        def conv_back(dact, z, sig, rows, taps, at):
            dconv = dact * (sig * (1.0 + z * (1.0 - sig)))
            here = slice(at, at + d)
            dtaps_ref[:, here] += jnp.concatenate(
                [jnp.sum(dconv * r, axis=0, keepdims=True) for r in rows], axis=0
            )
            dpre = dconv * taps[0:1]
            for j in (1, 2, 3):
                masked = dconv * masks[j - 1]
                both = jnp.concatenate([masked, carry[j - 1, :, here]], axis=0)
                dpre = dpre + both[j : n + j] * taps[j : j + 1]
                carry[j - 1, :, here] = masked[:8]
            dpre_ref[:, here] = dpre.astype(BF)

        for h in range(number):
            cut = slice(h * d, (h + 1) * d)
            cut_v = slice((number + h) * d, (number + h + 1) * d)
            q, k, v, w, u = q_ref[:, cut], k_ref[:, cut], v_ref[:, cut], w_ref[:, cut], u_ref[:, cut]
            do, e, held = do_ref[:, cut], e_ref[:, cut], kept_ref[0, h]
            at = part * number + h
            rate = cols_ref[:, at : at + 1]
            later = state[h]
            later_low = later.astype(BF)
            scores = jnp.where(visible, nt(q, k), 0.0).astype(BF)
            de = last * nn(k, later_low) + tn(scores, do)
            de_low = de.astype(BF)
            dscores = jnp.where(visible, nt(do, e), 0.0).astype(BF)
            both = nt(jnp.concatenate([do, de_low], axis=0), held)
            dq = first * both[:n] + nn(dscores, k)
            dw = -first * both[n:]
            dk = tn(dscores, q) + last * nt(e, later_low)
            pg = tn(a_ref[h], jnp.concatenate([dw.astype(BF), de_low], axis=1))
            p, g = pg[:, :d], pg[:, d:]
            dmix = jnp.where(lower, -nt(pg.astype(BF), jnp.concatenate([w, u], axis=1)), 0.0).astype(BF)
            kf = k.astype(F32)
            drk = p + nn(dmix, k)
            dk = dk + tn(dmix, (kf * rate).astype(BF)) + rate * drk
            dr = jnp.sum(drk * kf + g * v.astype(F32), axis=1, keepdims=True)
            rate_grads = jnp.where(lane == at, dr * rate * (1.0 - rate), rate_grads)
            left = jnp.concatenate([q.astype(F32) * first, w.astype(F32) * (-first)], axis=0).astype(BF)
            right = jnp.concatenate([do, de_low], axis=0)
            state[h] = keep * later + tn(left, right)

            taps = qtaps_ref[:, cut]
            rows = shifted_rows(qpre_ref[:, cut], qprev_ref[:, cut], masks)
            z = mix_rows(rows, taps)
            conv_back(dq * d ** (-0.5), z, sigmoid(z), rows, taps, h * d)
            taps = kvtaps_ref[:, cut]
            rows = shifted_rows(kvpre_ref[:, cut], kvprev_ref[:, cut], masks)
            z = mix_rows(rows, taps)
            sig = sigmoid(z)
            act = z * sig
            root = lax.rsqrt(jnp.sum(act * act, axis=1, keepdims=True) + EPSILON)
            unit = act * root
            dact = root * (dk - unit * jnp.sum(unit * dk, axis=1, keepdims=True))
            conv_back(dact, z, sig, rows, taps, (number + h) * d)
            taps = kvtaps_ref[:, cut_v]
            rows = shifted_rows(kvpre_ref[:, cut_v], kvprev_ref[:, cut_v], masks)
            z = mix_rows(rows, taps)
            conv_back(rate * g, z, sigmoid(z), rows, taps, (2 * number + h) * d)
        dbeta_ref[...] = rate_grads

    @pl.when(step == pl.num_programs(0) - 1)
    def _():
        wide = number * d
        for i, taps_ref, at in ((0, qtaps_ref, 0), (1, kvtaps_ref, 0), (2, kvtaps_ref, wide)):
            here = slice(i * wide, (i + 1) * wide)
            dpre = jnp.zeros((8, wide), F32)
            for j in (1, 2, 3):
                held = carry[j - 1, :, here]
                both = jnp.concatenate([jnp.zeros_like(held), held], axis=0)
                dpre = dpre + both[j : 8 + j] * taps_ref[j : j + 1, at : at + wide]
            dpre_ref[0:8, here] = dpre.astype(BF)


def prefix_kernel(peers, x_ref, out_ref):
    cols = out_ref.shape[2]
    held = jnp.zeros(out_ref.shape[1:], F32)
    for i in range(peers):
        out_ref[i] = held.astype(BF)
        held = nn(x_ref[i, :, cols:], held.astype(BF)) + x_ref[i, :, :cols].astype(F32)


def suffix_kernel(peers, t_ref, g_ref, out_ref):
    held = jnp.zeros(out_ref.shape[1:], F32)
    cols = out_ref.shape[2]
    for i in reversed(range(peers)):
        out_ref[i] = held.astype(BF)
        held = tn(t_ref[i, :, cols:], held.astype(BF)) + g_ref[i].astype(F32)


VMEM_LIMIT = 16 * 1024 * 1024


def in_hbm(*arrays):
    return [pltpu.with_memory_space_constraint(a, pltpu.HBM) for a in arrays]


def params():
    return pltpu.CompilerParams(dimension_semantics=("arbitrary",), vmem_limit_bytes=VMEM_LIMIT)


def cost(microseconds):
    return pl.CostEstimate(
        flops=int(microseconds * 1e9), bytes_accessed=int(microseconds * 3e6), transcendentals=0
    )


def specs(blocks, heads, d, flip):
    at = (lambda b: blocks - 1 - b) if flip else (lambda b: b)
    wide = pl.BlockSpec((SPAN, heads * d), lambda b: (at(b), 0))
    cols = pl.BlockSpec((SPAN, 2 * heads), lambda b: (at(b), 0))
    rows = pl.BlockSpec((1, 2 * heads, SPAN), lambda b: (at(b), 0, 0))
    state = pl.BlockSpec((heads, d, d), lambda b: (0, 0, 0))
    mix = pl.BlockSpec((heads, SPAN, SPAN), lambda b: (0, at(b), 0))
    kept = pl.BlockSpec((1, heads, d, d), lambda b: (at(b), 0, 0, 0))
    gain = pl.BlockSpec((1, d), lambda b: (0, 0))
    return wide, cols, rows, state, mix, kept, gain


def shape(dims, kind):
    return jax.ShapeDtypeStruct(dims, kind)


def before_block(blocks, rim, flip, size, column):
    def index(step):
        b = blocks - 1 - jnp.minimum(step, blocks - 1) if flip else step
        per = SPAN // rim
        return jnp.where(b == 0, blocks * per, b * per - 1), column

    return pl.BlockSpec((rim, size), index)


def delta_summary(pre, taps, cols, rows, heads):
    count, width = cols.shape[0], pre.shape[1] // 2
    d, blocks = width // heads, count // SPAN
    rim = pre.shape[0] - count
    wide, c, r, state, mix, kept, gain = specs(blocks, heads, d, False)
    return pl.pallas_call(
        partial(summary_kernel, heads, d),
        grid=(blocks,),
        in_specs=[
            pl.BlockSpec((SPAN, 2 * width), lambda b: (b, 0)),
            before_block(blocks, rim, False, 2 * width, 0),
            pl.BlockSpec((4, 2 * width), lambda b: (0, 0)),
            c,
            r,
        ],
        out_specs=[wide, wide, wide, wide, mix, pl.BlockSpec((heads, d, 2 * d), lambda b: (0, 0, 0))],
        out_shape=[
            shape((count, width), BF),
            shape((count, width), BF),
            shape((count, width), BF),
            shape((count, width), BF),
            shape((heads, count, SPAN), BF),
            shape((heads, d, 2 * d), BF),
        ],
        scratch_shapes=[pltpu.VMEM((heads, d, 2 * d), F32)],
        compiler_params=params(),
        cost_estimate=cost(24),
        name="delta_summary",
    )(*in_hbm(pre, pre, taps, cols, rows))


def delta_forward(pre, taps, k, w, u, cols, rows, entry, gain_full, heads):
    count, width = k.shape
    d, blocks = width // heads, count // SPAN
    rim = pre.shape[0] - count
    wide, c, r, state, mix, kept, gain = specs(blocks, heads, d, False)
    return pl.pallas_call(
        partial(forward_kernel, heads, d),
        grid=(blocks,),
        in_specs=[
            wide,
            before_block(blocks, rim, False, width, 0),
            pl.BlockSpec((4, width), lambda b: (0, 0)),
            wide,
            wide,
            wide,
            c,
            r,
            state,
            pl.BlockSpec((SPAN, width), lambda b: (b, 1)),
            gain,
        ],
        out_specs=[wide, wide, wide, wide, kept],
        out_shape=[
            shape((count, width), BF),
            shape((count, width), BF),
            shape((count, width), F32),
            shape((count, width), BF),
            shape((blocks, heads, d, d), BF),
        ],
        scratch_shapes=[pltpu.VMEM((heads, d, d), F32)],
        compiler_params=params(),
        cost_estimate=cost(16),
        name="delta_forward",
    )(*in_hbm(pre, pre, taps, k, w, u, cols, rows, entry, pre, gain_full))


def delta_adjoint(q, k, w, cols, rows, dy, o, gate, gain_full, heads):
    count, width = k.shape
    d, blocks = width // heads, count // SPAN
    wide, c, r, state, mix, kept, gain = specs(blocks, heads, d, True)
    return pl.pallas_call(
        partial(adjoint_kernel, heads, d),
        grid=(blocks,),
        in_specs=[
            wide,
            wide,
            wide,
            c,
            r,
            wide,
            wide,
            pl.BlockSpec((SPAN, width), lambda b: (blocks - 1 - b, 1)),
            gain,
        ],
        out_specs=[wide, wide, gain, state],
        out_shape=[
            shape((count, width), BF),
            shape((count, width), BF),
            shape((1, d), F32),
            shape((heads, d, d), BF),
        ],
        scratch_shapes=[pltpu.VMEM((heads, d, d), F32)],
        compiler_params=params(),
        cost_estimate=cost(15),
        name="delta_adjoint",
    )(*in_hbm(q, k, w, cols, rows, dy, o, gate, gain_full))


def delta_backward(part, q, k, v, w, u, a, e, kept_states, do, cols, rows, later, qg_pre, qtaps, kv_pre, kvtaps, heads):
    count, width = k.shape
    d, blocks = width // heads, count // SPAN
    rim = kv_pre.shape[0] - count
    number = heads // 2
    size = number * d

    def at(step):
        return blocks - 1 - jnp.minimum(step, blocks - 1)

    wide = pl.BlockSpec((SPAN, size), lambda b: (at(b), part))
    in_specs = [
        wide,
        wide,
        wide,
        wide,
        wide,
        pl.BlockSpec((number, SPAN, SPAN), lambda b: (part, at(b), 0)),
        wide,
        pl.BlockSpec((1, number, d, d), lambda b: (at(b), part, 0, 0)),
        wide,
        pl.BlockSpec((SPAN, 2 * heads), lambda b: (at(b), 0)),
        pl.BlockSpec((1, 2 * heads, SPAN), lambda b: (at(b), 0, 0)),
        pl.BlockSpec((number, d, d), lambda b: (part, 0, 0)),
        wide,
        before_block(blocks, rim, True, size, part),
        pl.BlockSpec((4, size), lambda b: (0, part)),
        pl.BlockSpec((SPAN, 2 * size), lambda b: (at(b), part)),
        before_block(blocks, rim, True, 2 * size, part),
        pl.BlockSpec((4, 2 * size), lambda b: (0, part)),
    ]
    return pl.pallas_call(
        partial(backward_kernel, heads, part, d),
        grid=(blocks + 1,),
        in_specs=in_specs,
        out_specs=[
            pl.BlockSpec((SPAN, 3 * size), lambda b: (jnp.where(b < blocks, blocks - 1 - b, blocks), 0)),
            pl.BlockSpec((SPAN, d), lambda b: (at(b), 0)),
            pl.BlockSpec((4, 3 * size), lambda b: (0, 0)),
        ],
        out_shape=[
            shape((count + rim, 3 * size), BF),
            shape((count, d), F32),
            shape((4, 3 * size), F32),
        ],
        scratch_shapes=[pltpu.VMEM((number, d, d), F32), pltpu.VMEM((3, rim, 3 * size), F32)],
        compiler_params=params(),
        cost_estimate=cost(32),
        name="delta_backward",
    )(*in_hbm(q, k, v, w, u, a, e, kept_states, do, cols, rows, later, qg_pre, qg_pre, qtaps, kv_pre, kv_pre, kvtaps))


def scan_states(x):
    peers, d, width = x.shape
    return pl.pallas_call(
        partial(prefix_kernel, peers),
        out_shape=shape((peers, d, width - d), BF),
        cost_estimate=cost(3),
        name="state_prefix",
    )(x)


def scan_grads(x, g):
    peers, d, width = g.shape
    return pl.pallas_call(
        partial(suffix_kernel, peers),
        out_shape=shape((peers, d, width), BF),
        cost_estimate=cost(3),
        name="state_suffix",
    )(x, g)


def hold(value, *after):
    return lax.optimization_barrier((value, after))[0]


class Place:
    def __init__(self):
        self.nf, self.nr = lax.axis_size("fsdp"), lax.axis_size("rep")
        self.ny = self.nf // 4
        self.nx = self.nr // 2
        self.f, self.r = lax.axis_index("fsdp"), lax.axis_index("rep")
        z = self.f // self.ny
        self.mine = {"v": z // 2, "w": z % 2, "y": self.f % self.ny, "x": self.r // 2, "c": self.r % 2}
        self.number = {"v": 2, "w": 2, "u": 2, "y": self.ny, "x": self.nx, "c": 2}
        self.stride = {"v": 2 * self.ny, "w": self.ny, "y": 1, "x": 2, "c": 1}

    def send(self, value, way, steps=1):
        if way == "u":
            return lax.ppermute(value, "fsdp", [(i, i ^ 3 * self.ny) for i in range(self.nf)])
        axis = "rep" if way in "xc" else "fsdp"
        total = self.nr if way in "xc" else self.nf
        number, stride = self.number[way], self.stride[way]
        pairs = []
        for i in range(total):
            at = i // stride % number
            pairs.append((i, i + ((at + steps) % number - at) * stride))
        return lax.ppermute(value, axis, pairs)


def place_kernel(count, rows, each, by_rows, widths, offs_ref, own_ref, *refs):
    stacks, outs, sems = refs[: len(count)], refs[len(count) : -1], refs[-1]
    copies = []

    def put(src, row, height, column, out):
        copy = pltpu.make_async_copy(src, out.at[pl.ds(row, height), column], sems.at[len(copies)])
        copy.start()
        copies.append(copy)

    starts = [sum(widths[:i]) for i in range(len(widths))]
    top = pl.multiple_of(offs_ref[0], rows)
    for start, width, out in zip(starts, widths, outs):
        put(own_ref.at[:, pl.ds(start, width)], top, rows, pl.ds(0, width), out)
    at = 1
    for stack, number in zip(stacks, count):
        for j in range(number):
            row = pl.multiple_of(offs_ref[at], each if by_rows else rows)
            if by_rows:
                for start, width, out in zip(starts, widths, outs):
                    put(stack.at[j, :, pl.ds(start, width)], row, each, pl.ds(0, width), out)
                at += 1
            else:
                column = pl.multiple_of(offs_ref[at + 1], each)
                put(stack.at[j], row, rows, pl.ds(column, each), outs[0])
                at += 2
    for copy in copies:
        copy.wait()


class Gather:
    def __init__(self, here, shard, widths, deep, by_rows=True):
        self.here, self.shard, self.widths, self.deep, self.by_rows = here, shard, widths, deep, by_rows
        rows, total = shard.shape
        parts = here.nr if deep else 2
        extent = rows if by_rows else total
        self.each = extent // parts
        self.plain = bool(extent % parts or self.each % (32 if by_rows else 128) or rows % 32)
        self.plain = self.plain or here.ny != 2 or here.nx != 2
        self.have = {}
        if self.plain:
            return
        part = here.r if deep else here.mine["c"]
        self.have[""] = lax.dynamic_slice_in_dim(shard, part * self.each, self.each, 0 if by_rows else 1)

    def got(self, *names):
        return [] if self.plain else [self.have[name] for name in names]

    def move(self, *names, after=()):
        if not self.plain:
            for name in names:
                self.have[name] = self.here.send(hold(self.have[name[:-1]], *after), name[-1])

    def pile(self):
        if not self.plain:
            self.have["z"] = jnp.stack([self.have[name] for name in ("", "w", "v", "vw")])

    def place(self):
        here, shard, widths = self.here, self.shard, self.widths
        rows, each = shard.shape[0], self.each
        if self.plain:
            whole = lax.all_gather(shard, "fsdp", axis=0, tiled=True)
            starts = [sum(widths[:i]) for i in range(len(widths))]
            return [whole[:, s : s + w] for s, w in zip(starts, widths)]
        mine = here.mine
        offsets = [here.f * rows]
        names = [name for name in self.have if name.startswith("z")]
        for name in names:
            x, c, y = ((mine[way] + (way in name)) % 2 for way in "xcy")
            inside = (x * 2 + c if self.deep else c) * each
            for j in range(4):
                v = (mine["v"] + j // 2) % 2
                w = (mine["w"] + j % 2) % 2
                source = (v * 2 + w) * here.ny + y
                offsets += [source * rows + inside] if self.by_rows else [source * rows, inside]
        offsets = jnp.stack(offsets).astype(jnp.int32)
        stacks = [self.have[name] for name in names]
        count = [4] * len(stacks)
        any_space = pl.BlockSpec(memory_space=pl.ANY)
        size = here.nf * rows
        return pl.pallas_call(
            partial(place_kernel, count, rows, each, self.by_rows, widths),
            grid_spec=pltpu.PrefetchScalarGridSpec(
                num_scalar_prefetch=1,
                grid=(1,),
                in_specs=[any_space] * (1 + len(stacks)),
                out_specs=[pl.BlockSpec((size, w), lambda i, o: (0, 0)) for w in widths],
                scratch_shapes=[pltpu.SemaphoreType.DMA(((1 + sum(count)) * len(widths),))],
            ),
            out_shape=[jax.ShapeDtypeStruct((size, w), shard.dtype) for w in widths],
            compiler_params=pltpu.CompilerParams(
                vmem_limit_bytes=2 * size * sum(widths) * 2 + (1 << 20)
            ),
            cost_estimate=cost(6),
            name="place_weights",
        )(offsets, shard, *stacks)


class Reduce:
    def __init__(self, here):
        self.here = here
        self.split = False

    def swap(self, away):
        self.away = away.astype(BF)
        self.came = self.here.send(self.away, "c")

    def take(self, part):
        self.begin(part + self.came.astype(F32))

    def begin(self, part):
        part = part.astype(BF)
        here = self.here
        rows = part.shape[0] // here.nf
        self.part = part.reshape(2, 2, here.ny, rows, part.shape[1])
        self.axes = ["v", "w", "y"]

    def go(self, way, *after):
        here = self.here
        part = hold(self.part, *after)
        number, mine = here.number[way], here.mine[way]
        if way in "xc" and not self.axes:
            self.total = part.astype(F32)
            self.got = [here.send(part, way, s) for s in range(1, number)]
            return
        if way == "x":
            axis = len(self.axes)
            shape = part.shape
            part = part.reshape(shape[:axis] + (number, shape[axis] // number) + shape[axis + 1 :])
            self.split = True
        else:
            axis = self.axes.index(way)
            self.axes.pop(axis)
        self.total = lax.dynamic_index_in_dim(part, mine, axis, keepdims=False).astype(F32)
        self.got = [
            here.send(
                lax.dynamic_index_in_dim(part, (mine + s) % number, axis, keepdims=False), way, s
            )
            for s in range(1, number)
        ]

    def begin_x(self, part, *after):
        self.part, self.axes = part, []
        self.go("x", *after)

    def both(self):
        self.total = self.part.astype(F32)
        self.got = [self.here.send(self.part, "c")]

    def end(self):
        total = self.total
        for came in self.got:
            total = total + came.astype(F32)
        self.part = total.astype(BF)

    def step(self, way, *after):
        self.go(way, *after)
        self.end()

    def go_z(self, *after):
        here = self.here
        part = hold(self.part, *after)
        v, w = here.mine["v"], here.mine["w"]

        def at(dv, dw):
            one = lax.dynamic_index_in_dim(part, (v + dv) % 2, 0, keepdims=False)
            return lax.dynamic_index_in_dim(one, (w + dw) % 2, 0, keepdims=False)

        self.total = at(0, 0).astype(F32)
        self.got = [here.send(at(*d), way) for d, way in (((1, 0), "v"), ((1, 1), "u"), ((0, 1), "w"))]
        self.axes = self.axes[2:]

    def rows(self):
        if self.split:
            self.part = join_way(self.here, self.part, "x", 0)

    def other(self):
        return self.here.send(self.part, "c")


def meet(value, *sums):
    value, came = lax.optimization_barrier((value, [one.got for one in sums]))
    for one, got in zip(sums, came):
        one.got = got
        one.end()
    return value


def join_way(here, array, way, axis):
    number, mine = here.number[way], here.mine[way]
    got = [array] + [here.send(array, way, s) for s in range(1, number)]
    if number == 2:
        ahead = jnp.concatenate(got, axis=axis)
        behind = jnp.concatenate(got[::-1], axis=axis)
        return jnp.where(mine == 0, ahead, behind)
    stack = jnp.stack(got)
    order = (mine - jnp.arange(number)) % number
    stack = jnp.take(stack, order, axis=0)
    return jnp.concatenate([stack[i] for i in range(number)], axis=axis)


def gather_apart(here, shard):
    rows = shard.shape[0] // here.nr
    piece = lax.dynamic_slice_in_dim(shard, here.r * rows, rows, 0)
    return lax.all_gather(piece, ("fsdp", "rep"), axis=0, tiled=True)


def scatter_owners(array):
    return lax.psum_scatter(array, "fsdp", scatter_dimension=0, tiled=True)


def sum_x(here, array, *after):
    array = hold(array, *after)
    total = array.astype(F32)
    for s in range(1, here.nx):
        total = total + here.send(array, "x", s).astype(F32)
    return total.astype(BF)


def contract(left, right, left_dim, right_dim):
    return lax.dot_general(
        left, right, (((left_dim,), (right_dim,)), ((), ())), preferred_element_type=F32
    )


def rms_norm(values, gain):
    return values * lax.rsqrt(jnp.mean(values * values, axis=-1, keepdims=True) + EPSILON) * gain


def swiglu(pair):
    half = pair.shape[1] // 2
    return jax.nn.silu(pair[:, :half]) * pair[:, half:]


def kv_order(array):
    half = array.shape[1] // 6
    return [array[:, i * half : (i + 1) * half] for i in (2, 4, 3, 5)]


def from_behind(value, steps):
    count = lax.axis_size("fsdp")
    first, last = (max(0, -steps), min(count, count - steps))
    return lax.ppermute(value, "fsdp", [(source, source + steps) for source in range(first, last)])


def to_owners(parts, fanout):
    heads, d, width = parts.shape
    cut = parts.reshape(heads, d, fanout, width // fanout)
    return jnp.swapaxes(cut, 1, 2).reshape(heads * fanout, d, width // fanout)


def to_heads(parts, fanout):
    owners, d, width = parts.shape
    cut = parts.reshape(owners // fanout, fanout, d, width)
    return jnp.swapaxes(cut, 1, 2).reshape(owners // fanout, d, width * fanout)


def swap(value):
    return lax.all_to_all(value, "fsdp", 0, 0, tiled=True)


def by_core(here, for_zero, for_one):
    return jnp.where(here.mine["c"] == 0, for_zero, for_one)


def on_device(
    hidden_in,
    seg_ids,
    attn_gain,
    qkv_weight,
    beta_weight,
    gate_weight,
    conv_taps,
    out_gain,
    out_weight,
    ffn_gain,
    ffn_gate,
    ffn_up,
    ffn_down,
    cotangent,
):
    here = Place()
    row_count, width = hidden_in.shape
    heads = beta_weight.shape[1]
    head_dim = width // heads
    blocks = row_count // SPAN
    rim = 8
    lanes = 128
    hidden_units = ffn_gate.shape[1]

    numbers = seg_ids + 1

    small = [attn_gain, out_gain, ffn_gain, conv_taps]
    shard_rows = qkv_weight.shape[0]
    flat = jnp.concatenate([a.reshape(-1) for a in small])
    columns = -(-flat.size // shard_rows)
    flat = jnp.pad(flat, (0, columns * shard_rows - flat.size)).reshape(shard_rows, columns)
    extra = jnp.concatenate(
        [beta_weight, flat, jnp.zeros((shard_rows, lanes - heads - columns), BF)], axis=1
    )
    first = Gather(
        here,
        jnp.concatenate(kv_order(qkv_weight) + [extra], axis=1),
        [2 * width, lanes],
        True,
    )
    second = Gather(
        here,
        jnp.concatenate([qkv_weight[:, :width], gate_weight, out_weight], axis=1),
        [2 * width, width],
        False,
    )
    pair_full = gather_apart(here, jnp.concatenate([ffn_gate, ffn_up], axis=1))
    down_full = gather_apart(here, ffn_down)
    rim_rows = from_behind(hidden_in[row_count - rim :], 1)
    rim_ids = from_behind(numbers[row_count - rim :], 1)
    first.move("v", "w")
    first.move("vw")
    first.pile()
    if not first.plain:
        first.have["z"], rim_rows, rim_ids = lax.optimization_barrier((first.have["z"], rim_rows, rim_ids))
    first.move("zy", "zx")
    first.move("zc")
    second.move("v", "w", after=first.got("z"))
    first.move("zyx", after=first.got("zx", "zc"))
    first.move("zyc", "zxc")
    first.move("zyxc", after=first.got("zyc", "zxc"))
    kv_full, extra_full = first.place()

    small_full = extra_full[:, heads : heads + columns].reshape(here.nf, -1)
    cuts, at = [], 0
    for array in small:
        cuts.append(small_full[:, at : at + array.size].astype(F32))
        at += array.size
    attn_scale = cuts[0].reshape(-1)
    outgain_scale = cuts[1].reshape(1, -1)
    ffngain_scale = cuts[2].reshape(-1)
    taps_count = conv_taps.shape[0]
    taps_scale = jnp.swapaxes(cuts[3].reshape(here.nf, taps_count, -1), 0, 1).reshape(taps_count, -1)
    query_taps = taps_scale[:, :width]
    kv_taps = jnp.concatenate(kv_order(taps_scale), axis=1)
    residual = hidden_in.astype(F32)
    extended_in = jnp.concatenate([hidden_in, rim_rows]).astype(F32)
    normed_ext = rms_norm(extended_in, attn_scale).astype(BF)
    normed_low = normed_ext[:row_count]
    kv_pre = jnp.dot(normed_ext, kv_full, preferred_element_type=F32)
    second.move("vw", after=[kv_full])
    second.pile()
    second.move("zy", after=[kv_pre])
    beta_pre = jnp.dot(normed_low, extra_full, preferred_element_type=F32)[:, :heads]
    rates = jax.nn.sigmoid(beta_pre)
    ids = jnp.concatenate([rim_ids, numbers]).astype(F32)
    own_ids = numbers.astype(F32)
    before = ids[rim - 1 : rim - 1 + row_count : SPAN]
    cols = jnp.concatenate(
        [rates, own_ids[:, None]]
        + [(ids[rim - j : rim - j + row_count] == own_ids).astype(F32)[:, None] for j in (1, 2, 3)]
        + [jnp.zeros((row_count, heads - 4), F32)],
        1,
    )
    rows = jnp.concatenate(
        [
            jnp.swapaxes(rates.reshape(blocks, SPAN, heads), 1, 2),
            own_ids.reshape(blocks, 1, SPAN),
            jnp.broadcast_to(before[:, None, None], (blocks, 1, SPAN)),
            jnp.zeros((blocks, heads - 2, SPAN), F32),
        ],
        1,
    )
    key_low, value_low, w, u, a, moves = delta_summary(kv_pre, kv_taps, cols, rows, heads)
    second.move("zc", "zyc", after=[moves])
    fanout = here.nf // heads
    if fanout > 1:
        moves = jnp.concatenate(
            [
                to_owners(moves[:, :, :head_dim], fanout),
                jnp.repeat(moves[:, :, head_dim:], fanout, axis=0),
            ],
            axis=2,
        )
    owned = swap(moves)
    qg_full, outw_full = second.place()
    qg_pre = jnp.dot(normed_ext, qg_full, preferred_element_type=F32)
    entry = swap(scan_states(owned))
    if fanout > 1:
        entry = to_heads(entry, fanout)
    query_low, gated_low, attn_heads, fresh, kept = delta_forward(
        qg_pre, query_taps, key_low, w, u, cols, rows, entry, outgain_scale, heads
    )
    middle = residual + jnp.dot(gated_low, outw_full, preferred_element_type=F32)
    normed_two, norm_two_back = jax.vjp(partial(rms_norm, gain=ffngain_scale), middle)
    normed_two_low = normed_two.astype(BF)
    pair_pre = jnp.dot(normed_two_low, pair_full, preferred_element_type=F32)
    hidden_ff, swiglu_back = jax.vjp(swiglu, pair_pre)
    hidden_low = hidden_ff.astype(BF)

    c = here.mine["c"]

    def shares(array, start, size):
        half = size // 2
        cut = [lax.dynamic_slice_in_dim(array, start + at * half, half, 1) for at in (1 - c, c)]
        return cut

    theirs, ours = shares(cotangent, 0, width)
    down_sum = Reduce(here)
    down_sum.swap(contract(hidden_low, theirs, 0, 0))
    hidden_grad = contract(cotangent, down_full, 1, 1)
    (pair_grad,) = swiglu_back(hidden_grad)
    pair_low = pair_grad.astype(BF)
    down_half = (contract(hidden_low, hold(ours, pair_low), 0, 0) + down_sum.came.astype(F32)).astype(BF)
    down_apart = scatter_owners(down_half)
    top_grad = cotangent.astype(F32)
    normed_two_grad = contract(pair_low, pair_full, 1, 1)
    (middle_back,) = norm_two_back(normed_two_grad)
    middle_grad = top_grad + middle_back
    middle_low = middle_grad.astype(BF)
    gated_grad = contract(middle_low, outw_full, 1, 1)
    theirs, ours = shares(pair_low, 0, 2 * hidden_units)
    pair_sum = Reduce(here)
    pair_sum.swap(contract(normed_two_low, theirs, 0, 0))
    gated_grad = hold(gated_grad, down_half, pair_sum.away)
    heads_grad, gatepre_low, outgain_grad, local_later = delta_adjoint(
        query_low, key_low, w, cols, rows, gated_grad, attn_heads, qg_pre, outgain_scale, heads
    )
    if fanout > 1:
        local_later = to_owners(local_later, fanout)
    came_later = swap(local_later)

    ours = hold(ours, local_later)
    pair_half = (contract(normed_two_low, ours, 0, 0) + pair_sum.came.astype(F32)).astype(BF)
    pair_apart = scatter_owners(pair_half)
    came_later = hold(came_later, pair_half)
    summed_later = scan_grads(owned, came_later)
    later = swap(summed_later)
    if fanout > 1:
        later = to_heads(later, fanout)
    hidden_held, middle_held, gatepre_held = hold((hidden_low, middle_low, gatepre_low), summed_later)
    out_grad = contract(gated_low, middle_held, 0, 0)
    gate_grad = contract(normed_low, gatepre_held, 0, 0)
    other_sum = Reduce(here)
    other_sum.swap(by_core(here, gate_grad, out_grad))
    output = (middle + jnp.dot(hidden_held, down_full, preferred_element_type=F32)).astype(BF)
    other_sum.take(hold(by_core(here, out_grad, gate_grad), output))
    later = hold(later, other_sum.part)
    other_sum.go("x")
    state = (query_low, key_low, value_low, w, u, a, fresh, kept, heads_grad, cols, rows)
    mixed_a, beta_a, taps_a = delta_backward(
        0, *state, later, qg_pre, query_taps, kv_pre, kv_taps, heads
    )
    mixed_a = meet(mixed_a, other_sum)
    other_sum.go("y")
    a_sum = Reduce(here)
    size = 3 * width // 2
    theirs, ours = shares(mixed_a, 0, size)
    a_sum.swap(contract(normed_ext, theirs, 0, 0))
    a_sum.take(contract(normed_ext, ours, 0, 0))
    later = hold(later, a_sum.part)
    a_sum.go("x")
    mixed_b, beta_b, taps_b = delta_backward(
        1, *state, later, qg_pre, query_taps, kv_pre, kv_taps, heads
    )
    mixed_b = hold(meet(mixed_b, other_sum, a_sum), pair_apart)
    a_sum.go("y")
    other_sum.go("w")
    eighth = width // 2

    def by_kind(first_heads, other_heads):
        cut = [slice(i * eighth, (i + 1) * eighth) for i in range(3)]
        both = [array[:, s] for s in cut for array in (first_heads, other_heads)]
        return jnp.concatenate(both, axis=1)

    betapre_low = (beta_a + beta_b).astype(BF)
    taps_grad = by_kind(taps_a, taps_b)
    parts = (
        outgain_grad.reshape(here.nf, -1),
        jnp.swapaxes(taps_grad.reshape(taps_count, here.nf, -1), 0, 1).reshape(here.nf, -1),
    )
    flat = jnp.concatenate(parts, axis=1)
    flat = jnp.pad(flat, ((0, 0), (0, columns * shard_rows - flat.shape[1])))
    extra = jnp.pad(flat.reshape(width, columns), ((0, 0), (heads, lanes - heads - columns)))
    small_sum = Reduce(here)
    small_sum.begin(contract(normed_low, hold(betapre_low, mixed_b), 0, 0) + extra)
    small_sum.both()
    b_sum = Reduce(here)
    theirs, ours = shares(mixed_b, 0, size)
    b_sum.swap(contract(normed_ext, theirs, 0, 0))
    b_sum.take(contract(normed_ext, ours, 0, 0))
    small_sum.end()
    mixed_b = hold(mixed_b, b_sum.part, small_sum.part)
    b_sum.go("x")
    small_sum.go("x")
    wide_grad = (
        contract(mixed_a[:, eighth:], kv_full[:, :width], 1, 1)
        + contract(mixed_b[:, eighth:], kv_full[:, width:], 1, 1)
        + contract(mixed_a[:, :eighth], qg_full[:, :eighth], 1, 1)
        + contract(mixed_b[:, :eighth], qg_full[:, eighth:width], 1, 1)
    )
    rim_grad = from_behind(wide_grad[row_count:].astype(BF), -1).astype(F32)
    normed_grad = (
        wide_grad[:row_count]
        + jnp.pad(rim_grad, ((row_count - rim, 0), (0, 0)))
        + contract(betapre_low, extra_full, 1, 1)
        + contract(gatepre_low, qg_full[:, width:], 1, 1)
    )
    normed_grad = meet(normed_grad, b_sum, a_sum, other_sum, small_sum)
    b_sum.go("y")
    small_sum.go("y")
    a_sum.go("w")
    other_sum.go("v")
    (input_back,) = jax.vjp(partial(rms_norm, gain=attn_scale), residual)[1](normed_grad)
    input_grad = meet((middle_grad + input_back).astype(BF), b_sum, a_sum, other_sum, small_sum)
    b_sum.go("w", input_grad)
    a_sum.go("v", input_grad)
    small_sum.go("w", input_grad)
    pair_sum.begin_x(pair_apart, input_grad)
    for one in (b_sum, a_sum, small_sum):
        one.end()
    b_sum.go("v", a_sum.part)
    small_sum.go("v", a_sum.part)
    held = meet(a_sum.part, b_sum, small_sum, pair_sum)
    down_sum.begin_x(down_apart, held)
    down_sum.end()
    both = Reduce(here)
    both.part = jnp.concatenate([b_sum.part, held, other_sum.part, small_sum.part], axis=1)
    both.split = True
    both.rows()
    down_total = join_way(here, down_sum.part, "c", 1).astype(F32)
    other = here.send(pair_sum.part, "c")
    hidgate_total = by_core(here, pair_sum.part, other).astype(F32)
    hidup_total = by_core(here, other, pair_sum.part).astype(F32)
    whole = both.other()
    piece = size // 2
    ends = [piece, 2 * piece, 2 * piece + width]

    def joined(start, end):
        mine, theirs = both.part[:, start:end], whole[:, start:end]
        return by_core(here, mine, theirs), by_core(here, theirs, mine)

    outproj_total, gate_total = [part.astype(F32) for part in joined(ends[1], ends[2])]
    b_first, b_second = joined(0, ends[0])
    a_first, a_second = joined(ends[0], ends[1])
    qkv_total = by_kind(
        jnp.concatenate([a_first, a_second], axis=1), jnp.concatenate([b_first, b_second], axis=1)
    ).astype(F32)
    extra = both.part[:, ends[2] :].astype(F32)
    beta_total = extra[:, :heads]

    def gain_grad(gain, pairs):
        total = sum(jnp.sum(weight.astype(F32) * grad, axis=1) for weight, grad in pairs)
        return total / gain.astype(F32)

    attngain_total = gain_grad(
        attn_gain, ((qkv_weight, qkv_total), (beta_weight, beta_total), (gate_weight, gate_total))
    )
    ffngain_total = gain_grad(ffn_gain, ((ffn_gate, hidgate_total), (ffn_up, hidup_total)))
    flat = extra[:, heads : heads + columns].reshape(-1)
    cut, at = [], 0
    for part in parts:
        cut.append(flat[at : at + part.shape[1]])
        at += part.shape[1]
    return (
        output,
        input_grad,
        attngain_total,
        qkv_total,
        beta_total,
        gate_total,
        cut[1].reshape(conv_taps.shape),
        cut[0],
        outproj_total,
        ffngain_total,
        hidgate_total,
        hidup_total,
        down_total,
    )


def solution(mesh):
    placed = (
        P(("rep", "fsdp"), None),
        P(("rep", "fsdp")),
        P("fsdp"),
        P("fsdp", None),
        P("fsdp", None),
        P("fsdp", None),
        P(None, "fsdp"),
        P("fsdp"),
        P("fsdp", None),
        P("fsdp"),
        P("fsdp", None),
        P("fsdp", None),
        P("fsdp", None),
        P(("rep", "fsdp"), None),
    )
    return jax.shard_map(
        on_device,
        mesh=mesh,
        in_specs=placed,
        out_specs=(
            P(("rep", "fsdp"), None),
            P(("rep", "fsdp"), None),
            P("fsdp"),
            P("fsdp", None),
            P("fsdp", None),
            P("fsdp", None),
            P(None, "fsdp"),
            P("fsdp"),
            P("fsdp", None),
            P("fsdp"),
            P("fsdp", None),
            P("fsdp", None),
            P("fsdp", None),
        ),
        check_vma=False,
    )
```

```python
from functools import partial

import jax
import jax.numpy as jnp
from jax import lax
from jax.experimental import pallas as pl
from jax.experimental.pallas import tpu as pltpu
from jax.sharding import PartitionSpec as P

SPAN = 64
TOGETHER = 8
EPSILON = 1e-06
BF = jnp.bfloat16
F32 = jnp.float32


def nn(a, b):
    return lax.dot_general(a, b, (((1,), (0,)), ((), ())), preferred_element_type=F32)


def nt(a, b):
    return lax.dot_general(a, b, (((1,), (1,)), ((), ())), preferred_element_type=F32)


def tn(a, b):
    return lax.dot_general(a, b, (((0,), (0,)), ((), ())), preferred_element_type=F32)


def in_turn(body, count, together):
    for start in range(0, count, together):
        running = [body(h) for h in range(start, min(start + together, count))]
        while running:
            running = [one for one in running if next(one, False)]


def block_masks(cols_ref, rows_ref, heads):
    n = SPAN
    row = lax.broadcasted_iota(jnp.int32, (n, n), 0)
    col = lax.broadcasted_iota(jnp.int32, (n, n), 1)
    ids = cols_ref[:, heads : heads + 1]
    ids_row = rows_ref[0, heads : heads + 1, :]
    before = rows_ref[0, heads + 1 : heads + 2, :]
    end = ids_row[:, n - 1 : n]
    same = ids == ids_row
    first = (ids == before[:, :1]).astype(F32)
    last = (ids == end).astype(F32)
    keep = (end == before[:, :1]).astype(F32)
    return row, col, same, first, last, keep


def sigmoid(z):
    return 0.5 * jnp.tanh(0.5 * z) + 0.5


def shifted_rows(x, prev, masks):
    both = jnp.concatenate([prev, x], axis=0)
    lead = prev.shape[0]
    return [x] + [pltpu.roll(both, j, 0)[lead:] * masks[j - 1] for j in (1, 2, 3)]


def mix_rows(rows, taps):
    mixed = rows[0] * taps[0:1]
    for j in (1, 2, 3):
        mixed = mixed + rows[j] * taps[j : j + 1]
    return mixed


def lag_masks(cols_ref, heads):
    return [cols_ref[:, heads + j : heads + j + 1] for j in (1, 2, 3)]


def head_parts(heads):
    return heads - heads // 4, heads // 4


def kv_at(heads, d, h):
    first, other = head_parts(heads)
    number, start, inside = (first, 0, h) if h < first else (other, 2 * first, h - first)
    at = (start + inside) * d
    return slice(at, at + d), slice(at + number * d, at + number * d + d)


def summary_kernel(
    heads, d, pre_ref, prev_ref, taps_ref, cols_ref, rows_ref,
    k_ref, v_ref, z_ref, w_ref, u_ref, a_ref, x_ref, state, levels,
):
    n = SPAN
    block = pl.program_id(0)

    @pl.when(block == 0)
    def _():
        at = lax.broadcasted_iota(jnp.int32, (n, n), 0)
        to = lax.broadcasted_iota(jnp.int32, (n, n), 1)
        for i in range(levels.shape[0]):
            size = 1 << i
            level = jnp.logical_and(
                (at // (2 * size)) == (to // (2 * size)),
                jnp.logical_and(((at // size) & 1) == 1, ((to // size) & 1) == 0),
            )
            levels[i] = level.astype(F32).astype(BF)
        r = lax.broadcasted_iota(jnp.int32, (d, 2 * d), 0)
        c = lax.broadcasted_iota(jnp.int32, (d, 2 * d), 1)
        unit = (r + d == c).astype(F32)
        for h in range(heads):
            state[h] = unit

    row, col, same, first, last, keep = block_masks(cols_ref, rows_ref, heads)
    lower = jnp.logical_and(same, row > col)
    unit = (row == col).astype(F32).astype(BF)
    masks = lag_masks(cols_ref, heads)
    keys, mixing, inverse = ([None] * heads for i in range(3))
    def features(h):
        cut = slice(h * d, (h + 1) * d)
        at_k, at_v = kv_at(heads, d, h)
        z = mix_rows(shifted_rows(pre_ref[:, at_k], prev_ref[:, at_k], masks), taps_ref[:, at_k])
        z_ref[:, at_k] = z
        yield True
        act = z * sigmoid(z)
        root = lax.rsqrt(jnp.sum(act * act, axis=1, keepdims=True) + EPSILON)
        yield True
        keys[h] = (act * root).astype(BF)
        k_ref[:, cut] = keys[h]
        yield True
        z = mix_rows(shifted_rows(pre_ref[:, at_v], prev_ref[:, at_v], masks), taps_ref[:, at_v])
        z_ref[:, at_v] = z
        v_ref[:, cut] = (z * sigmoid(z)).astype(BF)
        m = jnp.where(lower, nt(keys[h], keys[h]) * cols_ref[:, h : h + 1], 0.0).astype(BF)
        yield True
        mixing[h] = m
        inverse[h] = unit - m * levels[0]

    in_turn(features, heads, TOGETHER)
    for i in range(1, levels.shape[0]):
        level = levels[i]
        inner = [nn(mixing[h] * level, inverse[h]).astype(BF) for h in range(heads)]
        for h in range(heads):
            inverse[h] = inverse[h] - nn(inverse[h], inner[h]).astype(BF) * level
    def advance(h):
        cut = slice(h * d, (h + 1) * d)
        a_ref[h] = inverse[h]
        scaled = (inverse[h].astype(F32) * rows_ref[0, h : h + 1, :]).astype(BF)
        yield True
        both = nn(scaled, jnp.concatenate([keys[h], v_ref[:, cut]], axis=1))
        yield True
        w = both[:, :d].astype(BF)
        u = both[:, d:].astype(BF)
        w_ref[:, cut] = w
        u_ref[:, cut] = u
        yield True
        held = state[h]
        moved = nn(w, held.astype(BF)) * first
        yield True
        fresh = (jnp.concatenate([u.astype(F32), jnp.zeros((n, d), F32)], axis=1) - moved).astype(BF)
        yield True
        key_last = keys[h] * last.astype(BF)
        yield True
        state[h] = keep * held + tn(key_last, fresh)

    in_turn(advance, heads, TOGETHER)

    @pl.when(block == pl.num_programs(0) - 1)
    def _():
        x_ref[...] = state[...].astype(BF)


def forward_kernel(
    heads, d, pre_ref, prev_ref, taps_ref, k_ref, w_ref, u_ref, cols_ref, rows_ref, s_ref, gate_ref, gain_ref,
    q_ref, z_ref, y_ref, o_ref, e_ref, kept_ref, state,
):
    n = SPAN
    block = pl.program_id(0)

    @pl.when(block == 0)
    def _():
        state[...] = s_ref[...].astype(F32)

    row, col, same, first, last, keep = block_masks(cols_ref, rows_ref, heads)
    visible = jnp.logical_and(same, row >= col)
    masks = lag_masks(cols_ref, heads)
    def one_head(h):
        cut = slice(h * d, (h + 1) * d)
        z = mix_rows(shifted_rows(pre_ref[:, cut], prev_ref[:, cut], masks), taps_ref[:, cut])
        z_ref[:, cut] = z
        q = (z * sigmoid(z) * d ** (-0.5)).astype(BF)
        q_ref[:, cut] = q
        yield True
        k, w = k_ref[:, cut], w_ref[:, cut]
        held = state[h]
        held_low = held.astype(BF)
        kept_ref[0, h] = held_low
        both = nn(jnp.concatenate([w, q], axis=0), held_low)
        yield True
        fresh = (u_ref[:, cut].astype(F32) - first * both[:n]).astype(BF)
        e_ref[:, cut] = fresh
        yield True
        scores = jnp.where(visible, nt(q, k), 0.0).astype(BF)
        yield True
        out = first * both[n:] + nn(scores, fresh)
        yield True
        key_last = k * last.astype(BF)
        state[h] = keep * held + tn(key_last, fresh)
        yield True
        o_ref[:, cut] = out
        yield True
        g = gate_ref[:, cut]
        root = lax.rsqrt(jnp.mean(out * out, axis=1, keepdims=True) + EPSILON)
        yield True
        y_ref[:, cut] = (out * root * gain_ref[...] * (g * sigmoid(g))).astype(BF)

    in_turn(one_head, heads, TOGETHER)


def adjoint_kernel(
    heads, d, q_ref, k_ref, w_ref, cols_ref, rows_ref, dy_ref, o_ref, gate_ref, gain_ref,
    do_ref, dgate_ref, dgain_ref, ds_ref, state,
):
    n = SPAN
    step = pl.program_id(0)

    @pl.when(step == 0)
    def _():
        state[...] = jnp.zeros_like(state)
        dgain_ref[...] = jnp.zeros_like(dgain_ref)

    row, col, same, first, last, keep = block_masks(cols_ref, rows_ref, heads)
    visible = jnp.logical_and(same, row >= col)
    first_low = first.astype(BF)
    gain = gain_ref[...]
    gain_sum = jnp.zeros((1, d), F32)
    def one_head(h):
        nonlocal gain_sum
        cut = slice(h * d, (h + 1) * d)
        q, k, w = q_ref[:, cut], k_ref[:, cut], w_ref[:, cut]
        o, g, dy = o_ref[:, cut], gate_ref[:, cut], dy_ref[:, cut]
        root = lax.rsqrt(jnp.mean(o * o, axis=1, keepdims=True) + EPSILON)
        yield True
        unit = o * root
        sig = sigmoid(g)
        m = g * sig
        t = dy * m
        gain_sum = gain_sum + jnp.sum(t * unit, axis=0, keepdims=True)
        tg = t * gain
        do = root * (tg - unit * jnp.mean(tg * unit, axis=1, keepdims=True))
        yield True
        dgate_ref[:, cut] = (dy * gain * unit * (sig * (1.0 + g * (1.0 - sig)))).astype(BF)
        do_low = do.astype(BF)
        do_ref[:, cut] = do_low
        yield True
        scores = jnp.where(visible, nt(q, k), 0.0).astype(BF)
        yield True
        later = state[h]
        de = last * nn(k, later.astype(BF)) + tn(scores, do_low)
        yield True
        left = jnp.concatenate([q * first_low, w * -first_low], axis=0)
        right = jnp.concatenate([do_low, de.astype(BF)], axis=0)
        state[h] = keep * later + tn(left, right)
        yield True

    in_turn(one_head, heads, TOGETHER)
    dgain_ref[...] += gain_sum

    @pl.when(step == pl.num_programs(0) - 1)
    def _():
        ds_ref[...] = state[...].astype(BF)


def backward_kernel(
    heads, part, d, q_ref, k_ref, v_ref, w_ref, u_ref, a_ref, e_ref, kept_ref, do_ref, cols_ref, rows_ref, s_ref,
    qz_ref, qpre_ref, qrim_ref, qtaps_ref, kvz_ref, kvpre_ref, kvrim_ref, kvtaps_ref,
    dpre_ref, dbeta_ref, dtaps_ref, state, carry,
):
    n = SPAN
    step = pl.program_id(0)
    number = head_parts(heads)[part]
    base = heads - number if part else 0

    @pl.when(step == 0)
    def _():
        state[...] = s_ref[...].astype(F32)
        carry[...] = jnp.zeros_like(carry)
        dtaps_ref[...] = jnp.zeros_like(dtaps_ref)

    @pl.when(step < pl.num_programs(0) - 1)
    def _():
        row, col, same, first, last, keep = block_masks(cols_ref, rows_ref, heads)
        visible = jnp.logical_and(same, row >= col)
        lower = jnp.logical_and(same, row > col)
        lane = lax.broadcasted_iota(jnp.int32, (n, d), 1)
        masks = lag_masks(cols_ref, heads)
        rate_grads = jnp.zeros((n, d), F32)

        first_low = first.astype(BF)

        def conv_back(dact, z, sig, pre, taps, at):
            dconv = dact * (sig * (1.0 + z * (1.0 - sig)))
            here = slice(at, at + d)
            dpre = dconv * taps[0:1]
            sums = [jnp.sum(dconv * pre, axis=0, keepdims=True)]
            for j in (1, 2, 3):
                masked = dconv * masks[j - 1]
                both = jnp.concatenate([masked, carry[j - 1, :, here]], axis=0)
                moved = pltpu.roll(both, both.shape[0] - j, 0)[:n]
                dpre = dpre + moved * taps[j : j + 1]
                sums.append(jnp.sum(moved * pre, axis=0, keepdims=True))
                carry[j - 1, :, here] = masked[:8]
            dtaps_ref[:, here] += jnp.concatenate(sums, axis=0)
            dpre_ref[:, here] = dpre.astype(BF)

        def one_head(h):
            nonlocal rate_grads
            cut = slice(h * d, (h + 1) * d)
            cut_v = slice((number + h) * d, (number + h + 1) * d)
            q, k, v, w, u = q_ref[:, cut], k_ref[:, cut], v_ref[:, cut], w_ref[:, cut], u_ref[:, cut]
            do, e, held = do_ref[:, cut], e_ref[:, cut], kept_ref[0, h]
            at = base + h
            rate = cols_ref[:, at : at + 1]
            later = state[h]
            later_low = later.astype(BF)
            scores = jnp.where(visible, nt(q, k), 0.0).astype(BF)
            yield True
            de = last * nn(k, later_low) + tn(scores, do)
            yield True
            de_low = de.astype(BF)
            dscores = jnp.where(visible, nt(do, e), 0.0).astype(BF)
            yield True
            both = nt(jnp.concatenate([do, de_low], axis=0), held)
            yield True
            dq = first * both[:n] + nn(dscores, k)
            dw = -first * both[n:]
            dk = tn(dscores, q) + last * nt(e, later_low)
            yield True
            pg = tn(a_ref[h], jnp.concatenate([dw.astype(BF), de_low], axis=1))
            yield True
            p, g = pg[:, :d], pg[:, d:]
            dmix = jnp.where(lower, -nt(pg.astype(BF), jnp.concatenate([w, u], axis=1)), 0.0).astype(BF)
            yield True
            kf = k.astype(F32)
            drk = p + nn(dmix, k)
            dk = dk + tn(dmix, (kf * rate).astype(BF)) + rate * drk
            yield True
            dr = jnp.sum(drk * kf + g * v.astype(F32), axis=1, keepdims=True)
            rate_grads = jnp.where(lane == at, dr * rate * (1.0 - rate), rate_grads)
            left = jnp.concatenate([q * first_low, w * -first_low], axis=0)
            right = jnp.concatenate([do, de_low], axis=0)
            state[h] = keep * later + tn(left, right)
            yield True

            z = qz_ref[:, cut]
            conv_back(dq * d ** (-0.5), z, sigmoid(z), qpre_ref[:, cut], qtaps_ref[:, cut], h * d)
            yield True
            z = kvz_ref[:, cut]
            sig = sigmoid(z)
            act = z * sig
            root = lax.rsqrt(jnp.sum(act * act, axis=1, keepdims=True) + EPSILON)
            unit = act * root
            dact = root * (dk - unit * jnp.sum(unit * dk, axis=1, keepdims=True))
            conv_back(dact, z, sig, kvpre_ref[:, cut], kvtaps_ref[:, cut], (number + h) * d)
            yield True
            z = kvz_ref[:, cut_v]
            conv_back(
                rate * g, z, sigmoid(z), kvpre_ref[:, cut_v], kvtaps_ref[:, cut_v], (2 * number + h) * d
            )

        in_turn(one_head, number, TOGETHER)
        dbeta_ref[...] = rate_grads

    @pl.when(step == pl.num_programs(0) - 1)
    def _():
        wide = number * d
        for i, taps_ref, rim_ref, at in (
            (0, qtaps_ref, qrim_ref, 0),
            (1, kvtaps_ref, kvrim_ref, 0),
            (2, kvtaps_ref, kvrim_ref, wide),
        ):
            here, there = slice(i * wide, (i + 1) * wide), slice(at, at + wide)
            dpre = jnp.zeros((8, wide), F32)
            sums = [jnp.zeros((1, wide), F32)]
            for j in (1, 2, 3):
                held = carry[j - 1, :, here]
                moved = jnp.concatenate([jnp.zeros_like(held), held], axis=0)[j : 8 + j]
                dpre = dpre + moved * taps_ref[j : j + 1, there]
                sums.append(jnp.sum(moved * rim_ref[:, there], axis=0, keepdims=True))
            dtaps_ref[:, here] += jnp.concatenate(sums, axis=0)
            dpre_ref[0:8, here] = dpre.astype(BF)


def prefix_kernel(peers, x_ref, out_ref):
    cols = out_ref.shape[2]
    held = jnp.zeros(out_ref.shape[1:], F32)
    for i in range(peers):
        out_ref[i] = held.astype(BF)
        held = nn(x_ref[i, :, cols:], held.astype(BF)) + x_ref[i, :, :cols].astype(F32)


def suffix_kernel(peers, t_ref, g_ref, out_ref):
    held = jnp.zeros(out_ref.shape[1:], F32)
    cols = out_ref.shape[2]
    for i in reversed(range(peers)):
        out_ref[i] = held.astype(BF)
        held = tn(t_ref[i, :, cols:], held.astype(BF)) + g_ref[i].astype(F32)


VMEM_LIMIT = 16 * 1024 * 1024


def in_hbm(*arrays):
    return [pltpu.with_memory_space_constraint(a, pltpu.HBM) for a in arrays]


def params():
    return pltpu.CompilerParams(dimension_semantics=("arbitrary",), vmem_limit_bytes=VMEM_LIMIT)


def cost(microseconds):
    return pl.CostEstimate(
        flops=int(microseconds * 1e9), bytes_accessed=int(microseconds * 3e6), transcendentals=0
    )


def specs(blocks, heads, d, flip):
    at = (lambda b: blocks - 1 - b) if flip else (lambda b: b)
    wide = pl.BlockSpec((SPAN, heads * d), lambda b: (at(b), 0))
    cols = pl.BlockSpec((SPAN, 2 * heads), lambda b: (at(b), 0))
    rows = pl.BlockSpec((1, 2 * heads, SPAN), lambda b: (at(b), 0, 0))
    state = pl.BlockSpec((heads, d, d), lambda b: (0, 0, 0))
    mix = pl.BlockSpec((heads, SPAN, SPAN), lambda b: (0, at(b), 0))
    kept = pl.BlockSpec((1, heads, d, d), lambda b: (at(b), 0, 0, 0))
    gain = pl.BlockSpec((1, d), lambda b: (0, 0))
    return wide, cols, rows, state, mix, kept, gain


def shape(dims, kind):
    return pltpu.HBM(dims, kind)


def near(dims, kind):
    return jax.ShapeDtypeStruct(dims, kind)


def before_block(blocks, rim, size, column):
    def index(b):
        per = SPAN // rim
        return jnp.where(b == 0, blocks * per, b * per - 1), column

    return pl.BlockSpec((rim, size), index)


def delta_summary(pre, taps, cols, rows, heads):
    count, width = cols.shape[0], pre.shape[1] // 2
    d, blocks = width // heads, count // SPAN
    rim = pre.shape[0] - count
    wide, c, r, state, mix, kept, gain = specs(blocks, heads, d, False)
    return pl.pallas_call(
        partial(summary_kernel, heads, d),
        grid=(blocks,),
        in_specs=[
            pl.BlockSpec((SPAN, 2 * width), lambda b: (b, 0)),
            before_block(blocks, rim, 2 * width, 0),
            pl.BlockSpec((4, 2 * width), lambda b: (0, 0)),
            c,
            r,
        ],
        out_specs=[
            wide,
            wide,
            pl.BlockSpec((SPAN, 2 * width), lambda b: (b, 0)),
            wide,
            wide,
            mix,
            pl.BlockSpec((heads, d, 2 * d), lambda b: (0, 0, 0)),
        ],
        out_shape=[
            shape((count, width), BF),
            shape((count, width), BF),
            shape((count, 2 * width), F32),
            shape((count, width), BF),
            shape((count, width), BF),
            shape((heads, count, SPAN), BF),
            shape((heads, d, 2 * d), BF),
        ],
        scratch_shapes=[
            pltpu.VMEM((heads, d, 2 * d), F32),
            pltpu.VMEM((SPAN.bit_length() - 1, SPAN, SPAN), BF),
        ],
        compiler_params=params(),
        cost_estimate=cost(21),
        name="delta_summary",
    )(*in_hbm(pre, pre, taps, cols, rows))


def delta_forward(pre, taps, k, w, u, cols, rows, entry, gain_full, heads):
    count, width = k.shape
    d, blocks = width // heads, count // SPAN
    rim = pre.shape[0] - count
    wide, c, r, state, mix, kept, gain = specs(blocks, heads, d, False)
    return pl.pallas_call(
        partial(forward_kernel, heads, d),
        grid=(blocks,),
        in_specs=[
            wide,
            before_block(blocks, rim, width, 0),
            pl.BlockSpec((4, width), lambda b: (0, 0)),
            wide,
            wide,
            wide,
            c,
            r,
            state,
            pl.BlockSpec((SPAN, width), lambda b: (b, 1)),
            gain,
        ],
        out_specs=[wide, wide, wide, wide, wide, kept],
        out_shape=[
            shape((count, width), BF),
            shape((count, width), F32),
            shape((count, width), BF),
            shape((count, width), F32),
            shape((count, width), BF),
            shape((blocks, heads, d, d), BF),
        ],
        scratch_shapes=[pltpu.VMEM((heads, d, d), F32)],
        compiler_params=params(),
        cost_estimate=cost(11),
        name="delta_forward",
    )(*in_hbm(pre, pre, taps, k, w, u, cols, rows, entry, pre, gain_full))


def delta_adjoint(q, k, w, cols, rows, dy, o, gate, gain_full, heads):
    count, width = k.shape
    d, blocks = width // heads, count // SPAN
    wide, c, r, state, mix, kept, gain = specs(blocks, heads, d, True)
    return pl.pallas_call(
        partial(adjoint_kernel, heads, d),
        grid=(blocks,),
        in_specs=[
            wide,
            wide,
            wide,
            c,
            r,
            wide,
            wide,
            pl.BlockSpec((SPAN, width), lambda b: (blocks - 1 - b, 1)),
            gain,
        ],
        out_specs=[wide, wide, gain, state],
        out_shape=[
            shape((count, width), BF),
            shape((count, width), BF),
            shape((1, d), F32),
            shape((heads, d, d), BF),
        ],
        scratch_shapes=[pltpu.VMEM((heads, d, d), F32)],
        compiler_params=params(),
        cost_estimate=cost(11),
        name="delta_adjoint",
    )(*in_hbm(q, k, w, cols, rows, dy, o, gate, gain_full))


def delta_backward(part, q, k, v, w, u, a, e, kept_states, do, cols, rows, later, qz, qg_pre, qtaps, kvz, kv_pre, kvtaps, heads):
    count, width = k.shape
    d, blocks = width // heads, count // SPAN
    rim = kv_pre.shape[0] - count
    number = head_parts(heads)[part]
    part_at = (heads - number) // number if part else 0
    size = number * d

    def at(step):
        return blocks - 1 - jnp.minimum(step, blocks - 1)

    wide = pl.BlockSpec((SPAN, size), lambda b: (at(b), part_at))
    in_specs = [
        wide,
        wide,
        wide,
        wide,
        wide,
        pl.BlockSpec((number, SPAN, SPAN), lambda b: (part_at, at(b), 0)),
        wide,
        pl.BlockSpec((1, number, d, d), lambda b: (at(b), part_at, 0, 0)),
        wide,
        pl.BlockSpec((SPAN, 2 * heads), lambda b: (at(b), 0)),
        pl.BlockSpec((1, 2 * heads, SPAN), lambda b: (at(b), 0, 0)),
        pl.BlockSpec((number, d, d), lambda b: (part_at, 0, 0)),
        wide,
        wide,
        pl.BlockSpec((rim, size), lambda b: (count // rim, part_at)),
        pl.BlockSpec((4, size), lambda b: (0, part_at)),
        pl.BlockSpec((SPAN, 2 * size), lambda b: (at(b), part_at)),
        pl.BlockSpec((SPAN, 2 * size), lambda b: (at(b), part_at)),
        pl.BlockSpec((rim, 2 * size), lambda b: (count // rim, part_at)),
        pl.BlockSpec((4, 2 * size), lambda b: (0, part_at)),
    ]
    return pl.pallas_call(
        partial(backward_kernel, heads, part, d),
        grid=(blocks + 1,),
        in_specs=in_specs,
        out_specs=[
            pl.BlockSpec((SPAN, 3 * size), lambda b: (jnp.where(b < blocks, blocks - 1 - b, blocks), 0)),
            pl.BlockSpec((SPAN, d), lambda b: (at(b), 0)),
            pl.BlockSpec((4, 3 * size), lambda b: (0, 0)),
        ],
        out_shape=[
            shape((count + rim, 3 * size), BF),
            shape((count, d), F32),
            shape((4, 3 * size), F32),
        ],
        scratch_shapes=[pltpu.VMEM((number, d, d), F32), pltpu.VMEM((3, rim, 3 * size), F32)],
        compiler_params=params(),
        cost_estimate=cost(8 + 2 * number),
        name="delta_backward",
    )(*in_hbm(q, k, v, w, u, a, e, kept_states, do, cols, rows, later, qz, qg_pre, qg_pre, qtaps, kvz, kv_pre, kv_pre, kvtaps))


def scan_states(x):
    peers, d, width = x.shape
    return pl.pallas_call(
        partial(prefix_kernel, peers),
        out_shape=shape((peers, d, width - d), BF),
        cost_estimate=cost(3),
        name="state_prefix",
    )(x)


def scan_grads(x, g):
    peers, d, width = g.shape
    return pl.pallas_call(
        partial(suffix_kernel, peers),
        out_shape=shape((peers, d, width), BF),
        cost_estimate=cost(3),
        name="state_suffix",
    )(x, g)


def hold(value, *after):
    return lax.optimization_barrier((value, after))[0]


class Place:
    def __init__(self):
        self.nf, self.nr = lax.axis_size("fsdp"), lax.axis_size("rep")
        self.ny = self.nf // 4
        self.nx = self.nr // 2
        self.f, self.r = lax.axis_index("fsdp"), lax.axis_index("rep")
        z = self.f // self.ny
        self.mine = {"v": z // 2, "w": z % 2, "y": self.f % self.ny, "x": self.r // 2, "c": self.r % 2}
        self.number = {"v": 2, "w": 2, "u": 2, "y": self.ny, "x": self.nx, "c": 2}
        self.stride = {"v": 2 * self.ny, "w": self.ny, "y": 1, "x": 2, "c": 1}

    def send(self, value, way, steps=1):
        if way == "u":
            return lax.ppermute(value, "fsdp", [(i, i ^ 3 * self.ny) for i in range(self.nf)])
        axis = "rep" if way in "xc" else "fsdp"
        total = self.nr if way in "xc" else self.nf
        number, stride = self.number[way], self.stride[way]
        pairs = []
        for i in range(total):
            at = i // stride % number
            pairs.append((i, i + ((at + steps) % number - at) * stride))
        return lax.ppermute(value, axis, pairs)


def place_kernel(count, rows, each, by_rows, widths, offs_ref, own_ref, *refs):
    stacks, outs, sems = refs[: len(count)], refs[len(count) : -1], refs[-1]
    copies = []

    def put(src, row, height, column, out):
        copy = pltpu.make_async_copy(src, out.at[pl.ds(row, height), column], sems.at[len(copies)])
        copy.start()
        copies.append(copy)

    starts = [sum(widths[:i]) for i in range(len(widths))]
    top = pl.multiple_of(offs_ref[0], rows)
    for start, width, out in zip(starts, widths, outs):
        put(own_ref.at[:, pl.ds(start, width)], top, rows, pl.ds(0, width), out)
    at = 1
    for stack, number in zip(stacks, count):
        for j in range(number):
            row = pl.multiple_of(offs_ref[at], each if by_rows else rows)
            if by_rows:
                for start, width, out in zip(starts, widths, outs):
                    put(stack.at[j, :, pl.ds(start, width)], row, each, pl.ds(0, width), out)
                at += 1
            else:
                column = pl.multiple_of(offs_ref[at + 1], each)
                put(stack.at[j], row, rows, pl.ds(column, each), outs[0])
                at += 2
    for copy in copies:
        copy.wait()


class Gather:
    def __init__(self, here, shard, widths, deep, by_rows=True):
        self.here, self.shard, self.widths, self.deep, self.by_rows = here, shard, widths, deep, by_rows
        rows, total = shard.shape
        parts = here.nr if deep else 2
        extent = rows if by_rows else total
        self.each = extent // parts
        self.plain = bool(extent % parts or self.each % (32 if by_rows else 128) or rows % 32)
        self.plain = self.plain or here.ny != 2 or here.nx != 2
        self.have = {}
        if self.plain:
            return
        part = here.r if deep else here.mine["c"]
        self.have[""] = lax.dynamic_slice_in_dim(shard, part * self.each, self.each, 0 if by_rows else 1)

    def got(self, *names):
        return [] if self.plain else [self.have[name] for name in names]

    def move(self, *names, after=()):
        if not self.plain:
            for name in names:
                self.have[name] = self.here.send(hold(self.have[name[:-1]], *after), name[-1])

    def pile(self):
        if not self.plain:
            last = "u" if "u" in self.have else "vw"
            self.have["z"] = jnp.stack([self.have[name] for name in ("", "w", "v", last)])

    def place(self):
        here, shard, widths = self.here, self.shard, self.widths
        rows, each = shard.shape[0], self.each
        if self.plain:
            whole = lax.all_gather(shard, "fsdp", axis=0, tiled=True)
            starts = [sum(widths[:i]) for i in range(len(widths))]
            return [whole[:, s : s + w] for s, w in zip(starts, widths)]
        mine = here.mine
        offsets = [here.f * rows]
        names = [name for name in self.have if name.startswith("z")]
        for name in names:
            x, c, y = ((mine[way] + (way in name)) % 2 for way in "xcy")
            inside = (x * 2 + c if self.deep else c) * each
            for j in range(4):
                v = (mine["v"] + j // 2) % 2
                w = (mine["w"] + j % 2) % 2
                source = (v * 2 + w) * here.ny + y
                offsets += [source * rows + inside] if self.by_rows else [source * rows, inside]
        offsets = jnp.stack(offsets).astype(jnp.int32)
        stacks = [self.have[name] for name in names]
        count = [4] * len(stacks)
        any_space = pl.BlockSpec(memory_space=pl.ANY)
        size = here.nf * rows
        return pl.pallas_call(
            partial(place_kernel, count, rows, each, self.by_rows, widths),
            grid_spec=pltpu.PrefetchScalarGridSpec(
                num_scalar_prefetch=1,
                grid=(1,),
                in_specs=[any_space] * (1 + len(stacks)),
                out_specs=[pl.BlockSpec((size, w), lambda i, o: (0, 0)) for w in widths],
                scratch_shapes=[pltpu.SemaphoreType.DMA(((1 + sum(count)) * len(widths),))],
            ),
            out_shape=[jax.ShapeDtypeStruct((size, w), shard.dtype) for w in widths],
            compiler_params=pltpu.CompilerParams(
                vmem_limit_bytes=2 * size * sum(widths) * 2 + (1 << 20)
            ),
            cost_estimate=cost(6),
            name="place_weights",
        )(offsets, shard, *stacks)


class Reduce:
    def __init__(self, here):
        self.here = here
        self.split = False

    def swap(self, away):
        self.away = away.astype(BF)
        self.came = self.here.send(self.away, "c")

    def take(self, part):
        self.begin(part + self.came.astype(F32))

    def begin(self, part):
        part = part.astype(BF)
        here = self.here
        rows = part.shape[0] // here.nf
        self.part = part.reshape(2, 2, here.ny, rows, part.shape[1])
        self.axes = ["v", "w", "y"]

    def go(self, way, *after):
        here = self.here
        part = hold(self.part, *after)
        number, mine = here.number[way], here.mine[way]
        if way in "xc" and not self.axes:
            self.total = part.astype(F32)
            self.got = [here.send(part, way, s) for s in range(1, number)]
            return
        if way == "x":
            axis = len(self.axes)
            shape = part.shape
            part = part.reshape(shape[:axis] + (number, shape[axis] // number) + shape[axis + 1 :])
            self.split = True
        else:
            axis = self.axes.index(way)
            self.axes.pop(axis)
        self.total = lax.dynamic_index_in_dim(part, mine, axis, keepdims=False).astype(F32)
        self.got = [
            here.send(
                lax.dynamic_index_in_dim(part, (mine + s) % number, axis, keepdims=False), way, s
            )
            for s in range(1, number)
        ]

    def begin_x(self, part, *after):
        self.part, self.axes = part, []
        self.go("x", *after)

    def two(self, at):
        first, second = Reduce(self.here), Reduce(self.here)
        for one, cut in ((first, slice(0, at)), (second, slice(at, None))):
            one.part, one.axes = self.part[..., cut], list(self.axes)
        return first, second

    def join(self, first, second):
        self.part = jnp.concatenate([first.part, second.part], axis=-1)
        self.axes, self.split = list(first.axes), True

    def both(self):
        self.total = self.part.astype(F32)
        self.got = [self.here.send(self.part, "c")]

    def end(self):
        total = self.total
        for came in self.got:
            total = total + came.astype(F32)
        self.part = total.astype(BF)

    def step(self, way, *after):
        self.go(way, *after)
        self.end()

    def go_z(self, *after):
        here = self.here
        part = hold(self.part, *after)
        v, w = here.mine["v"], here.mine["w"]

        def at(dv, dw):
            one = lax.dynamic_index_in_dim(part, (v + dv) % 2, 0, keepdims=False)
            return lax.dynamic_index_in_dim(one, (w + dw) % 2, 0, keepdims=False)

        self.total = at(0, 0).astype(F32)
        self.got = [here.send(at(*d), way) for d, way in (((1, 0), "v"), ((1, 1), "u"), ((0, 1), "w"))]
        self.axes = self.axes[2:]

    def rows(self):
        if self.split:
            self.part = join_way(self.here, self.part, "x", 0)

    def other(self):
        return self.here.send(self.part, "c")


def meet(value, *sums):
    value, came = lax.optimization_barrier((value, [one.got for one in sums]))
    for one, got in zip(sums, came):
        one.got = got
        one.end()
    return value


def join_way(here, array, way, axis):
    number, mine = here.number[way], here.mine[way]
    got = [array] + [here.send(array, way, s) for s in range(1, number)]
    if number == 2:
        ahead = jnp.concatenate(got, axis=axis)
        behind = jnp.concatenate(got[::-1], axis=axis)
        return jnp.where(mine == 0, ahead, behind)
    stack = jnp.stack(got)
    order = (mine - jnp.arange(number)) % number
    stack = jnp.take(stack, order, axis=0)
    return jnp.concatenate([stack[i] for i in range(number)], axis=axis)


def gather_apart(here, shard):
    rows = shard.shape[0] // here.nr
    piece = lax.dynamic_slice_in_dim(shard, here.r * rows, rows, 0)
    return lax.all_gather(piece, ("fsdp", "rep"), axis=0, tiled=True)


def scatter_owners(array):
    return lax.psum_scatter(array, "fsdp", scatter_dimension=0, tiled=True)


def sum_x(here, array, *after):
    array = hold(array, *after)
    total = array.astype(F32)
    for s in range(1, here.nx):
        total = total + here.send(array, "x", s).astype(F32)
    return total.astype(BF)


def contract(left, right, left_dim, right_dim):
    return lax.dot_general(
        left, right, (((left_dim,), (right_dim,)), ((), ())), preferred_element_type=F32
    )


def rms_norm(values, gain):
    return values * lax.rsqrt(jnp.mean(values * values, axis=-1, keepdims=True) + EPSILON) * gain


def swiglu(pair):
    half = pair.shape[1] // 2
    return jax.nn.silu(pair[:, :half]) * pair[:, half:]


def kv_order(array):
    eighth = array.shape[1] // 24
    starts, sizes = (8, 16, 14, 22), (6, 6, 2, 2)
    return [array[:, i * eighth : (i + n) * eighth] for i, n in zip(starts, sizes)]


def from_behind(value, steps):
    count = lax.axis_size("fsdp")
    first, last = (max(0, -steps), min(count, count - steps))
    return lax.ppermute(value, "fsdp", [(source, source + steps) for source in range(first, last)])


def to_owners(parts, fanout):
    heads, d, width = parts.shape
    cut = parts.reshape(heads, d, fanout, width // fanout)
    return jnp.swapaxes(cut, 1, 2).reshape(heads * fanout, d, width // fanout)


def to_heads(parts, fanout):
    owners, d, width = parts.shape
    cut = parts.reshape(owners // fanout, fanout, d, width)
    return jnp.swapaxes(cut, 1, 2).reshape(owners // fanout, d, width * fanout)


def swap(value):
    return lax.all_to_all(value, "fsdp", 0, 0, tiled=True)


def by_core(here, for_zero, for_one):
    return jnp.where(here.mine["c"] == 0, for_zero, for_one)


def on_device(
    hidden_in,
    seg_ids,
    attn_gain,
    qkv_weight,
    beta_weight,
    gate_weight,
    conv_taps,
    out_gain,
    out_weight,
    ffn_gain,
    ffn_gate,
    ffn_up,
    ffn_down,
    cotangent,
):
    here = Place()
    row_count, width = hidden_in.shape
    heads = beta_weight.shape[1]
    head_dim = width // heads
    blocks = row_count // SPAN
    rim = 8
    lanes = 128
    hidden_units = ffn_gate.shape[1]

    numbers = seg_ids + 1

    small = [attn_gain, out_gain, ffn_gain, conv_taps]
    shard_rows = qkv_weight.shape[0]
    flat = jnp.concatenate([a.reshape(-1) for a in small])
    columns = -(-flat.size // shard_rows)
    flat = jnp.pad(flat, (0, columns * shard_rows - flat.size)).reshape(shard_rows, columns)
    extra = jnp.concatenate(
        [beta_weight, flat, jnp.zeros((shard_rows, lanes - heads - columns), BF)], axis=1
    )
    first = Gather(
        here,
        jnp.concatenate(kv_order(qkv_weight) + [extra], axis=1),
        [2 * width, lanes],
        True,
    )
    second = Gather(
        here,
        jnp.concatenate([qkv_weight[:, :width], gate_weight, out_weight], axis=1),
        [2 * width, width],
        True,
    )
    pair_full = gather_apart(here, jnp.concatenate([ffn_gate, ffn_up], axis=1))
    down_full = gather_apart(here, ffn_down)
    rim_rows = from_behind(hidden_in[row_count - rim :], 1)
    rim_ids = from_behind(numbers[row_count - rim :], 1)
    first.move("v", "w")
    first.move("vw")
    first.pile()
    if not first.plain:
        first.have["z"], rim_rows, rim_ids = lax.optimization_barrier((first.have["z"], rim_rows, rim_ids))
    first.move("zy", "zx")
    first.move("zc")
    second.move("v", "w", after=first.got("z"))
    first.move("zyx", after=first.got("zx", "zc"))
    first.move("zyc", "zxc")
    first.move("zyxc", after=first.got("zyc", "zxc"))
    kv_full, extra_full = first.place()

    small_full = extra_full[:, heads : heads + columns].reshape(here.nf, -1)
    cuts, at = [], 0
    for array in small:
        cuts.append(small_full[:, at : at + array.size].astype(F32))
        at += array.size
    attn_scale = cuts[0].reshape(-1)
    outgain_scale = cuts[1].reshape(1, -1)
    ffngain_scale = cuts[2].reshape(-1)
    taps_count = conv_taps.shape[0]
    taps_scale = jnp.swapaxes(cuts[3].reshape(here.nf, taps_count, -1), 0, 1).reshape(taps_count, -1)
    query_taps = taps_scale[:, :width]
    kv_taps = jnp.concatenate(kv_order(taps_scale), axis=1)
    residual = hidden_in.astype(F32)
    extended_in = jnp.concatenate([hidden_in, rim_rows]).astype(F32)
    normed_ext = rms_norm(extended_in, attn_scale).astype(BF)
    normed_low = normed_ext[:row_count]
    kv_pre = jnp.dot(normed_ext, kv_full, preferred_element_type=F32)
    second.move("vw", after=[kv_full])
    second.pile()
    second.move("zy", "zx", after=[kv_pre])
    beta_pre = jnp.dot(normed_low, extra_full, preferred_element_type=F32)[:, :heads]
    rates = jax.nn.sigmoid(beta_pre)
    ids = jnp.concatenate([rim_ids, numbers]).astype(F32)
    own_ids = numbers.astype(F32)
    before = ids[rim - 1 : rim - 1 + row_count : SPAN]
    cols = jnp.concatenate(
        [rates, own_ids[:, None]]
        + [(ids[rim - j : rim - j + row_count] == own_ids).astype(F32)[:, None] for j in (1, 2, 3)]
        + [jnp.zeros((row_count, heads - 4), F32)],
        1,
    )
    rows = jnp.concatenate(
        [
            jnp.swapaxes(rates.reshape(blocks, SPAN, heads), 1, 2),
            own_ids.reshape(blocks, 1, SPAN),
            jnp.broadcast_to(before[:, None, None], (blocks, 1, SPAN)),
            jnp.zeros((blocks, heads - 2, SPAN), F32),
        ],
        1,
    )
    key_low, value_low, kv_mixed, w, u, a, moves = delta_summary(kv_pre, kv_taps, cols, rows, heads)
    second.move("zyx", after=[moves] + second.got("zx"))
    second.move("zc", "zyc", "zxc", after=[moves])
    fanout = here.nf // heads
    if fanout > 1:
        moves = jnp.concatenate(
            [
                to_owners(moves[:, :, :head_dim], fanout),
                jnp.repeat(moves[:, :, head_dim:], fanout, axis=0),
            ],
            axis=2,
        )
    owned = swap(moves)
    second.move("zyxc", after=[owned])
    qg_full, outw_full = second.place()
    qg_pre = jnp.dot(normed_ext, qg_full, preferred_element_type=F32)
    entry = swap(scan_states(owned))
    if fanout > 1:
        entry = to_heads(entry, fanout)
    query_low, q_mixed, gated_low, attn_heads, fresh, kept = delta_forward(
        qg_pre, query_taps, key_low, w, u, cols, rows, entry, outgain_scale, heads
    )
    middle = residual + jnp.dot(gated_low, outw_full, preferred_element_type=F32)
    normed_two, norm_two_back = jax.vjp(partial(rms_norm, gain=ffngain_scale), middle)
    normed_two_low = normed_two.astype(BF)
    pair_pre = jnp.dot(normed_two_low, pair_full, preferred_element_type=F32)
    hidden_ff, swiglu_back = jax.vjp(swiglu, pair_pre)
    hidden_low = hidden_ff.astype(BF)

    c = here.mine["c"]

    def shares(array, start, size):
        half = size // 2
        cut = [lax.dynamic_slice_in_dim(array, start + at * half, half, 1) for at in (1 - c, c)]
        return cut

    theirs, ours = shares(cotangent, 0, width)
    down_sum = Reduce(here)
    down_sum.swap(contract(hidden_low, theirs, 0, 0))
    hidden_grad = contract(cotangent, down_full, 1, 1)
    (pair_grad,) = swiglu_back(hidden_grad)
    pair_low = pair_grad.astype(BF)
    down_half = (contract(hidden_low, hold(ours, pair_low), 0, 0) + down_sum.came.astype(F32)).astype(BF)
    down_apart = scatter_owners(down_half)
    top_grad = cotangent.astype(F32)
    normed_two_grad = contract(pair_low, pair_full, 1, 1)
    (middle_back,) = norm_two_back(normed_two_grad)
    middle_grad = top_grad + middle_back
    middle_low = middle_grad.astype(BF)
    gated_grad = contract(middle_low, outw_full, 1, 1)
    theirs, ours = shares(pair_low, 0, 2 * hidden_units)
    pair_sum = Reduce(here)
    pair_sum.swap(contract(normed_two_low, theirs, 0, 0))
    pair_half = (contract(normed_two_low, ours, 0, 0) + pair_sum.came.astype(F32)).astype(BF)
    pair_apart = scatter_owners(pair_half)
    gated_grad = hold(gated_grad, down_half, pair_half)
    heads_grad, gatepre_low, outgain_grad, local_later = delta_adjoint(
        query_low, key_low, w, cols, rows, gated_grad, attn_heads, qg_pre, outgain_scale, heads
    )
    if fanout > 1:
        local_later = to_owners(local_later, fanout)
    came_later = swap(local_later)

    summed_later = scan_grads(owned, came_later)
    later = swap(summed_later)
    if fanout > 1:
        later = to_heads(later, fanout)
    hidden_held, middle_held, gatepre_held = hold((hidden_low, middle_low, gatepre_low), summed_later)
    out_grad = contract(gated_low, middle_held, 0, 0)
    gate_grad = contract(normed_low, gatepre_held, 0, 0)
    other_sum = Reduce(here)
    other_sum.swap(by_core(here, gate_grad, out_grad))
    output = (middle + jnp.dot(hidden_held, down_full, preferred_element_type=F32)).astype(BF)
    other_sum.take(hold(by_core(here, out_grad, gate_grad), output))
    later = hold(later, other_sum.part)
    other_x, other_y = other_sum.two(width // 2)
    other_x.go("x", later)
    other_y.go("y", later)
    state = (query_low, key_low, value_low, w, u, a, fresh, kept, heads_grad, cols, rows)
    mixed_a, beta_a, taps_a = delta_backward(
        0, *state, later, q_mixed, qg_pre, query_taps, kv_mixed, kv_pre, kv_taps, heads
    )
    mixed_a = meet(mixed_a, other_x, other_y)
    other_x.go("y")
    other_y.go("x")
    a_sum = Reduce(here)
    cut = [number * head_dim for number in head_parts(heads)]
    theirs, ours = shares(mixed_a, 0, 3 * cut[0])
    a_sum.swap(contract(normed_ext, theirs, 0, 0))
    a_sum.take(contract(normed_ext, ours, 0, 0))
    later = meet(hold(later, a_sum.part), other_x, other_y)
    other_sum.join(other_x, other_y)
    a_x, a_y = a_sum.two((a_sum.part.shape[-1] // lanes + 1) // 2 * lanes)
    a_x.go("x", later)
    a_y.go("y", later)
    other_sum.go("w", later)
    mixed_b, beta_b, taps_b = delta_backward(
        1, *state, later, q_mixed, qg_pre, query_taps, kv_mixed, kv_pre, kv_taps, heads
    )
    mixed_b = hold(meet(mixed_b, other_sum, a_x, a_y), pair_apart)
    def by_kind(first_heads, other_heads):
        pieces = []
        for i in range(3):
            for array, wide in zip((first_heads, other_heads), cut):
                pieces.append(array[:, i * wide : (i + 1) * wide])
        return jnp.concatenate(pieces, axis=1)

    betapre_low = (beta_a + beta_b).astype(BF)
    taps_grad = by_kind(taps_a, taps_b)
    parts = (
        outgain_grad.reshape(here.nf, -1),
        jnp.swapaxes(taps_grad.reshape(taps_count, here.nf, -1), 0, 1).reshape(here.nf, -1),
    )
    flat = jnp.concatenate(parts, axis=1)
    flat = jnp.pad(flat, ((0, 0), (0, columns * shard_rows - flat.shape[1])))
    extra = jnp.pad(flat.reshape(width, columns), ((0, 0), (heads, lanes - heads - columns)))
    small_sum = Reduce(here)
    small_sum.begin(contract(normed_low, hold(betapre_low, mixed_b), 0, 0) + extra)
    small_sum.both()
    b_sum = Reduce(here)
    theirs, ours = shares(mixed_b, 0, 3 * cut[1])
    b_sum.swap(contract(normed_ext, theirs, 0, 0))
    b_sum.take(contract(normed_ext, ours, 0, 0))
    small_sum.end()
    mixed_b = hold(mixed_b, b_sum.part, small_sum.part)
    b_sum.go("x")
    a_x.go("y", mixed_b)
    a_y.go("x", mixed_b)
    other_sum.go("v", mixed_b)
    small_sum.go("x")
    wide_grad = (
        contract(mixed_a[:, cut[0] :], kv_full[:, : 2 * cut[0]], 1, 1)
        + contract(mixed_b[:, cut[1] :], kv_full[:, 2 * cut[0] :], 1, 1)
        + contract(mixed_a[:, : cut[0]], qg_full[:, : cut[0]], 1, 1)
        + contract(mixed_b[:, : cut[1]], qg_full[:, cut[0] : width], 1, 1)
    )
    rim_grad = from_behind(wide_grad[row_count:].astype(BF), -1).astype(F32)
    normed_grad = (
        wide_grad[:row_count]
        + jnp.pad(rim_grad, ((row_count - rim, 0), (0, 0)))
        + contract(betapre_low, extra_full, 1, 1)
        + contract(gatepre_low, qg_full[:, width:], 1, 1)
    )
    normed_grad = meet(normed_grad, b_sum, a_x, a_y, other_sum, small_sum)
    a_sum.join(a_x, a_y)
    b_sum.go("y")
    small_sum.go("y")
    pair_sum.begin_x(pair_apart, normed_grad)
    a_sum.go("w")
    (input_back,) = jax.vjp(partial(rms_norm, gain=attn_scale), residual)[1](normed_grad)
    input_grad = meet(
        (middle_grad + input_back).astype(BF), b_sum, a_sum, small_sum, pair_sum
    )
    b_sum.go("w", input_grad)
    a_sum.go("v", input_grad)
    small_sum.go("w", input_grad)
    down_sum.begin_x(down_apart, input_grad)
    for one in (b_sum, a_sum, small_sum):
        one.end()
    down_sum.end()
    b_sum.go("v", a_sum.part, down_sum.part)
    small_sum.go("v", a_sum.part)
    pair_part, down_part = hold((pair_sum.part, down_sum.part), a_sum.part)
    other = here.send(pair_part, "c")
    down_total = join_way(here, down_part, "c", 1).astype(F32)
    held = meet(a_sum.part, b_sum, small_sum)
    both = Reduce(here)
    both.part = jnp.concatenate([b_sum.part, held, other_sum.part, small_sum.part], axis=1)
    both.split = True
    both.rows()
    hidgate_total = by_core(here, pair_part, other).astype(F32)
    hidup_total = by_core(here, other, pair_part).astype(F32)
    whole = both.other()
    ends = [0]
    for one in (b_sum, a_sum, other_sum, small_sum):
        ends.append(ends[-1] + one.part.shape[1])

    def joined(start, end):
        mine, theirs = both.part[:, start:end], whole[:, start:end]
        return by_core(here, mine, theirs), by_core(here, theirs, mine)

    b_both, a_both, other_both = [joined(*pair) for pair in zip(ends[:3], ends[1:4])]
    outproj_total, gate_total = [part.astype(F32) for part in other_both]
    qkv_total = by_kind(jnp.concatenate(a_both, axis=1), jnp.concatenate(b_both, axis=1)).astype(F32)
    extra = both.part[:, ends[3] :].astype(F32)
    beta_total = extra[:, :heads]

    def gain_grad(gain, pairs):
        total = sum(jnp.sum(weight.astype(F32) * grad, axis=1) for weight, grad in pairs)
        return total / gain.astype(F32)

    attngain_total = gain_grad(
        attn_gain, ((qkv_weight, qkv_total), (beta_weight, beta_total), (gate_weight, gate_total))
    )
    ffngain_total = gain_grad(ffn_gain, ((ffn_gate, hidgate_total), (ffn_up, hidup_total)))
    flat = extra[:, heads : heads + columns].reshape(-1)
    cut, at = [], 0
    for part in parts:
        cut.append(flat[at : at + part.shape[1]])
        at += part.shape[1]
    return (
        output,
        input_grad,
        attngain_total,
        qkv_total,
        beta_total,
        gate_total,
        cut[1].reshape(conv_taps.shape),
        cut[0],
        outproj_total,
        ffngain_total,
        hidgate_total,
        hidup_total,
        down_total,
    )


def solution(mesh):
    placed = (
        P(("rep", "fsdp"), None),
        P(("rep", "fsdp")),
        P("fsdp"),
        P("fsdp", None),
        P("fsdp", None),
        P("fsdp", None),
        P(None, "fsdp"),
        P("fsdp"),
        P("fsdp", None),
        P("fsdp"),
        P("fsdp", None),
        P("fsdp", None),
        P("fsdp", None),
        P(("rep", "fsdp"), None),
    )
    return jax.shard_map(
        on_device,
        mesh=mesh,
        in_specs=placed,
        out_specs=(
            P(("rep", "fsdp"), None),
            P(("rep", "fsdp"), None),
            P("fsdp"),
            P("fsdp", None),
            P("fsdp", None),
            P("fsdp", None),
            P(None, "fsdp"),
            P("fsdp"),
            P("fsdp", None),
            P("fsdp"),
            P("fsdp", None),
            P("fsdp", None),
            P("fsdp", None),
        ),
        check_vma=False,
    )
```

```python
from functools import partial

import jax
import jax.numpy as jnp
from jax import lax
from jax.experimental import pallas as pl
from jax.experimental.pallas import tpu as pltpu
from jax.sharding import PartitionSpec as P

SPAN = 64
TOGETHER = 8
EPSILON = 1e-06
BF = jnp.bfloat16
F32 = jnp.float32


def nn(a, b):
    return lax.dot_general(a, b, (((1,), (0,)), ((), ())), preferred_element_type=F32)


def nt(a, b):
    return lax.dot_general(a, b, (((1,), (1,)), ((), ())), preferred_element_type=F32)


def tn(a, b):
    return lax.dot_general(a, b, (((0,), (0,)), ((), ())), preferred_element_type=F32)


def in_turn(body, count, together):
    for start in range(0, count, together):
        running = [body(h) for h in range(start, min(start + together, count))]
        while running:
            running = [one for one in running if next(one, False)]


def block_masks(cols_ref, rows_ref, heads):
    n = SPAN
    row = lax.broadcasted_iota(jnp.int32, (n, n), 0)
    col = lax.broadcasted_iota(jnp.int32, (n, n), 1)
    ids = cols_ref[:, heads : heads + 1]
    ids_row = rows_ref[0, heads : heads + 1, :]
    before = rows_ref[0, heads + 1 : heads + 2, :]
    end = ids_row[:, n - 1 : n]
    same = ids == ids_row
    first = (ids == before[:, :1]).astype(F32)
    last = (ids == end).astype(F32)
    keep = (end == before[:, :1]).astype(F32)
    return row, col, same, first, last, keep


def sigmoid(z):
    return 0.5 * jnp.tanh(0.5 * z) + 0.5


def shifted_rows(x, prev, masks):
    both = jnp.concatenate([prev, x], axis=0)
    lead = prev.shape[0]
    return [x] + [pltpu.roll(both, j, 0)[lead:] * masks[j - 1] for j in (1, 2, 3)]


def mix_rows(rows, taps):
    mixed = rows[0] * taps[0:1]
    for j in (1, 2, 3):
        mixed = mixed + rows[j] * taps[j : j + 1]
    return mixed


def lag_masks(cols_ref, heads):
    return [cols_ref[:, heads + j : heads + j + 1] for j in (1, 2, 3)]


def head_parts(heads):
    return heads - heads // 4, heads // 4


def kv_at(heads, d, h):
    first, other = head_parts(heads)
    number, start, inside = (first, 0, h) if h < first else (other, 2 * first, h - first)
    at = (start + inside) * d
    return slice(at, at + d), slice(at + number * d, at + number * d + d)


def summary_kernel(
    heads, d, pre_ref, prev_ref, taps_ref, cols_ref, rows_ref,
    k_ref, v_ref, z_ref, w_ref, u_ref, a_ref, x_ref, state, levels,
):
    n = SPAN
    block = pl.program_id(0)

    @pl.when(block == 0)
    def _():
        at = lax.broadcasted_iota(jnp.int32, (n, n), 0)
        to = lax.broadcasted_iota(jnp.int32, (n, n), 1)
        for i in range(levels.shape[0]):
            size = 1 << i
            level = jnp.logical_and(
                (at // (2 * size)) == (to // (2 * size)),
                jnp.logical_and(((at // size) & 1) == 1, ((to // size) & 1) == 0),
            )
            levels[i] = level.astype(F32).astype(BF)
        r = lax.broadcasted_iota(jnp.int32, (d, 2 * d), 0)
        c = lax.broadcasted_iota(jnp.int32, (d, 2 * d), 1)
        unit = (r + d == c).astype(F32)
        for h in range(heads):
            state[h] = unit

    row, col, same, first, last, keep = block_masks(cols_ref, rows_ref, heads)
    lower = jnp.logical_and(same, row > col)
    unit = (row == col).astype(F32).astype(BF)
    masks = lag_masks(cols_ref, heads)
    keys, mixing, inverse = ([None] * heads for i in range(3))
    def features(h):
        cut = slice(h * d, (h + 1) * d)
        at_k, at_v = kv_at(heads, d, h)
        z = mix_rows(shifted_rows(pre_ref[:, at_k], prev_ref[:, at_k], masks), taps_ref[:, at_k])
        z_ref[:, at_k] = z
        yield True
        act = z * sigmoid(z)
        root = lax.rsqrt(jnp.sum(act * act, axis=1, keepdims=True) + EPSILON)
        yield True
        keys[h] = (act * root).astype(BF)
        k_ref[:, cut] = keys[h]
        yield True
        z = mix_rows(shifted_rows(pre_ref[:, at_v], prev_ref[:, at_v], masks), taps_ref[:, at_v])
        z_ref[:, at_v] = z
        v_ref[:, cut] = (z * sigmoid(z)).astype(BF)
        m = jnp.where(lower, nt(keys[h], keys[h]) * cols_ref[:, h : h + 1], 0.0).astype(BF)
        yield True
        mixing[h] = m
        inverse[h] = unit - m * levels[0]

    in_turn(features, heads, TOGETHER)
    for i in range(1, levels.shape[0]):
        level = levels[i]
        inner = [nn(mixing[h] * level, inverse[h]).astype(BF) for h in range(heads)]
        for h in range(heads):
            inverse[h] = inverse[h] - nn(inverse[h], inner[h]).astype(BF) * level
    def advance(h):
        cut = slice(h * d, (h + 1) * d)
        a_ref[h] = inverse[h]
        scaled = (inverse[h].astype(F32) * rows_ref[0, h : h + 1, :]).astype(BF)
        yield True
        both = nn(scaled, jnp.concatenate([keys[h], v_ref[:, cut]], axis=1))
        yield True
        w = both[:, :d].astype(BF)
        u = both[:, d:].astype(BF)
        w_ref[:, cut] = w
        u_ref[:, cut] = u
        yield True
        held = state[h]
        moved = nn(w, held.astype(BF)) * first
        yield True
        fresh = (jnp.concatenate([u.astype(F32), jnp.zeros((n, d), F32)], axis=1) - moved).astype(BF)
        yield True
        key_last = keys[h] * last.astype(BF)
        yield True
        state[h] = keep * held + tn(key_last, fresh)

    in_turn(advance, heads, TOGETHER)

    @pl.when(block == pl.num_programs(0) - 1)
    def _():
        x_ref[...] = state[...].astype(BF)


def forward_kernel(
    heads, d, pre_ref, prev_ref, taps_ref, k_ref, w_ref, u_ref, cols_ref, rows_ref, s_ref, gate_ref, gain_ref,
    q_ref, z_ref, y_ref, o_ref, e_ref, kept_ref, state,
):
    n = SPAN
    block = pl.program_id(0)

    @pl.when(block == 0)
    def _():
        state[...] = s_ref[...].astype(F32)

    row, col, same, first, last, keep = block_masks(cols_ref, rows_ref, heads)
    visible = jnp.logical_and(same, row >= col)
    masks = lag_masks(cols_ref, heads)
    def one_head(h):
        cut = slice(h * d, (h + 1) * d)
        z = mix_rows(shifted_rows(pre_ref[:, cut], prev_ref[:, cut], masks), taps_ref[:, cut])
        z_ref[:, cut] = z
        q = (z * sigmoid(z) * d ** (-0.5)).astype(BF)
        q_ref[:, cut] = q
        yield True
        k, w = k_ref[:, cut], w_ref[:, cut]
        held = state[h]
        held_low = held.astype(BF)
        kept_ref[0, h] = held_low
        both = nn(jnp.concatenate([w, q], axis=0), held_low)
        yield True
        fresh = (u_ref[:, cut].astype(F32) - first * both[:n]).astype(BF)
        e_ref[:, cut] = fresh
        yield True
        scores = jnp.where(visible, nt(q, k), 0.0).astype(BF)
        yield True
        out = first * both[n:] + nn(scores, fresh)
        yield True
        key_last = k * last.astype(BF)
        state[h] = keep * held + tn(key_last, fresh)
        yield True
        o_ref[:, cut] = out
        yield True
        g = gate_ref[:, cut]
        root = lax.rsqrt(jnp.mean(out * out, axis=1, keepdims=True) + EPSILON)
        yield True
        y_ref[:, cut] = (out * root * gain_ref[...] * (g * sigmoid(g))).astype(BF)

    in_turn(one_head, heads, TOGETHER)


def adjoint_kernel(
    heads, d, q_ref, k_ref, w_ref, cols_ref, rows_ref, dy_ref, o_ref, gate_ref, gain_ref,
    do_ref, dgate_ref, dgain_ref, ds_ref, state,
):
    n = SPAN
    step = pl.program_id(0)

    @pl.when(step == 0)
    def _():
        state[...] = jnp.zeros_like(state)
        dgain_ref[...] = jnp.zeros_like(dgain_ref)

    row, col, same, first, last, keep = block_masks(cols_ref, rows_ref, heads)
    visible = jnp.logical_and(same, row >= col)
    first_low = first.astype(BF)
    gain = gain_ref[...]
    gain_sum = jnp.zeros((1, d), F32)
    def one_head(h):
        nonlocal gain_sum
        cut = slice(h * d, (h + 1) * d)
        q, k, w = q_ref[:, cut], k_ref[:, cut], w_ref[:, cut]
        o, g, dy = o_ref[:, cut], gate_ref[:, cut], dy_ref[:, cut]
        root = lax.rsqrt(jnp.mean(o * o, axis=1, keepdims=True) + EPSILON)
        yield True
        unit = o * root
        sig = sigmoid(g)
        m = g * sig
        t = dy * m
        gain_sum = gain_sum + jnp.sum(t * unit, axis=0, keepdims=True)
        tg = t * gain
        do = root * (tg - unit * jnp.mean(tg * unit, axis=1, keepdims=True))
        yield True
        dgate_ref[:, cut] = (dy * gain * unit * (sig * (1.0 + g * (1.0 - sig)))).astype(BF)
        do_low = do.astype(BF)
        do_ref[:, cut] = do_low
        yield True
        scores = jnp.where(visible, nt(q, k), 0.0).astype(BF)
        yield True
        later = state[h]
        de = last * nn(k, later.astype(BF)) + tn(scores, do_low)
        yield True
        left = jnp.concatenate([q * first_low, w * -first_low], axis=0)
        right = jnp.concatenate([do_low, de.astype(BF)], axis=0)
        state[h] = keep * later + tn(left, right)
        yield True

    in_turn(one_head, heads, TOGETHER)
    dgain_ref[...] += gain_sum

    @pl.when(step == pl.num_programs(0) - 1)
    def _():
        ds_ref[...] = state[...].astype(BF)


def backward_kernel(
    heads, part, d, q_ref, k_ref, v_ref, w_ref, u_ref, a_ref, e_ref, kept_ref, do_ref, cols_ref, rows_ref, s_ref,
    qz_ref, qpre_ref, qrim_ref, qtaps_ref, kvz_ref, kvpre_ref, kvrim_ref, kvtaps_ref,
    dpre_ref, dbeta_ref, dtaps_ref, state, carry,
):
    n = SPAN
    step = pl.program_id(0)
    number = head_parts(heads)[part]
    base = heads - number if part else 0

    @pl.when(step == 0)
    def _():
        state[...] = s_ref[...].astype(F32)
        carry[...] = jnp.zeros_like(carry)
        dtaps_ref[...] = jnp.zeros_like(dtaps_ref)

    @pl.when(step < pl.num_programs(0) - 1)
    def _():
        row, col, same, first, last, keep = block_masks(cols_ref, rows_ref, heads)
        visible = jnp.logical_and(same, row >= col)
        lower = jnp.logical_and(same, row > col)
        lane = lax.broadcasted_iota(jnp.int32, (n, d), 1)
        masks = lag_masks(cols_ref, heads)
        rate_grads = jnp.zeros((n, d), F32)

        first_low = first.astype(BF)

        def conv_back(dact, z, sig, pre, taps, at):
            dconv = dact * (sig * (1.0 + z * (1.0 - sig)))
            here = slice(at, at + d)
            dpre = dconv * taps[0:1]
            sums = [jnp.sum(dconv * pre, axis=0, keepdims=True)]
            for j in (1, 2, 3):
                masked = dconv * masks[j - 1]
                both = jnp.concatenate([masked, carry[j - 1, :, here]], axis=0)
                moved = pltpu.roll(both, both.shape[0] - j, 0)[:n]
                dpre = dpre + moved * taps[j : j + 1]
                sums.append(jnp.sum(moved * pre, axis=0, keepdims=True))
                carry[j - 1, :, here] = masked[:8]
            dtaps_ref[:, here] += jnp.concatenate(sums, axis=0)
            dpre_ref[:, here] = dpre.astype(BF)

        def one_head(h):
            nonlocal rate_grads
            cut = slice(h * d, (h + 1) * d)
            cut_v = slice((number + h) * d, (number + h + 1) * d)
            q, k, v, w, u = q_ref[:, cut], k_ref[:, cut], v_ref[:, cut], w_ref[:, cut], u_ref[:, cut]
            do, e, held = do_ref[:, cut], e_ref[:, cut], kept_ref[0, h]
            at = base + h
            rate = cols_ref[:, at : at + 1]
            later = state[h]
            later_low = later.astype(BF)
            scores = jnp.where(visible, nt(q, k), 0.0).astype(BF)
            yield True
            de = last * nn(k, later_low) + tn(scores, do)
            yield True
            de_low = de.astype(BF)
            dscores = jnp.where(visible, nt(do, e), 0.0).astype(BF)
            yield True
            both = nt(jnp.concatenate([do, de_low], axis=0), held)
            yield True
            dq = first * both[:n] + nn(dscores, k)
            dw = -first * both[n:]
            dk = tn(dscores, q) + last * nt(e, later_low)
            yield True
            pg = tn(a_ref[h], jnp.concatenate([dw.astype(BF), de_low], axis=1))
            yield True
            p, g = pg[:, :d], pg[:, d:]
            dmix = jnp.where(lower, -nt(pg.astype(BF), jnp.concatenate([w, u], axis=1)), 0.0).astype(BF)
            yield True
            kf = k.astype(F32)
            drk = p + nn(dmix, k)
            dk = dk + tn(dmix, (kf * rate).astype(BF)) + rate * drk
            yield True
            dr = jnp.sum(drk * kf + g * v.astype(F32), axis=1, keepdims=True)
            rate_grads = jnp.where(lane == at, dr * rate * (1.0 - rate), rate_grads)
            left = jnp.concatenate([q * first_low, w * -first_low], axis=0)
            right = jnp.concatenate([do, de_low], axis=0)
            state[h] = keep * later + tn(left, right)
            yield True

            z = qz_ref[:, cut]
            conv_back(dq * d ** (-0.5), z, sigmoid(z), qpre_ref[:, cut], qtaps_ref[:, cut], h * d)
            yield True
            z = kvz_ref[:, cut]
            sig = sigmoid(z)
            act = z * sig
            root = lax.rsqrt(jnp.sum(act * act, axis=1, keepdims=True) + EPSILON)
            unit = act * root
            dact = root * (dk - unit * jnp.sum(unit * dk, axis=1, keepdims=True))
            conv_back(dact, z, sig, kvpre_ref[:, cut], kvtaps_ref[:, cut], (number + h) * d)
            yield True
            z = kvz_ref[:, cut_v]
            conv_back(
                rate * g, z, sigmoid(z), kvpre_ref[:, cut_v], kvtaps_ref[:, cut_v], (2 * number + h) * d
            )

        in_turn(one_head, number, TOGETHER)
        dbeta_ref[...] = rate_grads

    @pl.when(step == pl.num_programs(0) - 1)
    def _():
        wide = number * d
        for i, taps_ref, rim_ref, at in (
            (0, qtaps_ref, qrim_ref, 0),
            (1, kvtaps_ref, kvrim_ref, 0),
            (2, kvtaps_ref, kvrim_ref, wide),
        ):
            here, there = slice(i * wide, (i + 1) * wide), slice(at, at + wide)
            dpre = jnp.zeros((8, wide), F32)
            sums = [jnp.zeros((1, wide), F32)]
            for j in (1, 2, 3):
                held = carry[j - 1, :, here]
                moved = jnp.concatenate([jnp.zeros_like(held), held], axis=0)[j : 8 + j]
                dpre = dpre + moved * taps_ref[j : j + 1, there]
                sums.append(jnp.sum(moved * rim_ref[:, there], axis=0, keepdims=True))
            dtaps_ref[:, here] += jnp.concatenate(sums, axis=0)
            dpre_ref[0:8, here] = dpre.astype(BF)


def prefix_kernel(peers, x_ref, out_ref):
    cols = out_ref.shape[2]
    held = jnp.zeros(out_ref.shape[1:], F32)
    for i in range(peers):
        out_ref[i] = held.astype(BF)
        held = nn(x_ref[i, :, cols:], held.astype(BF)) + x_ref[i, :, :cols].astype(F32)


def suffix_kernel(peers, t_ref, g_ref, out_ref):
    held = jnp.zeros(out_ref.shape[1:], F32)
    cols = out_ref.shape[2]
    for i in reversed(range(peers)):
        out_ref[i] = held.astype(BF)
        held = tn(t_ref[i, :, cols:], held.astype(BF)) + g_ref[i].astype(F32)


VMEM_LIMIT = 16 * 1024 * 1024


def in_hbm(*arrays):
    return [pltpu.with_memory_space_constraint(a, pltpu.HBM) for a in arrays]


def params():
    return pltpu.CompilerParams(dimension_semantics=("arbitrary",), vmem_limit_bytes=VMEM_LIMIT)


def cost(microseconds):
    return pl.CostEstimate(
        flops=int(microseconds * 1e9), bytes_accessed=int(microseconds * 3e6), transcendentals=0
    )


def specs(blocks, heads, d, flip):
    at = (lambda b: blocks - 1 - b) if flip else (lambda b: b)
    wide = pl.BlockSpec((SPAN, heads * d), lambda b: (at(b), 0))
    cols = pl.BlockSpec((SPAN, 2 * heads), lambda b: (at(b), 0))
    rows = pl.BlockSpec((1, 2 * heads, SPAN), lambda b: (at(b), 0, 0))
    state = pl.BlockSpec((heads, d, d), lambda b: (0, 0, 0))
    mix = pl.BlockSpec((heads, SPAN, SPAN), lambda b: (0, at(b), 0))
    kept = pl.BlockSpec((1, heads, d, d), lambda b: (at(b), 0, 0, 0))
    gain = pl.BlockSpec((1, d), lambda b: (0, 0))
    return wide, cols, rows, state, mix, kept, gain


def shape(dims, kind):
    return pltpu.HBM(dims, kind)


def near(dims, kind):
    return jax.ShapeDtypeStruct(dims, kind)


def before_block(blocks, rim, size, column):
    def index(b):
        per = SPAN // rim
        return jnp.where(b == 0, blocks * per, b * per - 1), column

    return pl.BlockSpec((rim, size), index)


def delta_summary(pre, taps, cols, rows, heads):
    count, width = cols.shape[0], pre.shape[1] // 2
    d, blocks = width // heads, count // SPAN
    rim = pre.shape[0] - count
    wide, c, r, state, mix, kept, gain = specs(blocks, heads, d, False)
    return pl.pallas_call(
        partial(summary_kernel, heads, d),
        grid=(blocks,),
        in_specs=[
            pl.BlockSpec((SPAN, 2 * width), lambda b: (b, 0)),
            before_block(blocks, rim, 2 * width, 0),
            pl.BlockSpec((4, 2 * width), lambda b: (0, 0)),
            c,
            r,
        ],
        out_specs=[
            wide,
            wide,
            pl.BlockSpec((SPAN, 2 * width), lambda b: (b, 0)),
            wide,
            wide,
            mix,
            pl.BlockSpec((heads, d, 2 * d), lambda b: (0, 0, 0)),
        ],
        out_shape=[
            shape((count, width), BF),
            shape((count, width), BF),
            shape((count, 2 * width), F32),
            shape((count, width), BF),
            shape((count, width), BF),
            shape((heads, count, SPAN), BF),
            shape((heads, d, 2 * d), BF),
        ],
        scratch_shapes=[
            pltpu.VMEM((heads, d, 2 * d), F32),
            pltpu.VMEM((SPAN.bit_length() - 1, SPAN, SPAN), BF),
        ],
        compiler_params=params(),
        cost_estimate=cost(21),
        name="delta_summary",
    )(*in_hbm(pre, pre, taps, cols, rows))


def delta_forward(pre, taps, k, w, u, cols, rows, entry, gain_full, heads):
    count, width = k.shape
    d, blocks = width // heads, count // SPAN
    rim = pre.shape[0] - count
    wide, c, r, state, mix, kept, gain = specs(blocks, heads, d, False)
    return pl.pallas_call(
        partial(forward_kernel, heads, d),
        grid=(blocks,),
        in_specs=[
            wide,
            before_block(blocks, rim, width, 0),
            pl.BlockSpec((4, width), lambda b: (0, 0)),
            wide,
            wide,
            wide,
            c,
            r,
            state,
            pl.BlockSpec((SPAN, width), lambda b: (b, 1)),
            gain,
        ],
        out_specs=[wide, wide, wide, wide, wide, kept],
        out_shape=[
            shape((count, width), BF),
            shape((count, width), F32),
            shape((count, width), BF),
            shape((count, width), F32),
            shape((count, width), BF),
            shape((blocks, heads, d, d), BF),
        ],
        scratch_shapes=[pltpu.VMEM((heads, d, d), F32)],
        compiler_params=params(),
        cost_estimate=cost(11),
        name="delta_forward",
    )(*in_hbm(pre, pre, taps, k, w, u, cols, rows, entry, pre, gain_full))


def delta_adjoint(q, k, w, cols, rows, dy, o, gate, gain_full, heads):
    count, width = k.shape
    d, blocks = width // heads, count // SPAN
    wide, c, r, state, mix, kept, gain = specs(blocks, heads, d, True)
    return pl.pallas_call(
        partial(adjoint_kernel, heads, d),
        grid=(blocks,),
        in_specs=[
            wide,
            wide,
            wide,
            c,
            r,
            wide,
            wide,
            pl.BlockSpec((SPAN, width), lambda b: (blocks - 1 - b, 1)),
            gain,
        ],
        out_specs=[wide, wide, gain, state],
        out_shape=[
            shape((count, width), BF),
            shape((count, width), BF),
            shape((1, d), F32),
            shape((heads, d, d), BF),
        ],
        scratch_shapes=[pltpu.VMEM((heads, d, d), F32)],
        compiler_params=params(),
        cost_estimate=cost(11),
        name="delta_adjoint",
    )(*in_hbm(q, k, w, cols, rows, dy, o, gate, gain_full))


def delta_backward(part, q, k, v, w, u, a, e, kept_states, do, cols, rows, later, qz, qg_pre, qtaps, kvz, kv_pre, kvtaps, heads):
    count, width = k.shape
    d, blocks = width // heads, count // SPAN
    rim = kv_pre.shape[0] - count
    number = head_parts(heads)[part]
    part_at = (heads - number) // number if part else 0
    size = number * d

    def at(step):
        return blocks - 1 - jnp.minimum(step, blocks - 1)

    wide = pl.BlockSpec((SPAN, size), lambda b: (at(b), part_at))
    in_specs = [
        wide,
        wide,
        wide,
        wide,
        wide,
        pl.BlockSpec((number, SPAN, SPAN), lambda b: (part_at, at(b), 0)),
        wide,
        pl.BlockSpec((1, number, d, d), lambda b: (at(b), part_at, 0, 0)),
        wide,
        pl.BlockSpec((SPAN, 2 * heads), lambda b: (at(b), 0)),
        pl.BlockSpec((1, 2 * heads, SPAN), lambda b: (at(b), 0, 0)),
        pl.BlockSpec((number, d, d), lambda b: (part_at, 0, 0)),
        wide,
        wide,
        pl.BlockSpec((rim, size), lambda b: (count // rim, part_at)),
        pl.BlockSpec((4, size), lambda b: (0, part_at)),
        pl.BlockSpec((SPAN, 2 * size), lambda b: (at(b), part_at)),
        pl.BlockSpec((SPAN, 2 * size), lambda b: (at(b), part_at)),
        pl.BlockSpec((rim, 2 * size), lambda b: (count // rim, part_at)),
        pl.BlockSpec((4, 2 * size), lambda b: (0, part_at)),
    ]
    return pl.pallas_call(
        partial(backward_kernel, heads, part, d),
        grid=(blocks + 1,),
        in_specs=in_specs,
        out_specs=[
            pl.BlockSpec((SPAN, 3 * size), lambda b: (jnp.where(b < blocks, blocks - 1 - b, blocks), 0)),
            pl.BlockSpec((SPAN, d), lambda b: (at(b), 0)),
            pl.BlockSpec((4, 3 * size), lambda b: (0, 0)),
        ],
        out_shape=[
            shape((count + rim, 3 * size), BF),
            shape((count, d), F32),
            shape((4, 3 * size), F32),
        ],
        scratch_shapes=[pltpu.VMEM((number, d, d), F32), pltpu.VMEM((3, rim, 3 * size), F32)],
        compiler_params=params(),
        cost_estimate=cost(8 + 2 * number),
        name="delta_backward",
    )(*in_hbm(q, k, v, w, u, a, e, kept_states, do, cols, rows, later, qz, qg_pre, qg_pre, qtaps, kvz, kv_pre, kv_pre, kvtaps))


def feed_kernel(
    n_ref, e_ref, mid_ref, g_ref, u_ref, d_ref, gb_ref, ub_ref, db_ref,
    f_ref, pair_ref, out_ref, dn_ref, total, held,
):
    step = pl.program_id(0)
    last = pl.num_programs(0) - 1
    wide = g_ref.shape[1]

    @pl.when(step == 0)
    def _():
        dn_ref[...] = jnp.zeros_like(dn_ref)
        total[...] = mid_ref[...]

    slot, other = step % 2, 1 - step % 2

    def first(i):
        gate = nn(n_ref[...], g_ref[...])
        yield True
        up = nn(n_ref[...], u_ref[...])
        yield True
        df = nt(e_ref[...], d_ref[...])
        yield True
        sig = sigmoid(gate)
        act = gate * sig
        f = (act * up).astype(BF)
        dgate = (df * up * (sig * (1.0 + gate * (1.0 - sig)))).astype(BF)
        dup = (df * act).astype(BF)
        f_ref[...] = f
        pair_ref[0] = dgate
        pair_ref[1] = dup
        held[slot, :, 0:wide] = f
        held[slot, :, wide : 2 * wide] = dgate
        held[slot, :, 2 * wide :] = dup
        yield True

    def second(i):
        total[...] += nn(held[other, :, 0:wide], db_ref[...])
        yield True
        both_w = jnp.concatenate([gb_ref[...], ub_ref[...]], axis=1)
        dn_ref[...] += nt(held[other, :, wide:], both_w)
        yield True

    def both(i):
        running = [first(i), second(i)]
        while running:
            running = [one for one in running if next(one, False)]
            yield True

    @pl.when(step == 0)
    def _():
        in_turn(first, 1, 1)

    @pl.when(jnp.logical_and(step > 0, step < last))
    def _():
        in_turn(both, 1, 1)

    @pl.when(step == last)
    def _():
        in_turn(second, 1, 1)
        out_ref[...] = total[...].astype(BF)


def feed_forward(normed, cotangent, middle, pair, down):
    count, width = normed.shape
    hidden = down.shape[0]
    wide = 2 * 128
    blocks = hidden // wide
    whole = pl.BlockSpec((count, width), lambda i: (0, 0))
    now = lambda i: jnp.minimum(i, blocks - 1)
    past = lambda i: jnp.maximum(i - 1, 0)
    weights = []
    for at in (now, past):
        weights += [
            pl.BlockSpec((width, wide), lambda i, at=at: (0, at(i))),
            pl.BlockSpec((width, wide), lambda i, at=at: (0, blocks + at(i))),
            pl.BlockSpec((wide, width), lambda i, at=at: (at(i), 0)),
        ]
    return pl.pallas_call(
        feed_kernel,
        grid=(blocks + 1,),
        in_specs=[whole, whole, whole] + weights,
        out_specs=[
            pl.BlockSpec((count, wide), lambda i: (0, now(i))),
            pl.BlockSpec((2, count, wide), lambda i: (0, 0, now(i))),
            whole,
            whole,
        ],
        out_shape=[
            shape((count, hidden), BF),
            shape((2, count, hidden), BF),
            shape((count, width), BF),
            shape((count, width), F32),
        ],
        scratch_shapes=[pltpu.VMEM((count, width), F32), pltpu.VMEM((2, count, 3 * wide), BF)],
        compiler_params=pltpu.CompilerParams(
            dimension_semantics=("arbitrary",), vmem_limit_bytes=40 * 1024 * 1024
        ),
        cost_estimate=cost(25),
        name="feed_forward",
    )(*in_hbm(normed, cotangent, middle, pair, pair, down, pair, pair, down))


def scan_states(x):
    peers, d, width = x.shape
    return pl.pallas_call(
        partial(prefix_kernel, peers),
        out_shape=shape((peers, d, width - d), BF),
        cost_estimate=cost(3),
        name="state_prefix",
    )(x)


def scan_grads(x, g):
    peers, d, width = g.shape
    return pl.pallas_call(
        partial(suffix_kernel, peers),
        out_shape=shape((peers, d, width), BF),
        cost_estimate=cost(3),
        name="state_suffix",
    )(x, g)


def hold(value, *after):
    return lax.optimization_barrier((value, after))[0]


class Place:
    def __init__(self):
        self.nf, self.nr = lax.axis_size("fsdp"), lax.axis_size("rep")
        self.ny = self.nf // 4
        self.nx = self.nr // 2
        self.f, self.r = lax.axis_index("fsdp"), lax.axis_index("rep")
        z = self.f // self.ny
        self.mine = {"v": z // 2, "w": z % 2, "y": self.f % self.ny, "x": self.r // 2, "c": self.r % 2}
        self.number = {"v": 2, "w": 2, "u": 2, "y": self.ny, "x": self.nx, "c": 2}
        self.stride = {"v": 2 * self.ny, "w": self.ny, "y": 1, "x": 2, "c": 1}

    def send(self, value, way, steps=1):
        if way == "u":
            return lax.ppermute(value, "fsdp", [(i, i ^ 3 * self.ny) for i in range(self.nf)])
        axis = "rep" if way in "xc" else "fsdp"
        total = self.nr if way in "xc" else self.nf
        number, stride = self.number[way], self.stride[way]
        pairs = []
        for i in range(total):
            at = i // stride % number
            pairs.append((i, i + ((at + steps) % number - at) * stride))
        return lax.ppermute(value, axis, pairs)


def place_kernel(count, rows, each, by_rows, widths, offs_ref, own_ref, *refs):
    stacks, outs, sems = refs[: len(count)], refs[len(count) : -1], refs[-1]
    copies = []

    def put(src, row, height, column, out):
        copy = pltpu.make_async_copy(src, out.at[pl.ds(row, height), column], sems.at[len(copies)])
        copy.start()
        copies.append(copy)

    starts = [sum(widths[:i]) for i in range(len(widths))]
    top = pl.multiple_of(offs_ref[0], rows)
    for start, width, out in zip(starts, widths, outs):
        put(own_ref.at[:, pl.ds(start, width)], top, rows, pl.ds(0, width), out)
    at = 1
    for stack, number in zip(stacks, count):
        for j in range(number):
            row = pl.multiple_of(offs_ref[at], each if by_rows else rows)
            if by_rows:
                for start, width, out in zip(starts, widths, outs):
                    put(stack.at[j, :, pl.ds(start, width)], row, each, pl.ds(0, width), out)
                at += 1
            else:
                column = pl.multiple_of(offs_ref[at + 1], each)
                put(stack.at[j], row, rows, pl.ds(column, each), outs[0])
                at += 2
    for copy in copies:
        copy.wait()


class Gather:
    def __init__(self, here, shard, widths, deep, by_rows=True):
        self.here, self.shard, self.widths, self.deep, self.by_rows = here, shard, widths, deep, by_rows
        rows, total = shard.shape
        parts = here.nr if deep else 2
        extent = rows if by_rows else total
        self.each = extent // parts
        self.plain = bool(extent % parts or self.each % (32 if by_rows else 128) or rows % 32)
        self.plain = self.plain or here.ny != 2 or here.nx != 2
        self.have = {}
        if self.plain:
            return
        part = here.r if deep else here.mine["c"]
        self.have[""] = lax.dynamic_slice_in_dim(shard, part * self.each, self.each, 0 if by_rows else 1)

    def got(self, *names):
        return [] if self.plain else [self.have[name] for name in names]

    def move(self, *names, after=()):
        if not self.plain:
            for name in names:
                self.have[name] = self.here.send(hold(self.have[name[:-1]], *after), name[-1])

    def pile(self):
        if not self.plain:
            last = "u" if "u" in self.have else "vw"
            self.have["z"] = jnp.stack([self.have[name] for name in ("", "w", "v", last)])

    def place(self):
        here, shard, widths = self.here, self.shard, self.widths
        rows, each = shard.shape[0], self.each
        if self.plain:
            whole = lax.all_gather(shard, "fsdp", axis=0, tiled=True)
            starts = [sum(widths[:i]) for i in range(len(widths))]
            return [whole[:, s : s + w] for s, w in zip(starts, widths)]
        mine = here.mine
        offsets = [here.f * rows]
        names = [name for name in self.have if name.startswith("z")]
        for name in names:
            x, c, y = ((mine[way] + (way in name)) % 2 for way in "xcy")
            inside = (x * 2 + c if self.deep else c) * each
            for j in range(4):
                v = (mine["v"] + j // 2) % 2
                w = (mine["w"] + j % 2) % 2
                source = (v * 2 + w) * here.ny + y
                offsets += [source * rows + inside] if self.by_rows else [source * rows, inside]
        offsets = jnp.stack(offsets).astype(jnp.int32)
        stacks = [self.have[name] for name in names]
        count = [4] * len(stacks)
        any_space = pl.BlockSpec(memory_space=pl.ANY)
        size = here.nf * rows
        return pl.pallas_call(
            partial(place_kernel, count, rows, each, self.by_rows, widths),
            grid_spec=pltpu.PrefetchScalarGridSpec(
                num_scalar_prefetch=1,
                grid=(1,),
                in_specs=[any_space] * (1 + len(stacks)),
                out_specs=[pl.BlockSpec((size, w), lambda i, o: (0, 0)) for w in widths],
                scratch_shapes=[pltpu.SemaphoreType.DMA(((1 + sum(count)) * len(widths),))],
            ),
            out_shape=[jax.ShapeDtypeStruct((size, w), shard.dtype) for w in widths],
            compiler_params=pltpu.CompilerParams(
                vmem_limit_bytes=2 * size * sum(widths) * 2 + (1 << 20)
            ),
            cost_estimate=cost(6),
            name="place_weights",
        )(offsets, shard, *stacks)


class Reduce:
    def __init__(self, here):
        self.here = here
        self.split = False

    def swap(self, away):
        self.away = away.astype(BF)
        self.came = self.here.send(self.away, "c")

    def take(self, part):
        self.begin(part + self.came.astype(F32))

    def begin(self, part):
        part = part.astype(BF)
        here = self.here
        rows = part.shape[0] // here.nf
        self.part = part.reshape(2, 2, here.ny, rows, part.shape[1])
        self.axes = ["v", "w", "y"]

    def go(self, way, *after):
        here = self.here
        part = hold(self.part, *after)
        number, mine = here.number[way], here.mine[way]
        if way in "xc" and not self.axes:
            self.total = part.astype(F32)
            self.outs = [part] * (number - 1)
        else:
            if way == "x":
                axis = len(self.axes)
                shape = part.shape
                part = part.reshape(
                    shape[:axis] + (number, shape[axis] // number) + shape[axis + 1 :]
                )
                self.split = True
            else:
                axis = self.axes.index(way)
                self.axes.pop(axis)
            self.total = lax.dynamic_index_in_dim(part, mine, axis, keepdims=False).astype(F32)
            self.outs = [
                lax.dynamic_index_in_dim(part, (mine + s) % number, axis, keepdims=False)
                for s in range(1, number)
            ]
        self.got = [here.send(out, way, s) for s, out in zip(range(1, number), self.outs)]

    def begin_x(self, part, *after):
        self.part, self.axes = part, []
        self.go("x", *after)

    def two(self, at):
        first, second = Reduce(self.here), Reduce(self.here)
        for one, cut in ((first, slice(0, at)), (second, slice(at, None))):
            one.part, one.axes = self.part[..., cut], list(self.axes)
        return first, second

    def join(self, first, second):
        self.part = jnp.concatenate([first.part, second.part], axis=-1)
        self.axes, self.split = list(first.axes), True

    def both(self):
        self.total = self.part.astype(F32)
        self.got = [self.here.send(self.part, "c")]

    def end(self):
        total = self.total
        for came in self.got:
            total = total + came.astype(F32)
        self.part = total.astype(BF)

    def step(self, way, *after):
        self.go(way, *after)
        self.end()

    def rows(self):
        if self.split:
            self.part = join_way(self.here, self.part, "x", 0)

    def other(self):
        return self.here.send(self.part, "c")


def meet(value, *sums):
    value, came = lax.optimization_barrier((value, [one.got for one in sums]))
    for one, got in zip(sums, came):
        one.got = got
        one.end()
    return value


def join_way(here, array, way, axis):
    number, mine = here.number[way], here.mine[way]
    got = [array] + [here.send(array, way, s) for s in range(1, number)]
    if number == 2:
        ahead = jnp.concatenate(got, axis=axis)
        behind = jnp.concatenate(got[::-1], axis=axis)
        return jnp.where(mine == 0, ahead, behind)
    stack = jnp.stack(got)
    order = (mine - jnp.arange(number)) % number
    stack = jnp.take(stack, order, axis=0)
    return jnp.concatenate([stack[i] for i in range(number)], axis=axis)


def gather_apart(here, shard):
    rows = shard.shape[0] // here.nr
    piece = lax.dynamic_slice_in_dim(shard, here.r * rows, rows, 0)
    return lax.all_gather(piece, ("fsdp", "rep"), axis=0, tiled=True)


def scatter_owners(array):
    return lax.psum_scatter(array, "fsdp", scatter_dimension=0, tiled=True)


def sum_x(here, array, *after):
    array = hold(array, *after)
    total = array.astype(F32)
    for s in range(1, here.nx):
        total = total + here.send(array, "x", s).astype(F32)
    return total.astype(BF)


def contract(left, right, left_dim, right_dim):
    return lax.dot_general(
        left, right, (((left_dim,), (right_dim,)), ((), ())), preferred_element_type=F32
    )


def rms_norm(values, gain):
    return values * lax.rsqrt(jnp.mean(values * values, axis=-1, keepdims=True) + EPSILON) * gain


def kv_order(array):
    eighth = array.shape[1] // 24
    starts, sizes = (8, 16, 14, 22), (6, 6, 2, 2)
    return [array[:, i * eighth : (i + n) * eighth] for i, n in zip(starts, sizes)]


def from_behind(value, steps):
    count = lax.axis_size("fsdp")
    first, last = (max(0, -steps), min(count, count - steps))
    return lax.ppermute(value, "fsdp", [(source, source + steps) for source in range(first, last)])


def to_owners(parts, fanout):
    heads, d, width = parts.shape
    cut = parts.reshape(heads, d, fanout, width // fanout)
    return jnp.swapaxes(cut, 1, 2).reshape(heads * fanout, d, width // fanout)


def to_heads(parts, fanout):
    owners, d, width = parts.shape
    cut = parts.reshape(owners // fanout, fanout, d, width)
    return jnp.swapaxes(cut, 1, 2).reshape(owners // fanout, d, width * fanout)


def swap(value):
    return lax.all_to_all(value, "fsdp", 0, 0, tiled=True)


def by_core(here, for_zero, for_one):
    return jnp.where(here.mine["c"] == 0, for_zero, for_one)


def on_device(
    hidden_in,
    seg_ids,
    attn_gain,
    qkv_weight,
    beta_weight,
    gate_weight,
    conv_taps,
    out_gain,
    out_weight,
    ffn_gain,
    ffn_gate,
    ffn_up,
    ffn_down,
    cotangent,
):
    here = Place()
    row_count, width = hidden_in.shape
    heads = beta_weight.shape[1]
    head_dim = width // heads
    blocks = row_count // SPAN
    rim = 8
    lanes = 128
    hidden_units = ffn_gate.shape[1]

    numbers = seg_ids + 1

    small = [attn_gain, out_gain, ffn_gain, conv_taps]
    shard_rows = qkv_weight.shape[0]
    flat = jnp.concatenate([a.reshape(-1) for a in small])
    columns = -(-flat.size // shard_rows)
    flat = jnp.pad(flat, (0, columns * shard_rows - flat.size)).reshape(shard_rows, columns)
    extra = jnp.concatenate(
        [beta_weight, flat, jnp.zeros((shard_rows, lanes - heads - columns), BF)], axis=1
    )
    first = Gather(
        here,
        jnp.concatenate(kv_order(qkv_weight) + [extra], axis=1),
        [2 * width, lanes],
        True,
    )
    second = Gather(
        here,
        jnp.concatenate([qkv_weight[:, :width], gate_weight, out_weight], axis=1),
        [2 * width, width],
        True,
    )
    rim_rows = from_behind(hidden_in[row_count - rim :], 1)
    rim_ids = from_behind(numbers[row_count - rim :], 1)
    pair_full = gather_apart(here, jnp.concatenate([ffn_gate, ffn_up], axis=1))
    first.move("v", "w")
    first.move("vw")
    first.pile()
    if not first.plain:
        first.have["z"], rim_rows, rim_ids = lax.optimization_barrier((first.have["z"], rim_rows, rim_ids))
    first.move("zy", "zx")
    first.move("zc")
    second.move("v", "w", after=first.got("z"))
    first.move("zyx", after=first.got("zx", "zc"))
    first.move("zyc", "zxc")
    first.move("zyxc", after=first.got("zyc", "zxc"))
    kv_full, extra_full = first.place()

    small_full = extra_full[:, heads : heads + columns].reshape(here.nf, -1)
    cuts, at = [], 0
    for array in small:
        cuts.append(small_full[:, at : at + array.size].astype(F32))
        at += array.size
    attn_scale = cuts[0].reshape(-1)
    outgain_scale = cuts[1].reshape(1, -1)
    ffngain_scale = cuts[2].reshape(-1)
    taps_count = conv_taps.shape[0]
    taps_scale = jnp.swapaxes(cuts[3].reshape(here.nf, taps_count, -1), 0, 1).reshape(taps_count, -1)
    query_taps = taps_scale[:, :width]
    kv_taps = jnp.concatenate(kv_order(taps_scale), axis=1)
    residual = hidden_in.astype(F32)
    extended_in = jnp.concatenate([hidden_in, rim_rows]).astype(F32)
    normed_ext = rms_norm(extended_in, attn_scale).astype(BF)
    normed_low = normed_ext[:row_count]
    kv_pre = jnp.dot(normed_ext, kv_full, preferred_element_type=F32)
    second.move("vw", after=[kv_full])
    second.pile()
    kv_pre = hold(kv_pre, second.got("z"))
    second.move("zy", "zx", after=[kv_pre])
    beta_pre = jnp.dot(normed_low, extra_full, preferred_element_type=F32)[:, :heads]
    rates = jax.nn.sigmoid(beta_pre)
    ids = jnp.concatenate([rim_ids, numbers]).astype(F32)
    own_ids = numbers.astype(F32)
    before = ids[rim - 1 : rim - 1 + row_count : SPAN]
    cols = jnp.concatenate(
        [rates, own_ids[:, None]]
        + [(ids[rim - j : rim - j + row_count] == own_ids).astype(F32)[:, None] for j in (1, 2, 3)]
        + [jnp.zeros((row_count, heads - 4), F32)],
        1,
    )
    rows = jnp.concatenate(
        [
            jnp.swapaxes(rates.reshape(blocks, SPAN, heads), 1, 2),
            own_ids.reshape(blocks, 1, SPAN),
            jnp.broadcast_to(before[:, None, None], (blocks, 1, SPAN)),
            jnp.zeros((blocks, heads - 2, SPAN), F32),
        ],
        1,
    )
    key_low, value_low, kv_mixed, w, u, a, moves = delta_summary(kv_pre, kv_taps, cols, rows, heads)
    moves = hold(moves, second.got("zy", "zx"))
    down_full = gather_apart(here, hold(ffn_down, pair_full, moves))
    second.move("zyx", after=[moves] + second.got("zx"))
    second.move("zc", "zyc", "zxc", after=[moves])
    fanout = here.nf // heads
    if fanout > 1:
        moves = jnp.concatenate(
            [
                to_owners(moves[:, :, :head_dim], fanout),
                jnp.repeat(moves[:, :, head_dim:], fanout, axis=0),
            ],
            axis=2,
        )
    owned = swap(moves)
    second.move("zyxc", after=[owned])
    qg_full, outw_full = second.place()
    qg_pre = jnp.dot(normed_ext, qg_full, preferred_element_type=F32)
    entry = swap(scan_states(owned))
    if fanout > 1:
        entry = to_heads(entry, fanout)
    query_low, q_mixed, gated_low, attn_heads, fresh, kept = delta_forward(
        qg_pre, query_taps, key_low, w, u, cols, rows, entry, outgain_scale, heads
    )
    middle = residual + jnp.dot(gated_low, outw_full, preferred_element_type=F32)
    normed_two, norm_two_back = jax.vjp(partial(rms_norm, gain=ffngain_scale), middle)
    normed_two_low = normed_two.astype(BF)
    hidden_low, pair_low, output, normed_two_grad = feed_forward(
        normed_two_low, cotangent, middle, pair_full, down_full
    )

    c = here.mine["c"]

    def shares(array, start, size):
        half = size // 2
        cut = [lax.dynamic_slice_in_dim(array, start + at * half, half, 1) for at in (1 - c, c)]
        return cut

    theirs, ours = shares(cotangent, 0, width)
    down_sum = Reduce(here)
    down_sum.swap(contract(hidden_low, theirs, 0, 0))
    theirs, ours = [lax.dynamic_index_in_dim(pair_low, at, 0, keepdims=False) for at in (1 - c, c)]
    pair_sum = Reduce(here)
    pair_sum.swap(contract(normed_two_low, theirs, 0, 0))
    down_theirs, down_ours = shares(cotangent, 0, width)
    down_sum = Reduce(here)
    down_sum.swap(contract(hidden_low, down_theirs, 0, 0))
    (middle_back,) = norm_two_back(normed_two_grad)
    middle_grad = cotangent.astype(F32) + middle_back
    middle_low = middle_grad.astype(BF)
    gated_grad = contract(middle_low, outw_full, 1, 1)
    pair_half = (contract(normed_two_low, ours, 0, 0) + pair_sum.came.astype(F32)).astype(BF)
    pair_apart = scatter_owners(pair_half)
    down_half = (contract(hidden_low, down_ours, 0, 0) + down_sum.came.astype(F32)).astype(BF)
    down_apart = scatter_owners(down_half)
    gated_grad = hold(gated_grad, down_half, pair_half)
    heads_grad, gatepre_low, outgain_grad, local_later = delta_adjoint(
        query_low, key_low, w, cols, rows, gated_grad, attn_heads, qg_pre, outgain_scale, heads
    )
    if fanout > 1:
        local_later = to_owners(local_later, fanout)
    came_later = swap(local_later)

    summed_later = scan_grads(owned, came_later)
    later = swap(summed_later)
    if fanout > 1:
        later = to_heads(later, fanout)
    middle_held, gatepre_held = hold((middle_low, gatepre_low), summed_later)
    out_grad = contract(gated_low, middle_held, 0, 0)
    gate_grad = contract(normed_low, gatepre_held, 0, 0)
    other_sum = Reduce(here)
    other_sum.swap(by_core(here, gate_grad, out_grad))
    other_sum.take(by_core(here, out_grad, gate_grad))
    later = hold(later, other_sum.part)
    other_x, other_y = other_sum.two(width // 2)
    other_x.go("x", later)
    other_y.go("y", later)
    later = hold(later, *other_x.outs, *other_y.outs)
    state = (query_low, key_low, value_low, w, u, a, fresh, kept, heads_grad, cols, rows)
    mixed_a, beta_a, taps_a = delta_backward(
        0, *state, later, q_mixed, qg_pre, query_taps, kv_mixed, kv_pre, kv_taps, heads
    )
    mixed_a = meet(mixed_a, other_x, other_y)
    other_x.go("y")
    other_y.go("x")
    a_sum = Reduce(here)
    cut = [number * head_dim for number in head_parts(heads)]
    theirs, ours = shares(mixed_a, 0, 3 * cut[0])
    a_sum.swap(contract(normed_ext, theirs, 0, 0))
    a_sum.take(contract(normed_ext, ours, 0, 0))
    later = meet(hold(later, a_sum.part), other_x, other_y)
    other_sum.join(other_x, other_y)
    a_x, a_y = a_sum.two((a_sum.part.shape[-1] // lanes + 1) // 2 * lanes)
    a_x.go("x", later)
    a_y.go("y", later)
    other_sum.go("w", later)
    later = hold(later, *a_x.outs, *a_y.outs, *other_sum.outs)
    mixed_b, beta_b, taps_b = delta_backward(
        1, *state, later, q_mixed, qg_pre, query_taps, kv_mixed, kv_pre, kv_taps, heads
    )
    mixed_b = hold(meet(mixed_b, other_sum, a_x, a_y), pair_apart)
    def by_kind(first_heads, other_heads):
        pieces = []
        for i in range(3):
            for array, wide in zip((first_heads, other_heads), cut):
                pieces.append(array[:, i * wide : (i + 1) * wide])
        return jnp.concatenate(pieces, axis=1)

    betapre_low = (beta_a + beta_b).astype(BF)
    taps_grad = by_kind(taps_a, taps_b)
    parts = (
        outgain_grad.reshape(here.nf, -1),
        jnp.swapaxes(taps_grad.reshape(taps_count, here.nf, -1), 0, 1).reshape(here.nf, -1),
    )
    flat = jnp.concatenate(parts, axis=1)
    flat = jnp.pad(flat, ((0, 0), (0, columns * shard_rows - flat.shape[1])))
    extra = jnp.pad(flat.reshape(width, columns), ((0, 0), (heads, lanes - heads - columns)))
    small_sum = Reduce(here)
    small_sum.begin(contract(normed_low, hold(betapre_low, mixed_b), 0, 0) + extra)
    small_sum.both()
    b_sum = Reduce(here)
    theirs, ours = shares(mixed_b, 0, 3 * cut[1])
    b_sum.swap(contract(normed_ext, theirs, 0, 0))
    b_sum.take(contract(normed_ext, ours, 0, 0))
    small_sum.end()
    mixed_b = hold(mixed_b, b_sum.part, small_sum.part)
    b_sum.go("x")
    a_x.go("y", mixed_b)
    a_y.go("x", mixed_b)
    small_sum.go("x")
    wide_grad = (
        contract(mixed_a[:, cut[0] :], kv_full[:, : 2 * cut[0]], 1, 1)
        + contract(mixed_b[:, cut[1] :], kv_full[:, 2 * cut[0] :], 1, 1)
        + contract(mixed_a[:, : cut[0]], qg_full[:, : cut[0]], 1, 1)
        + contract(mixed_b[:, : cut[1]], qg_full[:, cut[0] : width], 1, 1)
    )
    rim_grad = from_behind(wide_grad[row_count:].astype(BF), -1).astype(F32)
    normed_grad = (
        wide_grad[:row_count]
        + jnp.pad(rim_grad, ((row_count - rim, 0), (0, 0)))
        + contract(betapre_low, extra_full, 1, 1)
        + contract(gatepre_low, qg_full[:, width:], 1, 1)
    )
    normed_grad = meet(normed_grad, b_sum, a_x, a_y, small_sum)
    other_sum.go("v", normed_grad)
    a_sum.join(a_x, a_y)
    b_sum.go("y")
    small_sum.go("y")
    pair_sum.begin_x(pair_apart, normed_grad)
    a_sum.go("w")
    (input_back,) = jax.vjp(partial(rms_norm, gain=attn_scale), residual)[1](normed_grad)
    input_grad = meet(
        (middle_grad + input_back).astype(BF), b_sum, a_sum, other_sum, small_sum, pair_sum
    )
    b_sum.go("w", input_grad)
    a_sum.go("v", input_grad)
    small_sum.go("w", input_grad)
    for one in (b_sum, a_sum, small_sum):
        one.end()
    b_sum.go("v", a_sum.part)
    small_sum.go("v", a_sum.part)
    pair_part = hold(pair_sum.part, a_sum.part)
    other = here.send(pair_part, "c")
    held = meet(a_sum.part, b_sum, small_sum)
    both = Reduce(here)
    both.part = jnp.concatenate([b_sum.part, held, other_sum.part, small_sum.part], axis=1)
    both.split = True
    both.rows()
    down_sum.begin_x(down_apart, held)
    down_sum.end()
    down_total = join_way(here, down_sum.part, "c", 1).astype(F32)
    hidgate_total = by_core(here, pair_part, other).astype(F32)
    hidup_total = by_core(here, other, pair_part).astype(F32)
    whole = both.other()
    ends = [0]
    for one in (b_sum, a_sum, other_sum, small_sum):
        ends.append(ends[-1] + one.part.shape[1])

    def joined(start, end):
        mine, theirs = both.part[:, start:end], whole[:, start:end]
        return by_core(here, mine, theirs), by_core(here, theirs, mine)

    b_both, a_both, other_both = [joined(*pair) for pair in zip(ends[:3], ends[1:4])]
    outproj_total, gate_total = [part.astype(F32) for part in other_both]
    qkv_total = by_kind(jnp.concatenate(a_both, axis=1), jnp.concatenate(b_both, axis=1)).astype(F32)
    extra = both.part[:, ends[3] :].astype(F32)
    beta_total = extra[:, :heads]

    def gain_grad(gain, pairs):
        total = sum(jnp.sum(weight.astype(F32) * grad, axis=1) for weight, grad in pairs)
        return total / gain.astype(F32)

    attngain_total = gain_grad(
        attn_gain, ((qkv_weight, qkv_total), (beta_weight, beta_total), (gate_weight, gate_total))
    )
    ffngain_total = gain_grad(ffn_gain, ((ffn_gate, hidgate_total), (ffn_up, hidup_total)))
    flat = extra[:, heads : heads + columns].reshape(-1)
    cut, at = [], 0
    for part in parts:
        cut.append(flat[at : at + part.shape[1]])
        at += part.shape[1]
    return (
        output,
        input_grad,
        attngain_total,
        qkv_total,
        beta_total,
        gate_total,
        cut[1].reshape(conv_taps.shape),
        cut[0],
        outproj_total,
        ffngain_total,
        hidgate_total,
        hidup_total,
        down_total,
    )


def solution(mesh):
    placed = (
        P(("rep", "fsdp"), None),
        P(("rep", "fsdp")),
        P("fsdp"),
        P("fsdp", None),
        P("fsdp", None),
        P("fsdp", None),
        P(None, "fsdp"),
        P("fsdp"),
        P("fsdp", None),
        P("fsdp"),
        P("fsdp", None),
        P("fsdp", None),
        P("fsdp", None),
        P(("rep", "fsdp"), None),
    )
    return jax.shard_map(
        on_device,
        mesh=mesh,
        in_specs=placed,
        out_specs=(
            P(("rep", "fsdp"), None),
            P(("rep", "fsdp"), None),
            P("fsdp"),
            P("fsdp", None),
            P("fsdp", None),
            P("fsdp", None),
            P(None, "fsdp"),
            P("fsdp"),
            P("fsdp", None),
            P("fsdp"),
            P("fsdp", None),
            P("fsdp", None),
            P("fsdp", None),
        ),
        check_vma=False,
    )
```

```python
from functools import partial

import jax
import jax.numpy as jnp
from jax import lax
from jax.experimental import pallas as pl
from jax.experimental.pallas import tpu as pltpu
from jax.sharding import PartitionSpec as P

SPAN = 64
TOGETHER = 8
EPSILON = 1e-06
BF = jnp.bfloat16
F32 = jnp.float32


def nn(a, b):
    return lax.dot_general(a, b, (((1,), (0,)), ((), ())), preferred_element_type=F32)


def nt(a, b):
    return lax.dot_general(a, b, (((1,), (1,)), ((), ())), preferred_element_type=F32)


def tn(a, b):
    return lax.dot_general(a, b, (((0,), (0,)), ((), ())), preferred_element_type=F32)


def in_turn(body, count, together):
    for start in range(0, count, together):
        running = [body(h) for h in range(start, min(start + together, count))]
        while running:
            running = [one for one in running if next(one, False)]


def block_masks(cols_ref, rows_ref, heads):
    n = SPAN
    row = lax.broadcasted_iota(jnp.int32, (n, n), 0)
    col = lax.broadcasted_iota(jnp.int32, (n, n), 1)
    ids = cols_ref[:, heads : heads + 1]
    ids_row = rows_ref[0, heads : heads + 1, :]
    before = rows_ref[0, heads + 1 : heads + 2, :]
    end = ids_row[:, n - 1 : n]
    same = ids == ids_row
    first = (ids == before[:, :1]).astype(F32)
    last = (ids == end).astype(F32)
    keep = (end == before[:, :1]).astype(F32)
    return row, col, same, first, last, keep


def sigmoid(z):
    return 0.5 * jnp.tanh(0.5 * z) + 0.5


def shifted_rows(x, prev, masks):
    both = jnp.concatenate([prev, x], axis=0)
    lead = prev.shape[0]
    return [x] + [pltpu.roll(both, j, 0)[lead:] * masks[j - 1] for j in (1, 2, 3)]


def mix_rows(rows, taps):
    mixed = rows[0] * taps[0:1]
    for j in (1, 2, 3):
        mixed = mixed + rows[j] * taps[j : j + 1]
    return mixed


def lag_masks(cols_ref, heads):
    return [cols_ref[:, heads + j : heads + j + 1] for j in (1, 2, 3)]


def head_parts(heads):
    return heads - heads // 4, heads // 4


def kv_at(heads, d, h):
    first, other = head_parts(heads)
    number, start, inside = (first, 0, h) if h < first else (other, 2 * first, h - first)
    at = (start + inside) * d
    return slice(at, at + d), slice(at + number * d, at + number * d + d)


def summary_kernel(
    heads, d, pre_ref, prev_ref, taps_ref, cols_ref, rows_ref,
    k_ref, v_ref, z_ref, w_ref, u_ref, a_ref, x_ref, state, levels,
):
    n = SPAN
    block = pl.program_id(0)

    @pl.when(block == 0)
    def _():
        at = lax.broadcasted_iota(jnp.int32, (n, n), 0)
        to = lax.broadcasted_iota(jnp.int32, (n, n), 1)
        for i in range(levels.shape[0]):
            size = 1 << i
            level = jnp.logical_and(
                (at // (2 * size)) == (to // (2 * size)),
                jnp.logical_and(((at // size) & 1) == 1, ((to // size) & 1) == 0),
            )
            levels[i] = level.astype(F32).astype(BF)
        r = lax.broadcasted_iota(jnp.int32, (d, 2 * d), 0)
        c = lax.broadcasted_iota(jnp.int32, (d, 2 * d), 1)
        unit = (r + d == c).astype(F32)
        for h in range(heads):
            state[h] = unit

    row, col, same, first, last, keep = block_masks(cols_ref, rows_ref, heads)
    lower = jnp.logical_and(same, row > col)
    unit = (row == col).astype(F32).astype(BF)
    masks = lag_masks(cols_ref, heads)
    keys, mixing, inverse = ([None] * heads for i in range(3))
    def features(h):
        cut = slice(h * d, (h + 1) * d)
        at_k, at_v = kv_at(heads, d, h)
        z = mix_rows(shifted_rows(pre_ref[:, at_k], prev_ref[:, at_k], masks), taps_ref[:, at_k])
        z_ref[:, at_k] = z
        yield True
        act = z * sigmoid(z)
        root = lax.rsqrt(jnp.sum(act * act, axis=1, keepdims=True) + EPSILON)
        yield True
        keys[h] = (act * root).astype(BF)
        k_ref[:, cut] = keys[h]
        yield True
        z = mix_rows(shifted_rows(pre_ref[:, at_v], prev_ref[:, at_v], masks), taps_ref[:, at_v])
        z_ref[:, at_v] = z
        v_ref[:, cut] = (z * sigmoid(z)).astype(BF)
        m = jnp.where(lower, nt(keys[h], keys[h]) * cols_ref[:, h : h + 1], 0.0).astype(BF)
        yield True
        mixing[h] = m
        inverse[h] = unit - m * levels[0]

    in_turn(features, heads, TOGETHER)
    for i in range(1, levels.shape[0]):
        level = levels[i]
        inner = [nn(mixing[h] * level, inverse[h]).astype(BF) for h in range(heads)]
        for h in range(heads):
            inverse[h] = inverse[h] - nn(inverse[h], inner[h]).astype(BF) * level
    def advance(h):
        cut = slice(h * d, (h + 1) * d)
        a_ref[h] = inverse[h]
        scaled = (inverse[h].astype(F32) * rows_ref[0, h : h + 1, :]).astype(BF)
        yield True
        both = nn(scaled, jnp.concatenate([keys[h], v_ref[:, cut]], axis=1))
        yield True
        w = both[:, :d].astype(BF)
        u = both[:, d:].astype(BF)
        w_ref[:, cut] = w
        u_ref[:, cut] = u
        yield True
        held = state[h]
        moved = nn(w, held.astype(BF)) * first
        yield True
        fresh = (jnp.concatenate([u.astype(F32), jnp.zeros((n, d), F32)], axis=1) - moved).astype(BF)
        yield True
        key_last = keys[h] * last.astype(BF)
        yield True
        state[h] = keep * held + tn(key_last, fresh)

    in_turn(advance, heads, TOGETHER)

    @pl.when(block == pl.num_programs(0) - 1)
    def _():
        x_ref[...] = state[...].astype(BF)


def forward_kernel(
    heads, d, pre_ref, prev_ref, taps_ref, k_ref, w_ref, u_ref, cols_ref, rows_ref, s_ref, gate_ref, gain_ref,
    q_ref, z_ref, y_ref, o_ref, e_ref, kept_ref, state,
):
    n = SPAN
    block = pl.program_id(0)

    @pl.when(block == 0)
    def _():
        state[...] = s_ref[...].astype(F32)

    row, col, same, first, last, keep = block_masks(cols_ref, rows_ref, heads)
    visible = jnp.logical_and(same, row >= col)
    masks = lag_masks(cols_ref, heads)
    def one_head(h):
        cut = slice(h * d, (h + 1) * d)
        z = mix_rows(shifted_rows(pre_ref[:, cut], prev_ref[:, cut], masks), taps_ref[:, cut])
        z_ref[:, cut] = z
        q = (z * sigmoid(z) * d ** (-0.5)).astype(BF)
        q_ref[:, cut] = q
        yield True
        k, w = k_ref[:, cut], w_ref[:, cut]
        held = state[h]
        held_low = held.astype(BF)
        kept_ref[0, h] = held_low
        both = nn(jnp.concatenate([w, q], axis=0), held_low)
        yield True
        fresh = (u_ref[:, cut].astype(F32) - first * both[:n]).astype(BF)
        e_ref[:, cut] = fresh
        yield True
        scores = jnp.where(visible, nt(q, k), 0.0).astype(BF)
        yield True
        out = first * both[n:] + nn(scores, fresh)
        yield True
        key_last = k * last.astype(BF)
        state[h] = keep * held + tn(key_last, fresh)
        yield True
        o_ref[:, cut] = out
        yield True
        g = gate_ref[:, cut]
        root = lax.rsqrt(jnp.mean(out * out, axis=1, keepdims=True) + EPSILON)
        yield True
        y_ref[:, cut] = (out * root * gain_ref[...] * (g * sigmoid(g))).astype(BF)

    in_turn(one_head, heads, TOGETHER)


def adjoint_kernel(
    heads, d, q_ref, k_ref, w_ref, cols_ref, rows_ref, dy_ref, o_ref, gate_ref, gain_ref,
    do_ref, dgate_ref, dgain_ref, ds_ref, state,
):
    n = SPAN
    step = pl.program_id(0)

    @pl.when(step == 0)
    def _():
        state[...] = jnp.zeros_like(state)
        dgain_ref[...] = jnp.zeros_like(dgain_ref)

    row, col, same, first, last, keep = block_masks(cols_ref, rows_ref, heads)
    visible = jnp.logical_and(same, row >= col)
    first_low = first.astype(BF)
    gain = gain_ref[...]
    gain_sum = jnp.zeros((1, d), F32)
    def one_head(h):
        nonlocal gain_sum
        cut = slice(h * d, (h + 1) * d)
        q, k, w = q_ref[:, cut], k_ref[:, cut], w_ref[:, cut]
        o, g, dy = o_ref[:, cut], gate_ref[:, cut], dy_ref[:, cut]
        root = lax.rsqrt(jnp.mean(o * o, axis=1, keepdims=True) + EPSILON)
        yield True
        unit = o * root
        sig = sigmoid(g)
        m = g * sig
        t = dy * m
        gain_sum = gain_sum + jnp.sum(t * unit, axis=0, keepdims=True)
        tg = t * gain
        do = root * (tg - unit * jnp.mean(tg * unit, axis=1, keepdims=True))
        yield True
        dgate_ref[:, cut] = (dy * gain * unit * (sig * (1.0 + g * (1.0 - sig)))).astype(BF)
        do_low = do.astype(BF)
        do_ref[:, cut] = do_low
        yield True
        scores = jnp.where(visible, nt(q, k), 0.0).astype(BF)
        yield True
        later = state[h]
        de = last * nn(k, later.astype(BF)) + tn(scores, do_low)
        yield True
        left = jnp.concatenate([q * first_low, w * -first_low], axis=0)
        right = jnp.concatenate([do_low, de.astype(BF)], axis=0)
        state[h] = keep * later + tn(left, right)
        yield True

    in_turn(one_head, heads, TOGETHER)
    dgain_ref[...] += gain_sum

    @pl.when(step == pl.num_programs(0) - 1)
    def _():
        ds_ref[...] = state[...].astype(BF)


def backward_kernel(
    heads, part, d, q_ref, k_ref, v_ref, w_ref, u_ref, a_ref, e_ref, kept_ref, do_ref, cols_ref, rows_ref, s_ref,
    qz_ref, qpre_ref, qrim_ref, qtaps_ref, kvz_ref, kvpre_ref, kvrim_ref, kvtaps_ref,
    dpre_ref, dbeta_ref, dtaps_ref, state, carry,
):
    n = SPAN
    step = pl.program_id(0)
    number = head_parts(heads)[part]
    base = heads - number if part else 0

    @pl.when(step == 0)
    def _():
        state[...] = s_ref[...].astype(F32)
        carry[...] = jnp.zeros_like(carry)
        dtaps_ref[...] = jnp.zeros_like(dtaps_ref)

    @pl.when(step < pl.num_programs(0) - 1)
    def _():
        row, col, same, first, last, keep = block_masks(cols_ref, rows_ref, heads)
        visible = jnp.logical_and(same, row >= col)
        lower = jnp.logical_and(same, row > col)
        lane = lax.broadcasted_iota(jnp.int32, (n, d), 1)
        masks = lag_masks(cols_ref, heads)
        rate_grads = jnp.zeros((n, d), F32)

        first_low = first.astype(BF)

        def conv_back(dact, z, sig, pre, taps, at):
            dconv = dact * (sig * (1.0 + z * (1.0 - sig)))
            here = slice(at, at + d)
            dpre = dconv * taps[0:1]
            sums = [jnp.sum(dconv * pre, axis=0, keepdims=True)]
            for j in (1, 2, 3):
                masked = dconv * masks[j - 1]
                both = jnp.concatenate([masked, carry[j - 1, :, here]], axis=0)
                moved = pltpu.roll(both, both.shape[0] - j, 0)[:n]
                dpre = dpre + moved * taps[j : j + 1]
                sums.append(jnp.sum(moved * pre, axis=0, keepdims=True))
                carry[j - 1, :, here] = masked[:8]
            dtaps_ref[:, here] += jnp.concatenate(sums, axis=0)
            dpre_ref[:, here] = dpre.astype(BF)

        def one_head(h):
            nonlocal rate_grads
            cut = slice(h * d, (h + 1) * d)
            cut_v = slice((number + h) * d, (number + h + 1) * d)
            q, k, v, w, u = q_ref[:, cut], k_ref[:, cut], v_ref[:, cut], w_ref[:, cut], u_ref[:, cut]
            do, e, held = do_ref[:, cut], e_ref[:, cut], kept_ref[0, h]
            at = base + h
            rate = cols_ref[:, at : at + 1]
            later = state[h]
            later_low = later.astype(BF)
            scores = jnp.where(visible, nt(q, k), 0.0).astype(BF)
            yield True
            de = last * nn(k, later_low) + tn(scores, do)
            yield True
            de_low = de.astype(BF)
            dscores = jnp.where(visible, nt(do, e), 0.0).astype(BF)
            yield True
            both = nt(jnp.concatenate([do, de_low], axis=0), held)
            yield True
            dq = first * both[:n] + nn(dscores, k)
            dw = -first * both[n:]
            dk = tn(dscores, q) + last * nt(e, later_low)
            yield True
            pg = tn(a_ref[h], jnp.concatenate([dw.astype(BF), de_low], axis=1))
            yield True
            p, g = pg[:, :d], pg[:, d:]
            dmix = jnp.where(lower, -nt(pg.astype(BF), jnp.concatenate([w, u], axis=1)), 0.0).astype(BF)
            yield True
            kf = k.astype(F32)
            drk = p + nn(dmix, k)
            dk = dk + tn(dmix, (kf * rate).astype(BF)) + rate * drk
            yield True
            dr = jnp.sum(drk * kf + g * v.astype(F32), axis=1, keepdims=True)
            rate_grads = jnp.where(lane == at, dr * rate * (1.0 - rate), rate_grads)
            left = jnp.concatenate([q * first_low, w * -first_low], axis=0)
            right = jnp.concatenate([do, de_low], axis=0)
            state[h] = keep * later + tn(left, right)
            yield True

            z = qz_ref[:, cut]
            conv_back(dq * d ** (-0.5), z, sigmoid(z), qpre_ref[:, cut], qtaps_ref[:, cut], h * d)
            yield True
            z = kvz_ref[:, cut]
            sig = sigmoid(z)
            act = z * sig
            root = lax.rsqrt(jnp.sum(act * act, axis=1, keepdims=True) + EPSILON)
            unit = act * root
            dact = root * (dk - unit * jnp.sum(unit * dk, axis=1, keepdims=True))
            conv_back(dact, z, sig, kvpre_ref[:, cut], kvtaps_ref[:, cut], (number + h) * d)
            yield True
            z = kvz_ref[:, cut_v]
            conv_back(
                rate * g, z, sigmoid(z), kvpre_ref[:, cut_v], kvtaps_ref[:, cut_v], (2 * number + h) * d
            )

        in_turn(one_head, number, TOGETHER)
        dbeta_ref[...] = rate_grads

    @pl.when(step == pl.num_programs(0) - 1)
    def _():
        wide = number * d
        for i, taps_ref, rim_ref, at in (
            (0, qtaps_ref, qrim_ref, 0),
            (1, kvtaps_ref, kvrim_ref, 0),
            (2, kvtaps_ref, kvrim_ref, wide),
        ):
            here, there = slice(i * wide, (i + 1) * wide), slice(at, at + wide)
            dpre = jnp.zeros((8, wide), F32)
            sums = [jnp.zeros((1, wide), F32)]
            for j in (1, 2, 3):
                held = carry[j - 1, :, here]
                moved = jnp.concatenate([jnp.zeros_like(held), held], axis=0)[j : 8 + j]
                dpre = dpre + moved * taps_ref[j : j + 1, there]
                sums.append(jnp.sum(moved * rim_ref[:, there], axis=0, keepdims=True))
            dtaps_ref[:, here] += jnp.concatenate(sums, axis=0)
            dpre_ref[0:8, here] = dpre.astype(BF)


def prefix_kernel(peers, x_ref, out_ref):
    cols = out_ref.shape[2]
    held = jnp.zeros(out_ref.shape[1:], F32)
    for i in range(peers):
        out_ref[i] = held.astype(BF)
        held = nn(x_ref[i, :, cols:], held.astype(BF)) + x_ref[i, :, :cols].astype(F32)


def suffix_kernel(peers, t_ref, g_ref, out_ref):
    held = jnp.zeros(out_ref.shape[1:], F32)
    cols = out_ref.shape[2]
    for i in reversed(range(peers)):
        out_ref[i] = held.astype(BF)
        held = tn(t_ref[i, :, cols:], held.astype(BF)) + g_ref[i].astype(F32)


VMEM_LIMIT = 16 * 1024 * 1024


def in_hbm(*arrays):
    return [pltpu.with_memory_space_constraint(a, pltpu.HBM) for a in arrays]


def params():
    return pltpu.CompilerParams(dimension_semantics=("arbitrary",), vmem_limit_bytes=VMEM_LIMIT)


def cost(microseconds):
    return pl.CostEstimate(
        flops=int(microseconds * 1e9), bytes_accessed=int(microseconds * 3e6), transcendentals=0
    )


def specs(blocks, heads, d, flip):
    at = (lambda b: blocks - 1 - b) if flip else (lambda b: b)
    wide = pl.BlockSpec((SPAN, heads * d), lambda b: (at(b), 0))
    cols = pl.BlockSpec((SPAN, 2 * heads), lambda b: (at(b), 0))
    rows = pl.BlockSpec((1, 2 * heads, SPAN), lambda b: (at(b), 0, 0))
    state = pl.BlockSpec((heads, d, d), lambda b: (0, 0, 0))
    mix = pl.BlockSpec((heads, SPAN, SPAN), lambda b: (0, at(b), 0))
    kept = pl.BlockSpec((1, heads, d, d), lambda b: (at(b), 0, 0, 0))
    gain = pl.BlockSpec((1, d), lambda b: (0, 0))
    return wide, cols, rows, state, mix, kept, gain


def shape(dims, kind):
    return pltpu.HBM(dims, kind)


def near(dims, kind):
    return jax.ShapeDtypeStruct(dims, kind)


def before_block(blocks, rim, size, column):
    def index(b):
        per = SPAN // rim
        return jnp.where(b == 0, blocks * per, b * per - 1), column

    return pl.BlockSpec((rim, size), index)


def delta_summary(pre, taps, cols, rows, heads):
    count, width = cols.shape[0], pre.shape[1] // 2
    d, blocks = width // heads, count // SPAN
    rim = pre.shape[0] - count
    wide, c, r, state, mix, kept, gain = specs(blocks, heads, d, False)
    return pl.pallas_call(
        partial(summary_kernel, heads, d),
        grid=(blocks,),
        in_specs=[
            pl.BlockSpec((SPAN, 2 * width), lambda b: (b, 0)),
            before_block(blocks, rim, 2 * width, 0),
            pl.BlockSpec((4, 2 * width), lambda b: (0, 0)),
            c,
            r,
        ],
        out_specs=[
            wide,
            wide,
            pl.BlockSpec((SPAN, 2 * width), lambda b: (b, 0)),
            wide,
            wide,
            mix,
            pl.BlockSpec((heads, d, 2 * d), lambda b: (0, 0, 0)),
        ],
        out_shape=[
            shape((count, width), BF),
            shape((count, width), BF),
            shape((count, 2 * width), F32),
            shape((count, width), BF),
            shape((count, width), BF),
            shape((heads, count, SPAN), BF),
            shape((heads, d, 2 * d), BF),
        ],
        scratch_shapes=[
            pltpu.VMEM((heads, d, 2 * d), F32),
            pltpu.VMEM((SPAN.bit_length() - 1, SPAN, SPAN), BF),
        ],
        compiler_params=params(),
        cost_estimate=cost(21),
        name="delta_summary",
    )(*in_hbm(pre, pre, taps, cols, rows))


def delta_forward(pre, taps, k, w, u, cols, rows, entry, gain_full, heads):
    count, width = k.shape
    d, blocks = width // heads, count // SPAN
    rim = pre.shape[0] - count
    wide, c, r, state, mix, kept, gain = specs(blocks, heads, d, False)
    return pl.pallas_call(
        partial(forward_kernel, heads, d),
        grid=(blocks,),
        in_specs=[
            wide,
            before_block(blocks, rim, width, 0),
            pl.BlockSpec((4, width), lambda b: (0, 0)),
            wide,
            wide,
            wide,
            c,
            r,
            state,
            pl.BlockSpec((SPAN, width), lambda b: (b, 1)),
            gain,
        ],
        out_specs=[wide, wide, wide, wide, wide, kept],
        out_shape=[
            shape((count, width), BF),
            shape((count, width), F32),
            shape((count, width), BF),
            shape((count, width), F32),
            shape((count, width), BF),
            shape((blocks, heads, d, d), BF),
        ],
        scratch_shapes=[pltpu.VMEM((heads, d, d), F32)],
        compiler_params=params(),
        cost_estimate=cost(11),
        name="delta_forward",
    )(*in_hbm(pre, pre, taps, k, w, u, cols, rows, entry, pre, gain_full))


def delta_adjoint(q, k, w, cols, rows, dy, o, gate, gain_full, heads):
    count, width = k.shape
    d, blocks = width // heads, count // SPAN
    wide, c, r, state, mix, kept, gain = specs(blocks, heads, d, True)
    return pl.pallas_call(
        partial(adjoint_kernel, heads, d),
        grid=(blocks,),
        in_specs=[
            wide,
            wide,
            wide,
            c,
            r,
            wide,
            wide,
            pl.BlockSpec((SPAN, width), lambda b: (blocks - 1 - b, 1)),
            gain,
        ],
        out_specs=[wide, wide, gain, state],
        out_shape=[
            shape((count, width), BF),
            shape((count, width), BF),
            shape((1, d), F32),
            shape((heads, d, d), BF),
        ],
        scratch_shapes=[pltpu.VMEM((heads, d, d), F32)],
        compiler_params=params(),
        cost_estimate=cost(11),
        name="delta_adjoint",
    )(*in_hbm(q, k, w, cols, rows, dy, o, gate, gain_full))


def delta_backward(part, q, k, v, w, u, a, e, kept_states, do, cols, rows, later, qz, qg_pre, qtaps, kvz, kv_pre, kvtaps, heads):
    count, width = k.shape
    d, blocks = width // heads, count // SPAN
    rim = kv_pre.shape[0] - count
    number = head_parts(heads)[part]
    part_at = (heads - number) // number if part else 0
    size = number * d

    def at(step):
        return blocks - 1 - jnp.minimum(step, blocks - 1)

    wide = pl.BlockSpec((SPAN, size), lambda b: (at(b), part_at))
    in_specs = [
        wide,
        wide,
        wide,
        wide,
        wide,
        pl.BlockSpec((number, SPAN, SPAN), lambda b: (part_at, at(b), 0)),
        wide,
        pl.BlockSpec((1, number, d, d), lambda b: (at(b), part_at, 0, 0)),
        wide,
        pl.BlockSpec((SPAN, 2 * heads), lambda b: (at(b), 0)),
        pl.BlockSpec((1, 2 * heads, SPAN), lambda b: (at(b), 0, 0)),
        pl.BlockSpec((number, d, d), lambda b: (part_at, 0, 0)),
        wide,
        wide,
        pl.BlockSpec((rim, size), lambda b: (count // rim, part_at)),
        pl.BlockSpec((4, size), lambda b: (0, part_at)),
        pl.BlockSpec((SPAN, 2 * size), lambda b: (at(b), part_at)),
        pl.BlockSpec((SPAN, 2 * size), lambda b: (at(b), part_at)),
        pl.BlockSpec((rim, 2 * size), lambda b: (count // rim, part_at)),
        pl.BlockSpec((4, 2 * size), lambda b: (0, part_at)),
    ]
    return pl.pallas_call(
        partial(backward_kernel, heads, part, d),
        grid=(blocks + 1,),
        in_specs=in_specs,
        out_specs=[
            pl.BlockSpec((SPAN, 3 * size), lambda b: (jnp.where(b < blocks, blocks - 1 - b, blocks), 0)),
            pl.BlockSpec((SPAN, d), lambda b: (at(b), 0)),
            pl.BlockSpec((4, 3 * size), lambda b: (0, 0)),
        ],
        out_shape=[
            shape((count + rim, 3 * size), BF),
            shape((count, d), F32),
            shape((4, 3 * size), F32),
        ],
        scratch_shapes=[pltpu.VMEM((number, d, d), F32), pltpu.VMEM((3, rim, 3 * size), F32)],
        compiler_params=params(),
        cost_estimate=cost(8 + 2 * number),
        name="delta_backward",
    )(*in_hbm(q, k, v, w, u, a, e, kept_states, do, cols, rows, later, qz, qg_pre, qg_pre, qtaps, kvz, kv_pre, kv_pre, kvtaps))


def feed_kernel(
    n_ref, e_ref, mid_ref, g_ref, u_ref, d_ref, gb_ref, ub_ref, db_ref,
    f_ref, pair_ref, out_ref, dn_ref, total, held,
):
    step = pl.program_id(0)
    last = pl.num_programs(0) - 1
    wide = g_ref.shape[1]

    @pl.when(step == 0)
    def _():
        dn_ref[...] = jnp.zeros_like(dn_ref)
        total[...] = mid_ref[...]

    slot, other = step % 2, 1 - step % 2

    def first(i):
        gate = nn(n_ref[...], g_ref[...])
        yield True
        up = nn(n_ref[...], u_ref[...])
        yield True
        df = nt(e_ref[...], d_ref[...])
        yield True
        sig = sigmoid(gate)
        act = gate * sig
        f = (act * up).astype(BF)
        dgate = (df * up * (sig * (1.0 + gate * (1.0 - sig)))).astype(BF)
        dup = (df * act).astype(BF)
        f_ref[...] = f
        pair_ref[0] = dgate
        pair_ref[1] = dup
        held[slot, :, 0:wide] = f
        held[slot, :, wide : 2 * wide] = dgate
        held[slot, :, 2 * wide :] = dup
        yield True

    def second(i):
        total[...] += nn(held[other, :, 0:wide], db_ref[...])
        yield True
        both_w = jnp.concatenate([gb_ref[...], ub_ref[...]], axis=1)
        dn_ref[...] += nt(held[other, :, wide:], both_w)
        yield True

    def both(i):
        running = [first(i), second(i)]
        while running:
            running = [one for one in running if next(one, False)]
            yield True

    @pl.when(step == 0)
    def _():
        in_turn(first, 1, 1)

    @pl.when(jnp.logical_and(step > 0, step < last))
    def _():
        in_turn(both, 1, 1)

    @pl.when(step == last)
    def _():
        in_turn(second, 1, 1)
        out_ref[...] = total[...].astype(BF)


def feed_forward(normed, cotangent, middle, pair, down):
    count, width = normed.shape
    hidden = down.shape[0]
    wide = 2 * 128
    blocks = hidden // wide
    whole = pl.BlockSpec((count, width), lambda i: (0, 0))
    now = lambda i: jnp.minimum(i, blocks - 1)
    past = lambda i: jnp.maximum(i - 1, 0)
    weights = []
    for at in (now, past):
        weights += [
            pl.BlockSpec((width, wide), lambda i, at=at: (0, at(i))),
            pl.BlockSpec((width, wide), lambda i, at=at: (0, blocks + at(i))),
            pl.BlockSpec((wide, width), lambda i, at=at: (at(i), 0)),
        ]
    return pl.pallas_call(
        feed_kernel,
        grid=(blocks + 1,),
        in_specs=[whole, whole, whole] + weights,
        out_specs=[
            pl.BlockSpec((count, wide), lambda i: (0, now(i))),
            pl.BlockSpec((2, count, wide), lambda i: (0, 0, now(i))),
            whole,
            whole,
        ],
        out_shape=[
            shape((count, hidden), BF),
            shape((2, count, hidden), BF),
            shape((count, width), BF),
            shape((count, width), F32),
        ],
        scratch_shapes=[pltpu.VMEM((count, width), F32), pltpu.VMEM((2, count, 3 * wide), BF)],
        compiler_params=pltpu.CompilerParams(
            dimension_semantics=("arbitrary",), vmem_limit_bytes=40 * 1024 * 1024
        ),
        cost_estimate=cost(25),
        name="feed_forward",
    )(*in_hbm(normed, cotangent, middle, pair, pair, down, pair, pair, down))


def scan_states(x):
    peers, d, width = x.shape
    return pl.pallas_call(
        partial(prefix_kernel, peers),
        out_shape=shape((peers, d, width - d), BF),
        cost_estimate=cost(3),
        name="state_prefix",
    )(x)


def scan_grads(x, g):
    peers, d, width = g.shape
    return pl.pallas_call(
        partial(suffix_kernel, peers),
        out_shape=shape((peers, d, width), BF),
        cost_estimate=cost(3),
        name="state_suffix",
    )(x, g)


def hold(value, *after):
    return lax.optimization_barrier((value, after))[0]


class Place:
    def __init__(self):
        self.nf, self.nr = lax.axis_size("fsdp"), lax.axis_size("rep")
        self.ny = self.nf // 4
        self.nx = self.nr // 2
        self.f, self.r = lax.axis_index("fsdp"), lax.axis_index("rep")
        z = self.f // self.ny
        self.mine = {"v": z // 2, "w": z % 2, "y": self.f % self.ny, "x": self.r // 2, "c": self.r % 2}
        self.number = {"v": 2, "w": 2, "u": 2, "y": self.ny, "x": self.nx, "c": 2}
        self.stride = {"v": 2 * self.ny, "w": self.ny, "y": 1, "x": 2, "c": 1}

    def send(self, value, way, steps=1):
        if way == "u":
            return lax.ppermute(value, "fsdp", [(i, i ^ 3 * self.ny) for i in range(self.nf)])
        axis = "rep" if way in "xc" else "fsdp"
        total = self.nr if way in "xc" else self.nf
        number, stride = self.number[way], self.stride[way]
        pairs = []
        for i in range(total):
            at = i // stride % number
            pairs.append((i, i + ((at + steps) % number - at) * stride))
        return lax.ppermute(value, axis, pairs)


def place_kernel(count, rows, each, by_rows, widths, offs_ref, own_ref, *refs):
    stacks, outs, sems = refs[: len(count)], refs[len(count) : -1], refs[-1]
    copies = []

    def put(src, row, height, column, out):
        copy = pltpu.make_async_copy(src, out.at[pl.ds(row, height), column], sems.at[len(copies)])
        copy.start()
        copies.append(copy)

    starts = [sum(widths[:i]) for i in range(len(widths))]
    top = pl.multiple_of(offs_ref[0], rows)
    for start, width, out in zip(starts, widths, outs):
        put(own_ref.at[:, pl.ds(start, width)], top, rows, pl.ds(0, width), out)
    at = 1
    for stack, number in zip(stacks, count):
        for j in range(number):
            row = pl.multiple_of(offs_ref[at], each if by_rows else rows)
            if by_rows:
                for start, width, out in zip(starts, widths, outs):
                    put(stack.at[j, :, pl.ds(start, width)], row, each, pl.ds(0, width), out)
                at += 1
            else:
                column = pl.multiple_of(offs_ref[at + 1], each)
                put(stack.at[j], row, rows, pl.ds(column, each), outs[0])
                at += 2
    for copy in copies:
        copy.wait()


class Gather:
    def __init__(self, here, shard, widths, deep, by_rows=True):
        self.here, self.shard, self.widths, self.deep, self.by_rows = here, shard, widths, deep, by_rows
        rows, total = shard.shape
        parts = here.nr if deep else 2
        extent = rows if by_rows else total
        self.each = extent // parts
        self.plain = bool(extent % parts or self.each % (32 if by_rows else 128) or rows % 32)
        self.plain = self.plain or here.ny != 2 or here.nx != 2
        self.have = {}
        if self.plain:
            return
        part = here.r if deep else here.mine["c"]
        self.have[""] = lax.dynamic_slice_in_dim(shard, part * self.each, self.each, 0 if by_rows else 1)

    def got(self, *names):
        return [] if self.plain else [self.have[name] for name in names]

    def move(self, *names, after=()):
        if not self.plain:
            for name in names:
                self.have[name] = self.here.send(hold(self.have[name[:-1]], *after), name[-1])

    def pile(self):
        if not self.plain:
            last = "u" if "u" in self.have else "vw"
            self.have["z"] = jnp.stack([self.have[name] for name in ("", "w", "v", last)])

    def place(self):
        here, shard, widths = self.here, self.shard, self.widths
        rows, each = shard.shape[0], self.each
        if self.plain:
            whole = lax.all_gather(shard, "fsdp", axis=0, tiled=True)
            starts = [sum(widths[:i]) for i in range(len(widths))]
            return [whole[:, s : s + w] for s, w in zip(starts, widths)]
        mine = here.mine
        offsets = [here.f * rows]
        names = [name for name in self.have if name.startswith("z")]
        for name in names:
            x, c, y = ((mine[way] + (way in name)) % 2 for way in "xcy")
            inside = (x * 2 + c if self.deep else c) * each
            for j in range(4):
                v = (mine["v"] + j // 2) % 2
                w = (mine["w"] + j % 2) % 2
                source = (v * 2 + w) * here.ny + y
                offsets += [source * rows + inside] if self.by_rows else [source * rows, inside]
        offsets = jnp.stack(offsets).astype(jnp.int32)
        stacks = [self.have[name] for name in names]
        count = [4] * len(stacks)
        any_space = pl.BlockSpec(memory_space=pl.ANY)
        size = here.nf * rows
        return pl.pallas_call(
            partial(place_kernel, count, rows, each, self.by_rows, widths),
            grid_spec=pltpu.PrefetchScalarGridSpec(
                num_scalar_prefetch=1,
                grid=(1,),
                in_specs=[any_space] * (1 + len(stacks)),
                out_specs=[pl.BlockSpec((size, w), lambda i, o: (0, 0)) for w in widths],
                scratch_shapes=[pltpu.SemaphoreType.DMA(((1 + sum(count)) * len(widths),))],
            ),
            out_shape=[jax.ShapeDtypeStruct((size, w), shard.dtype) for w in widths],
            compiler_params=pltpu.CompilerParams(
                vmem_limit_bytes=2 * size * sum(widths) * 2 + (1 << 20)
            ),
            cost_estimate=cost(6),
            name="place_weights",
        )(offsets, shard, *stacks)


class Reduce:
    def __init__(self, here):
        self.here = here
        self.split = False

    def swap(self, away):
        self.away = away.astype(BF)
        self.came = self.here.send(self.away, "c")

    def take(self, part):
        self.begin(part + self.came.astype(F32))

    def begin(self, part):
        part = part.astype(BF)
        here = self.here
        rows = part.shape[0] // here.nf
        self.part = part.reshape(2, 2, here.ny, rows, part.shape[1])
        self.axes = ["v", "w", "y"]

    def go(self, way, *after):
        here = self.here
        part = hold(self.part, *after)
        number, mine = here.number[way], here.mine[way]
        if way in "xc" and not self.axes:
            self.total = part.astype(F32)
            self.outs = [part] * (number - 1)
        else:
            if way == "x":
                axis = len(self.axes)
                shape = part.shape
                part = part.reshape(
                    shape[:axis] + (number, shape[axis] // number) + shape[axis + 1 :]
                )
                self.split = True
            else:
                axis = self.axes.index(way)
                self.axes.pop(axis)
            self.total = lax.dynamic_index_in_dim(part, mine, axis, keepdims=False).astype(F32)
            self.outs = [
                lax.dynamic_index_in_dim(part, (mine + s) % number, axis, keepdims=False)
                for s in range(1, number)
            ]
        self.got = [here.send(out, way, s) for s, out in zip(range(1, number), self.outs)]

    def begin_x(self, part, *after):
        self.part, self.axes = part, []
        self.go("x", *after)

    def two(self, at):
        first, second = Reduce(self.here), Reduce(self.here)
        for one, cut in ((first, slice(0, at)), (second, slice(at, None))):
            one.part, one.axes = self.part[..., cut], list(self.axes)
        return first, second

    def join(self, first, second):
        self.part = jnp.concatenate([first.part, second.part], axis=-1)
        self.axes, self.split = list(first.axes), True

    def both(self):
        self.total = self.part.astype(F32)
        self.got = [self.here.send(self.part, "c")]

    def end(self):
        total = self.total
        for came in self.got:
            total = total + came.astype(F32)
        self.part = total.astype(BF)

    def step(self, way, *after):
        self.go(way, *after)
        self.end()

    def rows(self):
        if self.split:
            self.part = join_way(self.here, self.part, "x", 0)

    def other(self):
        return self.here.send(self.part, "c")


def meet(value, *sums):
    value, came = lax.optimization_barrier((value, [one.got for one in sums]))
    for one, got in zip(sums, came):
        one.got = got
        one.end()
    return value


def join_way(here, array, way, axis):
    number, mine = here.number[way], here.mine[way]
    got = [array] + [here.send(array, way, s) for s in range(1, number)]
    if number == 2:
        ahead = jnp.concatenate(got, axis=axis)
        behind = jnp.concatenate(got[::-1], axis=axis)
        return jnp.where(mine == 0, ahead, behind)
    stack = jnp.stack(got)
    order = (mine - jnp.arange(number)) % number
    stack = jnp.take(stack, order, axis=0)
    return jnp.concatenate([stack[i] for i in range(number)], axis=axis)


def gather_apart(here, shard):
    rows = shard.shape[0] // here.nr
    piece = lax.dynamic_slice_in_dim(shard, here.r * rows, rows, 0)
    return lax.all_gather(piece, ("fsdp", "rep"), axis=0, tiled=True)


def scatter_owners(array):
    return lax.psum_scatter(array, "fsdp", scatter_dimension=0, tiled=True)


def sum_x(here, array, *after):
    array = hold(array, *after)
    total = array.astype(F32)
    for s in range(1, here.nx):
        total = total + here.send(array, "x", s).astype(F32)
    return total.astype(BF)


def contract(left, right, left_dim, right_dim):
    return lax.dot_general(
        left, right, (((left_dim,), (right_dim,)), ((), ())), preferred_element_type=F32
    )


def rms_norm(values, gain):
    return values * lax.rsqrt(jnp.mean(values * values, axis=-1, keepdims=True) + EPSILON) * gain


def kv_order(array):
    eighth = array.shape[1] // 24
    starts, sizes = (8, 16, 14, 22), (6, 6, 2, 2)
    return [array[:, i * eighth : (i + n) * eighth] for i, n in zip(starts, sizes)]


def from_behind(value, steps):
    count = lax.axis_size("fsdp")
    first, last = (max(0, -steps), min(count, count - steps))
    return lax.ppermute(value, "fsdp", [(source, source + steps) for source in range(first, last)])


def to_owners(parts, fanout):
    heads, d, width = parts.shape
    cut = parts.reshape(heads, d, fanout, width // fanout)
    return jnp.swapaxes(cut, 1, 2).reshape(heads * fanout, d, width // fanout)


def to_heads(parts, fanout):
    owners, d, width = parts.shape
    cut = parts.reshape(owners // fanout, fanout, d, width)
    return jnp.swapaxes(cut, 1, 2).reshape(owners // fanout, d, width * fanout)


def swap(value):
    return lax.all_to_all(value, "fsdp", 0, 0, tiled=True)


def by_core(here, for_zero, for_one):
    return jnp.where(here.mine["c"] == 0, for_zero, for_one)


def on_device(
    hidden_in,
    seg_ids,
    attn_gain,
    qkv_weight,
    beta_weight,
    gate_weight,
    conv_taps,
    out_gain,
    out_weight,
    ffn_gain,
    ffn_gate,
    ffn_up,
    ffn_down,
    cotangent,
):
    here = Place()
    row_count, width = hidden_in.shape
    heads = beta_weight.shape[1]
    head_dim = width // heads
    blocks = row_count // SPAN
    rim = 8
    lanes = 128
    hidden_units = ffn_gate.shape[1]

    numbers = seg_ids + 1

    small = [attn_gain, out_gain, ffn_gain, conv_taps]
    shard_rows = qkv_weight.shape[0]
    flat = jnp.concatenate([a.reshape(-1) for a in small])
    columns = -(-flat.size // shard_rows)
    flat = jnp.pad(flat, (0, columns * shard_rows - flat.size)).reshape(shard_rows, columns)
    extra = jnp.concatenate(
        [beta_weight, flat, jnp.zeros((shard_rows, lanes - heads - columns), BF)], axis=1
    )
    first = Gather(
        here,
        jnp.concatenate(kv_order(qkv_weight) + [extra], axis=1),
        [2 * width, lanes],
        True,
    )
    second = Gather(
        here,
        jnp.concatenate([qkv_weight[:, :width], gate_weight, out_weight], axis=1),
        [2 * width, width],
        True,
    )
    rim_rows = from_behind(hidden_in[row_count - rim :], 1)
    rim_ids = from_behind(numbers[row_count - rim :], 1)
    pair_full = gather_apart(here, jnp.concatenate([ffn_gate, ffn_up], axis=1))
    first.move("v", "w")
    first.move("vw")
    first.pile()
    if not first.plain:
        first.have["z"], rim_rows, rim_ids = lax.optimization_barrier((first.have["z"], rim_rows, rim_ids))
    first.move("zy", "zx")
    first.move("zc")
    second.move("v", "w", after=first.got("z"))
    first.move("zyx", after=first.got("zx", "zc"))
    first.move("zyc", "zxc")
    first.move("zyxc", after=first.got("zyc", "zxc"))
    kv_full, extra_full = first.place()

    small_full = extra_full[:, heads : heads + columns].reshape(here.nf, -1)
    cuts, at = [], 0
    for array in small:
        cuts.append(small_full[:, at : at + array.size].astype(F32))
        at += array.size
    attn_scale = cuts[0].reshape(-1)
    outgain_scale = cuts[1].reshape(1, -1)
    ffngain_scale = cuts[2].reshape(-1)
    taps_count = conv_taps.shape[0]
    taps_scale = jnp.swapaxes(cuts[3].reshape(here.nf, taps_count, -1), 0, 1).reshape(taps_count, -1)
    query_taps = taps_scale[:, :width]
    kv_taps = jnp.concatenate(kv_order(taps_scale), axis=1)
    residual = hidden_in.astype(F32)
    extended_in = jnp.concatenate([hidden_in, rim_rows]).astype(F32)
    normed_ext = rms_norm(extended_in, attn_scale).astype(BF)
    normed_low = normed_ext[:row_count]
    kv_pre = jnp.dot(normed_ext, kv_full, preferred_element_type=F32)
    second.move("vw", after=[kv_full])
    second.pile()
    kv_pre = hold(kv_pre, second.got("z"))
    second.move("zy", "zx", after=[kv_pre])
    beta_pre = jnp.dot(normed_low, extra_full, preferred_element_type=F32)[:, :heads]
    rates = jax.nn.sigmoid(beta_pre)
    ids = jnp.concatenate([rim_ids, numbers]).astype(F32)
    own_ids = numbers.astype(F32)
    before = ids[rim - 1 : rim - 1 + row_count : SPAN]
    cols = jnp.concatenate(
        [rates, own_ids[:, None]]
        + [(ids[rim - j : rim - j + row_count] == own_ids).astype(F32)[:, None] for j in (1, 2, 3)]
        + [jnp.zeros((row_count, heads - 4), F32)],
        1,
    )
    rows = jnp.concatenate(
        [
            jnp.swapaxes(rates.reshape(blocks, SPAN, heads), 1, 2),
            own_ids.reshape(blocks, 1, SPAN),
            jnp.broadcast_to(before[:, None, None], (blocks, 1, SPAN)),
            jnp.zeros((blocks, heads - 2, SPAN), F32),
        ],
        1,
    )
    key_low, value_low, kv_mixed, w, u, a, moves = delta_summary(kv_pre, kv_taps, cols, rows, heads)
    moves = hold(moves, second.got("zy", "zx"))
    down_full = gather_apart(here, hold(ffn_down, pair_full, moves))
    second.move("zyx", after=[moves] + second.got("zx"))
    second.move("zc", "zyc", "zxc", after=[moves])
    fanout = here.nf // heads
    if fanout > 1:
        moves = jnp.concatenate(
            [
                to_owners(moves[:, :, :head_dim], fanout),
                jnp.repeat(moves[:, :, head_dim:], fanout, axis=0),
            ],
            axis=2,
        )
    owned = swap(moves)
    states = scan_states(owned)
    second.move("zyxc", after=[states])
    entry = swap(states)
    qg_full, outw_full = second.place()
    qg_pre = jnp.dot(normed_ext, qg_full, preferred_element_type=F32)
    if fanout > 1:
        entry = to_heads(entry, fanout)
    query_low, q_mixed, gated_low, attn_heads, fresh, kept = delta_forward(
        qg_pre, query_taps, key_low, w, u, cols, rows, entry, outgain_scale, heads
    )
    middle = residual + jnp.dot(gated_low, outw_full, preferred_element_type=F32)
    normed_two, norm_two_back = jax.vjp(partial(rms_norm, gain=ffngain_scale), middle)
    normed_two_low = normed_two.astype(BF)
    hidden_low, pair_low, output, normed_two_grad = feed_forward(
        normed_two_low, cotangent, middle, pair_full, down_full
    )

    c = here.mine["c"]

    def shares(array, start, size):
        half = size // 2
        cut = [lax.dynamic_slice_in_dim(array, start + at * half, half, 1) for at in (1 - c, c)]
        return cut

    theirs, ours = shares(cotangent, 0, width)
    down_sum = Reduce(here)
    down_sum.swap(contract(hidden_low, theirs, 0, 0))
    theirs, ours = [lax.dynamic_index_in_dim(pair_low, at, 0, keepdims=False) for at in (1 - c, c)]
    pair_sum = Reduce(here)
    pair_sum.swap(contract(normed_two_low, theirs, 0, 0))
    down_theirs, down_ours = shares(cotangent, 0, width)
    down_sum = Reduce(here)
    down_sum.swap(contract(hidden_low, down_theirs, 0, 0))
    (middle_back,) = norm_two_back(normed_two_grad)
    middle_grad = cotangent.astype(F32) + middle_back
    middle_low = middle_grad.astype(BF)
    gated_grad = contract(middle_low, outw_full, 1, 1)
    ours = hold(ours, down_sum.away)
    pair_half = (contract(normed_two_low, ours, 0, 0) + pair_sum.came.astype(F32)).astype(BF)
    pair_apart = scatter_owners(pair_half)
    down_sum.take(contract(hidden_low, down_ours, 0, 0))
    gated_grad = hold(gated_grad, down_sum.part, pair_half)
    down_sum.go("x")
    heads_grad, gatepre_low, outgain_grad, local_later = delta_adjoint(
        query_low, key_low, w, cols, rows, gated_grad, attn_heads, qg_pre, outgain_scale, heads
    )
    if fanout > 1:
        local_later = to_owners(local_later, fanout)
    came_later = swap(local_later)

    middle_held, gatepre_held = hold((middle_low, gatepre_low), local_later)
    out_grad = contract(gated_low, middle_held, 0, 0)
    gate_grad = contract(normed_low, gatepre_held, 0, 0)
    other_sum = Reduce(here)
    other_sum.swap(by_core(here, gate_grad, out_grad))
    came_later = hold(came_later, other_sum.away)
    summed_later = scan_grads(owned, came_later)
    later = swap(summed_later)
    if fanout > 1:
        later = to_heads(later, fanout)
    other_sum.take(by_core(here, out_grad, gate_grad))
    later = meet(hold(later, other_sum.part), down_sum)
    down_apart = scatter_owners(down_sum.part.reshape(-1, width // 2))
    other_x, other_y = other_sum.two(width // 2)
    other_x.go("x", later)
    other_y.go("y", later)
    later = hold(later, *other_x.outs, *other_y.outs)
    state = (query_low, key_low, value_low, w, u, a, fresh, kept, heads_grad, cols, rows)
    mixed_a, beta_a, taps_a = delta_backward(
        0, *state, later, q_mixed, qg_pre, query_taps, kv_mixed, kv_pre, kv_taps, heads
    )
    mixed_a = meet(mixed_a, other_x, other_y)
    other_x.go("y")
    other_y.go("x")
    a_sum = Reduce(here)
    cut = [number * head_dim for number in head_parts(heads)]
    theirs, ours = shares(mixed_a, 0, 3 * cut[0])
    a_sum.swap(contract(normed_ext, theirs, 0, 0))
    a_sum.take(contract(normed_ext, ours, 0, 0))
    later = meet(hold(later, a_sum.part), other_x, other_y)
    other_sum.join(other_x, other_y)
    a_x, a_y = a_sum.two((a_sum.part.shape[-1] // lanes + 1) // 2 * lanes)
    a_x.go("x", later)
    a_y.go("y", later)
    other_sum.go("w", later)
    later = hold(later, *a_x.outs, *a_y.outs, *other_sum.outs)
    mixed_b, beta_b, taps_b = delta_backward(
        1, *state, later, q_mixed, qg_pre, query_taps, kv_mixed, kv_pre, kv_taps, heads
    )
    mixed_b = hold(meet(mixed_b, other_sum, a_x, a_y), pair_apart)
    a_x.go("y")
    a_y.go("x")
    b_sum = Reduce(here)
    theirs, ours = shares(mixed_b, 0, 3 * cut[1])
    b_sum.swap(contract(normed_ext, theirs, 0, 0))
    taps_b, beta_b = hold((taps_b, beta_b), b_sum.away)

    def by_kind(first_heads, other_heads):
        pieces = []
        for i in range(3):
            for array, wide in zip((first_heads, other_heads), cut):
                pieces.append(array[:, i * wide : (i + 1) * wide])
        return jnp.concatenate(pieces, axis=1)

    betapre_low = (beta_a + beta_b).astype(BF)
    taps_grad = by_kind(taps_a, taps_b)
    parts = (
        outgain_grad.reshape(here.nf, -1),
        jnp.swapaxes(taps_grad.reshape(taps_count, here.nf, -1), 0, 1).reshape(here.nf, -1),
    )
    flat = jnp.concatenate(parts, axis=1)
    flat = jnp.pad(flat, ((0, 0), (0, columns * shard_rows - flat.shape[1])))
    extra = jnp.pad(flat.reshape(width, columns), ((0, 0), (heads, lanes - heads - columns)))
    small_sum = Reduce(here)
    small_sum.begin(contract(normed_low, hold(betapre_low, mixed_b), 0, 0) + extra)
    small_sum.both()
    b_sum.take(contract(normed_ext, ours, 0, 0))
    small_sum.end()
    mixed_b = hold(mixed_b, b_sum.part, small_sum.part)
    b_sum.go("x")
    small_sum.go("x")
    wide_grad = (
        contract(mixed_a[:, cut[0] :], kv_full[:, : 2 * cut[0]], 1, 1)
        + contract(mixed_b[:, cut[1] :], kv_full[:, 2 * cut[0] :], 1, 1)
        + contract(mixed_a[:, : cut[0]], qg_full[:, : cut[0]], 1, 1)
        + contract(mixed_b[:, : cut[1]], qg_full[:, cut[0] : width], 1, 1)
    )
    rim_grad = from_behind(wide_grad[row_count:].astype(BF), -1).astype(F32)
    normed_grad = (
        wide_grad[:row_count]
        + jnp.pad(rim_grad, ((row_count - rim, 0), (0, 0)))
        + contract(betapre_low, extra_full, 1, 1)
        + contract(gatepre_low, qg_full[:, width:], 1, 1)
    )
    normed_grad = meet(normed_grad, b_sum, a_x, a_y, small_sum)
    other_sum.go("v", normed_grad)
    a_sum.join(a_x, a_y)
    b_sum.go("y")
    small_sum.go("y")
    pair_sum.begin_x(pair_apart, normed_grad)
    a_sum.go("w")
    (input_back,) = jax.vjp(partial(rms_norm, gain=attn_scale), residual)[1](normed_grad)
    input_grad = meet(
        (middle_grad + input_back).astype(BF), b_sum, a_sum, other_sum, small_sum, pair_sum
    )
    b_sum.go("w", input_grad)
    a_sum.go("v", input_grad)
    small_sum.go("w", input_grad)
    def gain_grad(gain, pairs):
        total = sum(jnp.sum(weight.astype(F32) * grad, axis=1) for weight, grad in pairs)
        return total / gain.astype(F32)

    other = here.send(pair_sum.part, "c")
    hidgate_total = by_core(here, pair_sum.part, other).astype(F32)
    hidup_total = by_core(here, other, pair_sum.part).astype(F32)
    ffngain_total = gain_grad(ffn_gain, ((ffn_gate, hidgate_total), (ffn_up, hidup_total)))
    hidgate_total, hidup_total, ffngain_total = meet(
        (hidgate_total, hidup_total, ffngain_total), b_sum, a_sum, small_sum
    )
    b_sum.go("v", a_sum.part)
    small_sum.go("v", a_sum.part)
    held = meet(a_sum.part, b_sum, small_sum)
    both = Reduce(here)
    both.part = jnp.concatenate([b_sum.part, held, other_sum.part, small_sum.part], axis=1)
    both.split = True
    both.rows()
    down_sum.part = hold(down_apart, held)
    down_sum.rows()
    down_total = join_way(here, down_sum.part, "c", 1).astype(F32)
    whole = both.other()
    ends = [0]
    for one in (b_sum, a_sum, other_sum, small_sum):
        ends.append(ends[-1] + one.part.shape[1])

    def joined(start, end):
        mine, theirs = both.part[:, start:end], whole[:, start:end]
        return by_core(here, mine, theirs), by_core(here, theirs, mine)

    b_both, a_both, other_both = [joined(*pair) for pair in zip(ends[:3], ends[1:4])]
    outproj_total, gate_total = [part.astype(F32) for part in other_both]
    qkv_total = by_kind(jnp.concatenate(a_both, axis=1), jnp.concatenate(b_both, axis=1)).astype(F32)
    extra = both.part[:, ends[3] :].astype(F32)
    beta_total = extra[:, :heads]

    attngain_total = gain_grad(
        attn_gain, ((qkv_weight, qkv_total), (beta_weight, beta_total), (gate_weight, gate_total))
    )
    flat = extra[:, heads : heads + columns].reshape(-1)
    cut, at = [], 0
    for part in parts:
        cut.append(flat[at : at + part.shape[1]])
        at += part.shape[1]
    return (
        output,
        input_grad,
        attngain_total,
        qkv_total,
        beta_total,
        gate_total,
        cut[1].reshape(conv_taps.shape),
        cut[0],
        outproj_total,
        ffngain_total,
        hidgate_total,
        hidup_total,
        down_total,
    )


def solution(mesh):
    placed = (
        P(("rep", "fsdp"), None),
        P(("rep", "fsdp")),
        P("fsdp"),
        P("fsdp", None),
        P("fsdp", None),
        P("fsdp", None),
        P(None, "fsdp"),
        P("fsdp"),
        P("fsdp", None),
        P("fsdp"),
        P("fsdp", None),
        P("fsdp", None),
        P("fsdp", None),
        P(("rep", "fsdp"), None),
    )
    return jax.shard_map(
        on_device,
        mesh=mesh,
        in_specs=placed,
        out_specs=(
            P(("rep", "fsdp"), None),
            P(("rep", "fsdp"), None),
            P("fsdp"),
            P("fsdp", None),
            P("fsdp", None),
            P("fsdp", None),
            P(None, "fsdp"),
            P("fsdp"),
            P("fsdp", None),
            P("fsdp"),
            P("fsdp", None),
            P("fsdp", None),
            P("fsdp", None),
        ),
        check_vma=False,
    )
```

```python
from functools import partial

import jax
import jax.numpy as jnp
from jax import lax
from jax.experimental import pallas as pl
from jax.experimental.pallas import tpu as pltpu
from jax.sharding import PartitionSpec as P

SPAN = 64
TOGETHER = 8
EPSILON = 1e-06
BF = jnp.bfloat16
F32 = jnp.float32


def nn(a, b):
    return lax.dot_general(a, b, (((1,), (0,)), ((), ())), preferred_element_type=F32)


def nt(a, b):
    return lax.dot_general(a, b, (((1,), (1,)), ((), ())), preferred_element_type=F32)


def tn(a, b):
    return lax.dot_general(a, b, (((0,), (0,)), ((), ())), preferred_element_type=F32)


def in_turn(body, count, together):
    for start in range(0, count, together):
        running = [body(h) for h in range(start, min(start + together, count))]
        while running:
            running = [one for one in running if next(one, False)]


def block_masks(cols_ref, rows_ref, heads):
    n = SPAN
    row = lax.broadcasted_iota(jnp.int32, (n, n), 0)
    col = lax.broadcasted_iota(jnp.int32, (n, n), 1)
    ids = cols_ref[:, heads : heads + 1]
    ids_row = rows_ref[0, heads : heads + 1, :]
    before = rows_ref[0, heads + 1 : heads + 2, :]
    end = ids_row[:, n - 1 : n]
    same = ids == ids_row
    first = (ids == before[:, :1]).astype(F32)
    last = (ids == end).astype(F32)
    keep = (end == before[:, :1]).astype(F32)
    return row, col, same, first, last, keep


def sigmoid(z):
    return 0.5 * jnp.tanh(0.5 * z) + 0.5


def shifted_rows(x, prev, masks):
    both = jnp.concatenate([prev, x], axis=0)
    lead = prev.shape[0]
    return [x] + [pltpu.roll(both, j, 0)[lead:] * masks[j - 1] for j in (1, 2, 3)]


def mix_rows(rows, taps):
    mixed = rows[0] * taps[0:1]
    for j in (1, 2, 3):
        mixed = mixed + rows[j] * taps[j : j + 1]
    return mixed


def lag_masks(cols_ref, heads):
    return [cols_ref[:, heads + j : heads + j + 1] for j in (1, 2, 3)]


def head_parts(heads):
    return heads - heads // 4, heads // 4


def kv_at(heads, d, h):
    first, other = head_parts(heads)
    number, start, inside = (first, 0, h) if h < first else (other, 2 * first, h - first)
    at = (start + inside) * d
    return slice(at, at + d), slice(at + number * d, at + number * d + d)


def summary_kernel(
    heads, d, pre_ref, prev_ref, taps_ref, cols_ref, rows_ref,
    k_ref, v_ref, z_ref, w_ref, u_ref, a_ref, x_ref, state, levels,
):
    n = SPAN
    block = pl.program_id(0)

    @pl.when(block == 0)
    def _():
        at = lax.broadcasted_iota(jnp.int32, (n, n), 0)
        to = lax.broadcasted_iota(jnp.int32, (n, n), 1)
        for i in range(levels.shape[0]):
            size = 1 << i
            level = jnp.logical_and(
                (at // (2 * size)) == (to // (2 * size)),
                jnp.logical_and(((at // size) & 1) == 1, ((to // size) & 1) == 0),
            )
            levels[i] = level.astype(F32).astype(BF)
        r = lax.broadcasted_iota(jnp.int32, (d, 2 * d), 0)
        c = lax.broadcasted_iota(jnp.int32, (d, 2 * d), 1)
        unit = (r + d == c).astype(F32)
        for h in range(heads):
            state[h] = unit

    row, col, same, first, last, keep = block_masks(cols_ref, rows_ref, heads)
    lower = jnp.logical_and(same, row > col)
    unit = (row == col).astype(F32).astype(BF)
    masks = lag_masks(cols_ref, heads)
    keys, mixing, inverse = ([None] * heads for i in range(3))
    def features(h):
        cut = slice(h * d, (h + 1) * d)
        at_k, at_v = kv_at(heads, d, h)
        z = mix_rows(shifted_rows(pre_ref[:, at_k], prev_ref[:, at_k], masks), taps_ref[:, at_k])
        z_ref[:, at_k] = z
        yield True
        act = z * sigmoid(z)
        root = lax.rsqrt(jnp.sum(act * act, axis=1, keepdims=True) + EPSILON)
        yield True
        keys[h] = (act * root).astype(BF)
        k_ref[:, cut] = keys[h]
        yield True
        z = mix_rows(shifted_rows(pre_ref[:, at_v], prev_ref[:, at_v], masks), taps_ref[:, at_v])
        z_ref[:, at_v] = z
        v_ref[:, cut] = (z * sigmoid(z)).astype(BF)
        m = jnp.where(lower, nt(keys[h], keys[h]) * cols_ref[:, h : h + 1], 0.0).astype(BF)
        yield True
        mixing[h] = m
        inverse[h] = unit - m * levels[0]

    in_turn(features, heads, TOGETHER)
    for i in range(1, levels.shape[0]):
        level = levels[i]
        inner = [nn(mixing[h] * level, inverse[h]).astype(BF) for h in range(heads)]
        for h in range(heads):
            inverse[h] = inverse[h] - nn(inverse[h], inner[h]).astype(BF) * level
    def advance(h):
        cut = slice(h * d, (h + 1) * d)
        a_ref[h] = inverse[h]
        scaled = (inverse[h].astype(F32) * rows_ref[0, h : h + 1, :]).astype(BF)
        yield True
        both = nn(scaled, jnp.concatenate([keys[h], v_ref[:, cut]], axis=1))
        yield True
        w = both[:, :d].astype(BF)
        u = both[:, d:].astype(BF)
        w_ref[:, cut] = w
        u_ref[:, cut] = u
        yield True
        held = state[h]
        moved = nn(w, held.astype(BF)) * first
        yield True
        fresh = (jnp.concatenate([u.astype(F32), jnp.zeros((n, d), F32)], axis=1) - moved).astype(BF)
        yield True
        key_last = keys[h] * last.astype(BF)
        yield True
        state[h] = keep * held + tn(key_last, fresh)

    in_turn(advance, heads, TOGETHER)

    @pl.when(block == pl.num_programs(0) - 1)
    def _():
        x_ref[...] = state[...].astype(BF)


def forward_kernel(
    heads, d, pre_ref, prev_ref, taps_ref, k_ref, w_ref, u_ref, cols_ref, rows_ref, s_ref, gate_ref, gain_ref,
    q_ref, z_ref, y_ref, o_ref, e_ref, kept_ref, state,
):
    n = SPAN
    block = pl.program_id(0)

    @pl.when(block == 0)
    def _():
        state[...] = s_ref[...].astype(F32)

    row, col, same, first, last, keep = block_masks(cols_ref, rows_ref, heads)
    visible = jnp.logical_and(same, row >= col)
    masks = lag_masks(cols_ref, heads)
    def one_head(h):
        cut = slice(h * d, (h + 1) * d)
        z = mix_rows(shifted_rows(pre_ref[:, cut], prev_ref[:, cut], masks), taps_ref[:, cut])
        z_ref[:, cut] = z
        q = (z * sigmoid(z) * d ** (-0.5)).astype(BF)
        q_ref[:, cut] = q
        yield True
        k, w = k_ref[:, cut], w_ref[:, cut]
        held = state[h]
        held_low = held.astype(BF)
        kept_ref[0, h] = held_low
        both = nn(jnp.concatenate([w, q], axis=0), held_low)
        yield True
        fresh = (u_ref[:, cut].astype(F32) - first * both[:n]).astype(BF)
        e_ref[:, cut] = fresh
        yield True
        scores = jnp.where(visible, nt(q, k), 0.0).astype(BF)
        yield True
        out = first * both[n:] + nn(scores, fresh)
        yield True
        key_last = k * last.astype(BF)
        state[h] = keep * held + tn(key_last, fresh)
        yield True
        o_ref[:, cut] = out
        yield True
        g = gate_ref[:, cut]
        root = lax.rsqrt(jnp.mean(out * out, axis=1, keepdims=True) + EPSILON)
        yield True
        y_ref[:, cut] = (out * root * gain_ref[...] * (g * sigmoid(g))).astype(BF)

    in_turn(one_head, heads, TOGETHER)


def adjoint_kernel(
    heads, d, q_ref, k_ref, w_ref, cols_ref, rows_ref, dy_ref, o_ref, gate_ref, gain_ref,
    do_ref, dgate_ref, dgain_ref, ds_ref, state,
):
    n = SPAN
    step = pl.program_id(0)

    @pl.when(step == 0)
    def _():
        state[...] = jnp.zeros_like(state)
        dgain_ref[...] = jnp.zeros_like(dgain_ref)

    row, col, same, first, last, keep = block_masks(cols_ref, rows_ref, heads)
    visible = jnp.logical_and(same, row >= col)
    first_low = first.astype(BF)
    gain = gain_ref[...]
    gain_sum = jnp.zeros((1, d), F32)
    def one_head(h):
        nonlocal gain_sum
        cut = slice(h * d, (h + 1) * d)
        q, k, w = q_ref[:, cut], k_ref[:, cut], w_ref[:, cut]
        o, g, dy = o_ref[:, cut], gate_ref[:, cut], dy_ref[:, cut]
        root = lax.rsqrt(jnp.mean(o * o, axis=1, keepdims=True) + EPSILON)
        yield True
        unit = o * root
        sig = sigmoid(g)
        m = g * sig
        t = dy * m
        gain_sum = gain_sum + jnp.sum(t * unit, axis=0, keepdims=True)
        tg = t * gain
        do = root * (tg - unit * jnp.mean(tg * unit, axis=1, keepdims=True))
        yield True
        dgate_ref[:, cut] = (dy * gain * unit * (sig * (1.0 + g * (1.0 - sig)))).astype(BF)
        do_low = do.astype(BF)
        do_ref[:, cut] = do_low
        yield True
        scores = jnp.where(visible, nt(q, k), 0.0).astype(BF)
        yield True
        later = state[h]
        de = last * nn(k, later.astype(BF)) + tn(scores, do_low)
        yield True
        left = jnp.concatenate([q * first_low, w * -first_low], axis=0)
        right = jnp.concatenate([do_low, de.astype(BF)], axis=0)
        state[h] = keep * later + tn(left, right)
        yield True

    in_turn(one_head, heads, TOGETHER)
    dgain_ref[...] += gain_sum

    @pl.when(step == pl.num_programs(0) - 1)
    def _():
        ds_ref[...] = state[...].astype(BF)


def backward_kernel(
    heads, part, d, q_ref, k_ref, v_ref, w_ref, u_ref, a_ref, e_ref, kept_ref, do_ref, cols_ref, rows_ref, s_ref,
    qz_ref, qpre_ref, qrim_ref, qtaps_ref, kvz_ref, kvpre_ref, kvrim_ref, kvtaps_ref,
    dpre_ref, dbeta_ref, dtaps_ref, state, carry,
):
    n = SPAN
    step = pl.program_id(0)
    number = head_parts(heads)[part]
    base = heads - number if part else 0

    @pl.when(step == 0)
    def _():
        state[...] = s_ref[...].astype(F32)
        carry[...] = jnp.zeros_like(carry)
        dtaps_ref[...] = jnp.zeros_like(dtaps_ref)

    @pl.when(step < pl.num_programs(0) - 1)
    def _():
        row, col, same, first, last, keep = block_masks(cols_ref, rows_ref, heads)
        visible = jnp.logical_and(same, row >= col)
        lower = jnp.logical_and(same, row > col)
        lane = lax.broadcasted_iota(jnp.int32, (n, d), 1)
        masks = lag_masks(cols_ref, heads)
        rate_grads = jnp.zeros((n, d), F32)

        first_low = first.astype(BF)

        def conv_back(dact, z, sig, pre, taps, at):
            dconv = dact * (sig * (1.0 + z * (1.0 - sig)))
            here = slice(at, at + d)
            dpre = dconv * taps[0:1]
            sums = [jnp.sum(dconv * pre, axis=0, keepdims=True)]
            for j in (1, 2, 3):
                masked = dconv * masks[j - 1]
                both = jnp.concatenate([masked, carry[j - 1, :, here]], axis=0)
                moved = pltpu.roll(both, both.shape[0] - j, 0)[:n]
                dpre = dpre + moved * taps[j : j + 1]
                sums.append(jnp.sum(moved * pre, axis=0, keepdims=True))
                carry[j - 1, :, here] = masked[:8]
            dtaps_ref[:, here] += jnp.concatenate(sums, axis=0)
            dpre_ref[:, here] = dpre.astype(BF)

        def one_head(h):
            nonlocal rate_grads
            cut = slice(h * d, (h + 1) * d)
            cut_v = slice((number + h) * d, (number + h + 1) * d)
            q, k, v, w, u = q_ref[:, cut], k_ref[:, cut], v_ref[:, cut], w_ref[:, cut], u_ref[:, cut]
            do, e, held = do_ref[:, cut], e_ref[:, cut], kept_ref[0, h]
            at = base + h
            rate = cols_ref[:, at : at + 1]
            later = state[h]
            later_low = later.astype(BF)
            scores = jnp.where(visible, nt(q, k), 0.0).astype(BF)
            yield True
            de = last * nn(k, later_low) + tn(scores, do)
            yield True
            de_low = de.astype(BF)
            dscores = jnp.where(visible, nt(do, e), 0.0).astype(BF)
            yield True
            both = nt(jnp.concatenate([do, de_low], axis=0), held)
            yield True
            dq = first * both[:n] + nn(dscores, k)
            dw = -first * both[n:]
            dk = tn(dscores, q) + last * nt(e, later_low)
            yield True
            pg = tn(a_ref[h], jnp.concatenate([dw.astype(BF), de_low], axis=1))
            yield True
            p, g = pg[:, :d], pg[:, d:]
            dmix = jnp.where(lower, -nt(pg.astype(BF), jnp.concatenate([w, u], axis=1)), 0.0).astype(BF)
            yield True
            kf = k.astype(F32)
            drk = p + nn(dmix, k)
            dk = dk + tn(dmix, (kf * rate).astype(BF)) + rate * drk
            yield True
            dr = jnp.sum(drk * kf + g * v.astype(F32), axis=1, keepdims=True)
            rate_grads = jnp.where(lane == at, dr * rate * (1.0 - rate), rate_grads)
            left = jnp.concatenate([q * first_low, w * -first_low], axis=0)
            right = jnp.concatenate([do, de_low], axis=0)
            state[h] = keep * later + tn(left, right)
            yield True

            z = qz_ref[:, cut]
            conv_back(dq * d ** (-0.5), z, sigmoid(z), qpre_ref[:, cut], qtaps_ref[:, cut], h * d)
            yield True
            z = kvz_ref[:, cut]
            sig = sigmoid(z)
            act = z * sig
            root = lax.rsqrt(jnp.sum(act * act, axis=1, keepdims=True) + EPSILON)
            unit = act * root
            dact = root * (dk - unit * jnp.sum(unit * dk, axis=1, keepdims=True))
            conv_back(dact, z, sig, kvpre_ref[:, cut], kvtaps_ref[:, cut], (number + h) * d)
            yield True
            z = kvz_ref[:, cut_v]
            conv_back(
                rate * g, z, sigmoid(z), kvpre_ref[:, cut_v], kvtaps_ref[:, cut_v], (2 * number + h) * d
            )

        in_turn(one_head, number, TOGETHER)
        dbeta_ref[...] = rate_grads

    @pl.when(step == pl.num_programs(0) - 1)
    def _():
        wide = number * d
        for i, taps_ref, rim_ref, at in (
            (0, qtaps_ref, qrim_ref, 0),
            (1, kvtaps_ref, kvrim_ref, 0),
            (2, kvtaps_ref, kvrim_ref, wide),
        ):
            here, there = slice(i * wide, (i + 1) * wide), slice(at, at + wide)
            dpre = jnp.zeros((8, wide), F32)
            sums = [jnp.zeros((1, wide), F32)]
            for j in (1, 2, 3):
                held = carry[j - 1, :, here]
                moved = jnp.concatenate([jnp.zeros_like(held), held], axis=0)[j : 8 + j]
                dpre = dpre + moved * taps_ref[j : j + 1, there]
                sums.append(jnp.sum(moved * rim_ref[:, there], axis=0, keepdims=True))
            dtaps_ref[:, here] += jnp.concatenate(sums, axis=0)
            dpre_ref[0:8, here] = dpre.astype(BF)


def prefix_kernel(peers, x_ref, out_ref):
    cols = out_ref.shape[2]
    held = jnp.zeros(out_ref.shape[1:], F32)
    for i in range(peers):
        out_ref[i] = held.astype(BF)
        held = nn(x_ref[i, :, cols:], held.astype(BF)) + x_ref[i, :, :cols].astype(F32)


def suffix_kernel(peers, t_ref, g_ref, out_ref):
    held = jnp.zeros(out_ref.shape[1:], F32)
    cols = out_ref.shape[2]
    for i in reversed(range(peers)):
        out_ref[i] = held.astype(BF)
        held = tn(t_ref[i, :, cols:], held.astype(BF)) + g_ref[i].astype(F32)


VMEM_LIMIT = 16 * 1024 * 1024


def in_hbm(*arrays):
    return [pltpu.with_memory_space_constraint(a, pltpu.HBM) for a in arrays]


def params():
    return pltpu.CompilerParams(dimension_semantics=("arbitrary",), vmem_limit_bytes=VMEM_LIMIT)


def cost(microseconds):
    return pl.CostEstimate(
        flops=int(microseconds * 1e9), bytes_accessed=int(microseconds * 3e6), transcendentals=0
    )


def specs(blocks, heads, d, flip):
    at = (lambda b: blocks - 1 - b) if flip else (lambda b: b)
    wide = pl.BlockSpec((SPAN, heads * d), lambda b: (at(b), 0))
    cols = pl.BlockSpec((SPAN, 2 * heads), lambda b: (at(b), 0))
    rows = pl.BlockSpec((1, 2 * heads, SPAN), lambda b: (at(b), 0, 0))
    state = pl.BlockSpec((heads, d, d), lambda b: (0, 0, 0))
    mix = pl.BlockSpec((heads, SPAN, SPAN), lambda b: (0, at(b), 0))
    kept = pl.BlockSpec((1, heads, d, d), lambda b: (at(b), 0, 0, 0))
    gain = pl.BlockSpec((1, d), lambda b: (0, 0))
    return wide, cols, rows, state, mix, kept, gain


def shape(dims, kind):
    return pltpu.HBM(dims, kind)


def near(dims, kind):
    return jax.ShapeDtypeStruct(dims, kind)


def before_block(blocks, rim, size, column):
    def index(b):
        per = SPAN // rim
        return jnp.where(b == 0, blocks * per, b * per - 1), column

    return pl.BlockSpec((rim, size), index)


def delta_summary(pre, taps, cols, rows, heads):
    count, width = cols.shape[0], pre.shape[1] // 2
    d, blocks = width // heads, count // SPAN
    rim = pre.shape[0] - count
    wide, c, r, state, mix, kept, gain = specs(blocks, heads, d, False)
    return pl.pallas_call(
        partial(summary_kernel, heads, d),
        grid=(blocks,),
        in_specs=[
            pl.BlockSpec((SPAN, 2 * width), lambda b: (b, 0)),
            before_block(blocks, rim, 2 * width, 0),
            pl.BlockSpec((4, 2 * width), lambda b: (0, 0)),
            c,
            r,
        ],
        out_specs=[
            wide,
            wide,
            pl.BlockSpec((SPAN, 2 * width), lambda b: (b, 0)),
            wide,
            wide,
            mix,
            pl.BlockSpec((heads, d, 2 * d), lambda b: (0, 0, 0)),
        ],
        out_shape=[
            shape((count, width), BF),
            shape((count, width), BF),
            shape((count, 2 * width), F32),
            shape((count, width), BF),
            shape((count, width), BF),
            shape((heads, count, SPAN), BF),
            shape((heads, d, 2 * d), BF),
        ],
        scratch_shapes=[
            pltpu.VMEM((heads, d, 2 * d), F32),
            pltpu.VMEM((SPAN.bit_length() - 1, SPAN, SPAN), BF),
        ],
        compiler_params=params(),
        cost_estimate=cost(21),
        name="delta_summary",
    )(*in_hbm(pre, pre, taps, cols, rows))


def delta_forward(pre, taps, k, w, u, cols, rows, entry, gain_full, heads):
    count, width = k.shape
    d, blocks = width // heads, count // SPAN
    rim = pre.shape[0] - count
    wide, c, r, state, mix, kept, gain = specs(blocks, heads, d, False)
    return pl.pallas_call(
        partial(forward_kernel, heads, d),
        grid=(blocks,),
        in_specs=[
            wide,
            before_block(blocks, rim, width, 0),
            pl.BlockSpec((4, width), lambda b: (0, 0)),
            wide,
            wide,
            wide,
            c,
            r,
            state,
            pl.BlockSpec((SPAN, width), lambda b: (b, 1)),
            gain,
        ],
        out_specs=[wide, wide, wide, wide, wide, kept],
        out_shape=[
            shape((count, width), BF),
            shape((count, width), F32),
            shape((count, width), BF),
            shape((count, width), F32),
            shape((count, width), BF),
            shape((blocks, heads, d, d), BF),
        ],
        scratch_shapes=[pltpu.VMEM((heads, d, d), F32)],
        compiler_params=params(),
        cost_estimate=cost(11),
        name="delta_forward",
    )(*in_hbm(pre, pre, taps, k, w, u, cols, rows, entry, pre, gain_full))


def delta_adjoint(q, k, w, cols, rows, dy, o, gate, gain_full, heads):
    count, width = k.shape
    d, blocks = width // heads, count // SPAN
    wide, c, r, state, mix, kept, gain = specs(blocks, heads, d, True)
    return pl.pallas_call(
        partial(adjoint_kernel, heads, d),
        grid=(blocks,),
        in_specs=[
            wide,
            wide,
            wide,
            c,
            r,
            wide,
            wide,
            pl.BlockSpec((SPAN, width), lambda b: (blocks - 1 - b, 1)),
            gain,
        ],
        out_specs=[wide, wide, gain, state],
        out_shape=[
            shape((count, width), BF),
            shape((count, width), BF),
            shape((1, d), F32),
            shape((heads, d, d), BF),
        ],
        scratch_shapes=[pltpu.VMEM((heads, d, d), F32)],
        compiler_params=params(),
        cost_estimate=cost(11),
        name="delta_adjoint",
    )(*in_hbm(q, k, w, cols, rows, dy, o, gate, gain_full))


def delta_backward(part, q, k, v, w, u, a, e, kept_states, do, cols, rows, later, qz, qg_pre, qtaps, kvz, kv_pre, kvtaps, heads):
    count, width = k.shape
    d, blocks = width // heads, count // SPAN
    rim = kv_pre.shape[0] - count
    number = head_parts(heads)[part]
    part_at = (heads - number) // number if part else 0
    size = number * d

    def at(step):
        return blocks - 1 - jnp.minimum(step, blocks - 1)

    wide = pl.BlockSpec((SPAN, size), lambda b: (at(b), part_at))
    in_specs = [
        wide,
        wide,
        wide,
        wide,
        wide,
        pl.BlockSpec((number, SPAN, SPAN), lambda b: (part_at, at(b), 0)),
        wide,
        pl.BlockSpec((1, number, d, d), lambda b: (at(b), part_at, 0, 0)),
        wide,
        pl.BlockSpec((SPAN, 2 * heads), lambda b: (at(b), 0)),
        pl.BlockSpec((1, 2 * heads, SPAN), lambda b: (at(b), 0, 0)),
        pl.BlockSpec((number, d, d), lambda b: (part_at, 0, 0)),
        wide,
        wide,
        pl.BlockSpec((rim, size), lambda b: (count // rim, part_at)),
        pl.BlockSpec((4, size), lambda b: (0, part_at)),
        pl.BlockSpec((SPAN, 2 * size), lambda b: (at(b), part_at)),
        pl.BlockSpec((SPAN, 2 * size), lambda b: (at(b), part_at)),
        pl.BlockSpec((rim, 2 * size), lambda b: (count // rim, part_at)),
        pl.BlockSpec((4, 2 * size), lambda b: (0, part_at)),
    ]
    return pl.pallas_call(
        partial(backward_kernel, heads, part, d),
        grid=(blocks + 1,),
        in_specs=in_specs,
        out_specs=[
            pl.BlockSpec((SPAN, 3 * size), lambda b: (jnp.where(b < blocks, blocks - 1 - b, blocks), 0)),
            pl.BlockSpec((SPAN, d), lambda b: (at(b), 0)),
            pl.BlockSpec((4, 3 * size), lambda b: (0, 0)),
        ],
        out_shape=[
            shape((count + rim, 3 * size), BF),
            shape((count, d), F32),
            shape((4, 3 * size), F32),
        ],
        scratch_shapes=[pltpu.VMEM((number, d, d), F32), pltpu.VMEM((3, rim, 3 * size), F32)],
        compiler_params=params(),
        cost_estimate=cost(8 + 2 * number),
        name="delta_backward",
    )(*in_hbm(q, k, v, w, u, a, e, kept_states, do, cols, rows, later, qz, qg_pre, qg_pre, qtaps, kvz, kv_pre, kv_pre, kvtaps))


def feed_kernel(
    n_ref, e_ref, mid_ref, g_ref, u_ref, d_ref, gb_ref, ub_ref, db_ref,
    f_ref, pair_ref, out_ref, dn_ref, total, held,
):
    step = pl.program_id(0)
    last = pl.num_programs(0) - 1
    wide = g_ref.shape[1]

    @pl.when(step == 0)
    def _():
        dn_ref[...] = jnp.zeros_like(dn_ref)
        total[...] = mid_ref[...]

    slot, other = step % 2, 1 - step % 2

    def first(i):
        gate = nn(n_ref[...], g_ref[...])
        yield True
        up = nn(n_ref[...], u_ref[...])
        yield True
        df = nt(e_ref[...], d_ref[...])
        yield True
        sig = sigmoid(gate)
        act = gate * sig
        f = (act * up).astype(BF)
        dgate = (df * up * (sig * (1.0 + gate * (1.0 - sig)))).astype(BF)
        dup = (df * act).astype(BF)
        f_ref[...] = f
        pair_ref[0] = dgate
        pair_ref[1] = dup
        held[slot, :, 0:wide] = f
        held[slot, :, wide : 2 * wide] = dgate
        held[slot, :, 2 * wide :] = dup
        yield True

    def second(i):
        total[...] += nn(held[other, :, 0:wide], db_ref[...])
        yield True
        both_w = jnp.concatenate([gb_ref[...], ub_ref[...]], axis=1)
        dn_ref[...] += nt(held[other, :, wide:], both_w)
        yield True

    def both(i):
        running = [first(i), second(i)]
        while running:
            running = [one for one in running if next(one, False)]
            yield True

    @pl.when(step == 0)
    def _():
        in_turn(first, 1, 1)

    @pl.when(jnp.logical_and(step > 0, step < last))
    def _():
        in_turn(both, 1, 1)

    @pl.when(step == last)
    def _():
        in_turn(second, 1, 1)
        out_ref[...] = total[...].astype(BF)


def feed_forward(normed, cotangent, middle, pair, down):
    count, width = normed.shape
    hidden = down.shape[0]
    wide = 2 * 128
    blocks = hidden // wide
    whole = pl.BlockSpec((count, width), lambda i: (0, 0))
    now = lambda i: jnp.minimum(i, blocks - 1)
    past = lambda i: jnp.maximum(i - 1, 0)
    weights = []
    for at in (now, past):
        weights += [
            pl.BlockSpec((width, wide), lambda i, at=at: (0, at(i))),
            pl.BlockSpec((width, wide), lambda i, at=at: (0, blocks + at(i))),
            pl.BlockSpec((wide, width), lambda i, at=at: (at(i), 0)),
        ]
    return pl.pallas_call(
        feed_kernel,
        grid=(blocks + 1,),
        in_specs=[whole, whole, whole] + weights,
        out_specs=[
            pl.BlockSpec((count, wide), lambda i: (0, now(i))),
            pl.BlockSpec((2, count, wide), lambda i: (0, 0, now(i))),
            whole,
            whole,
        ],
        out_shape=[
            shape((count, hidden), BF),
            shape((2, count, hidden), BF),
            shape((count, width), BF),
            shape((count, width), F32),
        ],
        scratch_shapes=[pltpu.VMEM((count, width), F32), pltpu.VMEM((2, count, 3 * wide), BF)],
        compiler_params=pltpu.CompilerParams(
            dimension_semantics=("arbitrary",), vmem_limit_bytes=40 * 1024 * 1024
        ),
        cost_estimate=cost(25),
        name="feed_forward",
    )(*in_hbm(normed, cotangent, middle, pair, pair, down, pair, pair, down))


def scan_states(x):
    peers, d, width = x.shape
    return pl.pallas_call(
        partial(prefix_kernel, peers),
        out_shape=shape((peers, d, width - d), BF),
        cost_estimate=cost(3),
        name="state_prefix",
    )(x)


def scan_grads(x, g):
    peers, d, width = g.shape
    return pl.pallas_call(
        partial(suffix_kernel, peers),
        out_shape=shape((peers, d, width), BF),
        cost_estimate=cost(3),
        name="state_suffix",
    )(x, g)


def hold(value, *after):
    return lax.optimization_barrier((value, after))[0]


class Place:
    def __init__(self):
        self.nf, self.nr = lax.axis_size("fsdp"), lax.axis_size("rep")
        self.ny = self.nf // 4
        self.nx = self.nr // 2
        self.f, self.r = lax.axis_index("fsdp"), lax.axis_index("rep")
        z = self.f // self.ny
        self.mine = {"v": z // 2, "w": z % 2, "y": self.f % self.ny, "x": self.r // 2, "c": self.r % 2}
        self.number = {"v": 2, "w": 2, "u": 2, "y": self.ny, "x": self.nx, "c": 2}
        self.stride = {"v": 2 * self.ny, "w": self.ny, "y": 1, "x": 2, "c": 1}

    def send(self, value, way, steps=1):
        if way == "u":
            return lax.ppermute(value, "fsdp", [(i, i ^ 3 * self.ny) for i in range(self.nf)])
        axis = "rep" if way in "xc" else "fsdp"
        total = self.nr if way in "xc" else self.nf
        number, stride = self.number[way], self.stride[way]
        pairs = []
        for i in range(total):
            at = i // stride % number
            pairs.append((i, i + ((at + steps) % number - at) * stride))
        return lax.ppermute(value, axis, pairs)


def place_kernel(count, rows, each, by_rows, widths, offs_ref, own_ref, *refs):
    stacks, outs, sems = refs[: len(count)], refs[len(count) : -1], refs[-1]
    copies = []

    def put(src, row, height, column, out):
        copy = pltpu.make_async_copy(src, out.at[pl.ds(row, height), column], sems.at[len(copies)])
        copy.start()
        copies.append(copy)

    starts = [sum(widths[:i]) for i in range(len(widths))]
    top = pl.multiple_of(offs_ref[0], rows)
    for start, width, out in zip(starts, widths, outs):
        put(own_ref.at[:, pl.ds(start, width)], top, rows, pl.ds(0, width), out)
    at = 1
    for stack, number in zip(stacks, count):
        for j in range(number):
            row = pl.multiple_of(offs_ref[at], each if by_rows else rows)
            if by_rows:
                for start, width, out in zip(starts, widths, outs):
                    put(stack.at[j, :, pl.ds(start, width)], row, each, pl.ds(0, width), out)
                at += 1
            else:
                column = pl.multiple_of(offs_ref[at + 1], each)
                put(stack.at[j], row, rows, pl.ds(column, each), outs[0])
                at += 2
    for copy in copies:
        copy.wait()


class Gather:
    def __init__(self, here, shard, widths, deep, by_rows=True):
        self.here, self.shard, self.widths, self.deep, self.by_rows = here, shard, widths, deep, by_rows
        rows, total = shard.shape
        parts = here.nr if deep else 2
        extent = rows if by_rows else total
        self.each = extent // parts
        self.plain = bool(extent % parts or self.each % (32 if by_rows else 128) or rows % 32)
        self.plain = self.plain or here.ny != 2 or here.nx != 2
        self.have = {}
        if self.plain:
            return
        part = here.r if deep else here.mine["c"]
        self.have[""] = lax.dynamic_slice_in_dim(shard, part * self.each, self.each, 0 if by_rows else 1)

    def got(self, *names):
        return [] if self.plain else [self.have[name] for name in names]

    def move(self, *names, after=()):
        if not self.plain:
            for name in names:
                self.have[name] = self.here.send(hold(self.have[name[:-1]], *after), name[-1])

    def pile(self):
        if not self.plain:
            last = "u" if "u" in self.have else "vw"
            self.have["z"] = jnp.stack([self.have[name] for name in ("", "w", "v", last)])

    def place(self):
        here, shard, widths = self.here, self.shard, self.widths
        rows, each = shard.shape[0], self.each
        if self.plain:
            whole = lax.all_gather(shard, "fsdp", axis=0, tiled=True)
            starts = [sum(widths[:i]) for i in range(len(widths))]
            return [whole[:, s : s + w] for s, w in zip(starts, widths)]
        mine = here.mine
        offsets = [here.f * rows]
        names = [name for name in self.have if name.startswith("z")]
        for name in names:
            x, c, y = ((mine[way] + (way in name)) % 2 for way in "xcy")
            inside = (x * 2 + c if self.deep else c) * each
            for j in range(4):
                v = (mine["v"] + j // 2) % 2
                w = (mine["w"] + j % 2) % 2
                source = (v * 2 + w) * here.ny + y
                offsets += [source * rows + inside] if self.by_rows else [source * rows, inside]
        offsets = jnp.stack(offsets).astype(jnp.int32)
        stacks = [self.have[name] for name in names]
        count = [4] * len(stacks)
        any_space = pl.BlockSpec(memory_space=pl.ANY)
        size = here.nf * rows
        return pl.pallas_call(
            partial(place_kernel, count, rows, each, self.by_rows, widths),
            grid_spec=pltpu.PrefetchScalarGridSpec(
                num_scalar_prefetch=1,
                grid=(1,),
                in_specs=[any_space] * (1 + len(stacks)),
                out_specs=[pl.BlockSpec((size, w), lambda i, o: (0, 0)) for w in widths],
                scratch_shapes=[pltpu.SemaphoreType.DMA(((1 + sum(count)) * len(widths),))],
            ),
            out_shape=[jax.ShapeDtypeStruct((size, w), shard.dtype) for w in widths],
            compiler_params=pltpu.CompilerParams(
                vmem_limit_bytes=2 * size * sum(widths) * 2 + (1 << 20)
            ),
            cost_estimate=cost(6),
            name="place_weights",
        )(offsets, shard, *stacks)


class Reduce:
    def __init__(self, here):
        self.here = here
        self.split = False

    def swap(self, away):
        self.away = away.astype(BF)
        self.came = self.here.send(self.away, "c")

    def take(self, part):
        self.begin(part + self.came.astype(F32))

    def begin(self, part):
        part = part.astype(BF)
        here = self.here
        rows = part.shape[0] // here.nf
        self.part = part.reshape(2, 2, here.ny, rows, part.shape[1])
        self.axes = ["v", "w", "y"]

    def go(self, way, *after):
        here = self.here
        part = hold(self.part, *after)
        number, mine = here.number[way], here.mine[way]
        if way in "xc" and not self.axes:
            self.total = part.astype(F32)
            self.outs = [part] * (number - 1)
        else:
            if way == "x":
                axis = len(self.axes)
                shape = part.shape
                part = part.reshape(
                    shape[:axis] + (number, shape[axis] // number) + shape[axis + 1 :]
                )
                self.split = True
            else:
                axis = self.axes.index(way)
                self.axes.pop(axis)
            self.total = lax.dynamic_index_in_dim(part, mine, axis, keepdims=False).astype(F32)
            self.outs = [
                lax.dynamic_index_in_dim(part, (mine + s) % number, axis, keepdims=False)
                for s in range(1, number)
            ]
        self.got = [here.send(out, way, s) for s, out in zip(range(1, number), self.outs)]

    def begin_x(self, part, *after):
        self.part, self.axes = part, []
        self.go("x", *after)

    def two(self, at):
        first, second = Reduce(self.here), Reduce(self.here)
        for one, cut in ((first, slice(0, at)), (second, slice(at, None))):
            one.part, one.axes = self.part[..., cut], list(self.axes)
        return first, second

    def join(self, first, second):
        self.part = jnp.concatenate([first.part, second.part], axis=-1)
        self.axes, self.split = list(first.axes), True

    def both(self):
        self.total = self.part.astype(F32)
        self.got = [self.here.send(self.part, "c")]

    def end(self):
        total = self.total
        for came in self.got:
            total = total + came.astype(F32)
        self.part = total.astype(BF)

    def step(self, way, *after):
        self.go(way, *after)
        self.end()

    def rows(self):
        if self.split:
            self.part = join_way(self.here, self.part, "x", 0)

    def other(self):
        return self.here.send(self.part, "c")


def meet(value, *sums):
    value, came = lax.optimization_barrier((value, [one.got for one in sums]))
    for one, got in zip(sums, came):
        one.got = got
        one.end()
    return value


def join_way(here, array, way, axis):
    number, mine = here.number[way], here.mine[way]
    got = [array] + [here.send(array, way, s) for s in range(1, number)]
    if number == 2:
        ahead = jnp.concatenate(got, axis=axis)
        behind = jnp.concatenate(got[::-1], axis=axis)
        return jnp.where(mine == 0, ahead, behind)
    stack = jnp.stack(got)
    order = (mine - jnp.arange(number)) % number
    stack = jnp.take(stack, order, axis=0)
    return jnp.concatenate([stack[i] for i in range(number)], axis=axis)


def gather_apart(here, shard):
    rows = shard.shape[0] // here.nr
    piece = lax.dynamic_slice_in_dim(shard, here.r * rows, rows, 0)
    return lax.all_gather(piece, ("fsdp", "rep"), axis=0, tiled=True)


def scatter_owners(array):
    return lax.psum_scatter(array, "fsdp", scatter_dimension=0, tiled=True)


def sum_x(here, array, *after):
    array = hold(array, *after)
    total = array.astype(F32)
    for s in range(1, here.nx):
        total = total + here.send(array, "x", s).astype(F32)
    return total.astype(BF)


def contract(left, right, left_dim, right_dim):
    return lax.dot_general(
        left, right, (((left_dim,), (right_dim,)), ((), ())), preferred_element_type=F32
    )


def rms_norm(values, gain):
    return values * lax.rsqrt(jnp.mean(values * values, axis=-1, keepdims=True) + EPSILON) * gain


def kv_order(array):
    eighth = array.shape[1] // 24
    starts, sizes = (8, 16, 14, 22), (6, 6, 2, 2)
    return [array[:, i * eighth : (i + n) * eighth] for i, n in zip(starts, sizes)]


def from_behind(value, steps):
    count = lax.axis_size("fsdp")
    first, last = (max(0, -steps), min(count, count - steps))
    return lax.ppermute(value, "fsdp", [(source, source + steps) for source in range(first, last)])


def to_owners(parts, fanout):
    heads, d, width = parts.shape
    cut = parts.reshape(heads, d, fanout, width // fanout)
    return jnp.swapaxes(cut, 1, 2).reshape(heads * fanout, d, width // fanout)


def to_heads(parts, fanout):
    owners, d, width = parts.shape
    cut = parts.reshape(owners // fanout, fanout, d, width)
    return jnp.swapaxes(cut, 1, 2).reshape(owners // fanout, d, width * fanout)


def swap(value):
    return lax.all_to_all(value, "fsdp", 0, 0, tiled=True)


def by_core(here, for_zero, for_one):
    return jnp.where(here.mine["c"] == 0, for_zero, for_one)


def on_device(
    hidden_in,
    seg_ids,
    attn_gain,
    qkv_weight,
    beta_weight,
    gate_weight,
    conv_taps,
    out_gain,
    out_weight,
    ffn_gain,
    ffn_gate,
    ffn_up,
    ffn_down,
    cotangent,
):
    here = Place()
    row_count, width = hidden_in.shape
    heads = beta_weight.shape[1]
    head_dim = width // heads
    blocks = row_count // SPAN
    rim = 8
    lanes = 128
    hidden_units = ffn_gate.shape[1]

    numbers = seg_ids + 1

    small = [attn_gain, out_gain, ffn_gain, conv_taps]
    shard_rows = qkv_weight.shape[0]
    flat = jnp.concatenate([a.reshape(-1) for a in small])
    columns = -(-flat.size // shard_rows)
    flat = jnp.pad(flat, (0, columns * shard_rows - flat.size)).reshape(shard_rows, columns)
    extra = jnp.concatenate(
        [beta_weight, flat, jnp.zeros((shard_rows, lanes - heads - columns), BF)], axis=1
    )
    first = Gather(
        here,
        jnp.concatenate(kv_order(qkv_weight) + [extra], axis=1),
        [2 * width, lanes],
        True,
    )
    second = Gather(
        here,
        jnp.concatenate([qkv_weight[:, :width], gate_weight, out_weight], axis=1),
        [2 * width, width],
        True,
    )
    rim_rows = from_behind(hidden_in[row_count - rim :], 1)
    rim_ids = from_behind(numbers[row_count - rim :], 1)
    pair_full = gather_apart(here, jnp.concatenate([ffn_gate, ffn_up], axis=1))
    first.move("v", "w")
    first.move("vw")
    first.pile()
    if not first.plain:
        first.have["z"], rim_rows, rim_ids = lax.optimization_barrier((first.have["z"], rim_rows, rim_ids))
    first.move("zy", "zx")
    first.move("zc")
    second.move("v", "w", after=first.got("z"))
    first.move("zyx", after=first.got("zx", "zc"))
    first.move("zyc", "zxc")
    first.move("zyxc", after=first.got("zyc", "zxc"))
    kv_full, extra_full = first.place()

    small_full = extra_full[:, heads : heads + columns].reshape(here.nf, -1)
    cuts, at = [], 0
    for array in small:
        cuts.append(small_full[:, at : at + array.size].astype(F32))
        at += array.size
    attn_scale = cuts[0].reshape(-1)
    outgain_scale = cuts[1].reshape(1, -1)
    ffngain_scale = cuts[2].reshape(-1)
    taps_count = conv_taps.shape[0]
    taps_scale = jnp.swapaxes(cuts[3].reshape(here.nf, taps_count, -1), 0, 1).reshape(taps_count, -1)
    query_taps = taps_scale[:, :width]
    kv_taps = jnp.concatenate(kv_order(taps_scale), axis=1)
    residual = hidden_in.astype(F32)
    extended_in = jnp.concatenate([hidden_in, rim_rows]).astype(F32)
    normed_ext = rms_norm(extended_in, attn_scale).astype(BF)
    normed_low = normed_ext[:row_count]
    kv_pre = jnp.dot(normed_ext, kv_full, preferred_element_type=F32)
    second.move("vw", after=[kv_full])
    second.pile()
    kv_pre = hold(kv_pre, second.got("z"))
    second.move("zy", "zx", after=[kv_pre])
    beta_pre = jnp.dot(normed_low, extra_full, preferred_element_type=F32)[:, :heads]
    rates = jax.nn.sigmoid(beta_pre)
    ids = jnp.concatenate([rim_ids, numbers]).astype(F32)
    own_ids = numbers.astype(F32)
    before = ids[rim - 1 : rim - 1 + row_count : SPAN]
    cols = jnp.concatenate(
        [rates, own_ids[:, None]]
        + [(ids[rim - j : rim - j + row_count] == own_ids).astype(F32)[:, None] for j in (1, 2, 3)]
        + [jnp.zeros((row_count, heads - 4), F32)],
        1,
    )
    rows = jnp.concatenate(
        [
            jnp.swapaxes(rates.reshape(blocks, SPAN, heads), 1, 2),
            own_ids.reshape(blocks, 1, SPAN),
            jnp.broadcast_to(before[:, None, None], (blocks, 1, SPAN)),
            jnp.zeros((blocks, heads - 2, SPAN), F32),
        ],
        1,
    )
    key_low, value_low, kv_mixed, w, u, a, moves = delta_summary(kv_pre, kv_taps, cols, rows, heads)
    moves = hold(moves, second.got("zy", "zx"))
    down_full = gather_apart(here, hold(ffn_down, pair_full, moves))
    second.move("zyx", after=[moves] + second.got("zx"))
    second.move("zc", "zyc", "zxc", after=[moves])
    fanout = here.nf // heads
    if fanout > 1:
        moves = jnp.concatenate(
            [
                to_owners(moves[:, :, :head_dim], fanout),
                jnp.repeat(moves[:, :, head_dim:], fanout, axis=0),
            ],
            axis=2,
        )
    owned = swap(moves)
    states = scan_states(owned)
    second.move("zyxc", after=[states])
    entry = swap(states)
    qg_full, outw_full = second.place()
    qg_pre = jnp.dot(normed_ext, qg_full, preferred_element_type=F32)
    if fanout > 1:
        entry = to_heads(entry, fanout)
    query_low, q_mixed, gated_low, attn_heads, fresh, kept = delta_forward(
        qg_pre, query_taps, key_low, w, u, cols, rows, entry, outgain_scale, heads
    )
    middle = residual + jnp.dot(gated_low, outw_full, preferred_element_type=F32)
    normed_two, norm_two_back = jax.vjp(partial(rms_norm, gain=ffngain_scale), middle)
    normed_two_low = normed_two.astype(BF)
    hidden_low, pair_low, output, normed_two_grad = feed_forward(
        normed_two_low, cotangent, middle, pair_full, down_full
    )

    c = here.mine["c"]

    def shares(array, start, size):
        half = size // 2
        cut = [lax.dynamic_slice_in_dim(array, start + at * half, half, 1) for at in (1 - c, c)]
        return cut

    theirs, ours = shares(cotangent, 0, width)
    down_sum = Reduce(here)
    down_sum.swap(contract(hidden_low, theirs, 0, 0))
    theirs, ours = [lax.dynamic_index_in_dim(pair_low, at, 0, keepdims=False) for at in (1 - c, c)]
    pair_sum = Reduce(here)
    pair_sum.swap(contract(normed_two_low, theirs, 0, 0))
    down_theirs, down_ours = shares(cotangent, 0, width)
    down_sum = Reduce(here)
    down_sum.swap(contract(hidden_low, down_theirs, 0, 0))
    (middle_back,) = norm_two_back(normed_two_grad)
    middle_grad = cotangent.astype(F32) + middle_back
    middle_low = middle_grad.astype(BF)
    gated_grad = contract(middle_low, outw_full, 1, 1)
    ours = hold(ours, down_sum.away)
    pair_half = (contract(normed_two_low, ours, 0, 0) + pair_sum.came.astype(F32)).astype(BF)
    pair_apart = scatter_owners(pair_half)
    gated_grad = hold(gated_grad, pair_half)
    heads_grad, gatepre_low, outgain_grad, local_later = delta_adjoint(
        query_low, key_low, w, cols, rows, gated_grad, attn_heads, qg_pre, outgain_scale, heads
    )
    if fanout > 1:
        local_later = to_owners(local_later, fanout)
    came_later = swap(local_later)
    down_sum.take(contract(hidden_low, hold(down_ours, local_later), 0, 0))
    down_sum.go("x")

    middle_held, gatepre_held = hold((middle_low, gatepre_low), local_later)
    out_grad = contract(gated_low, middle_held, 0, 0)
    gate_grad = contract(normed_low, gatepre_held, 0, 0)
    other_sum = Reduce(here)
    other_sum.swap(by_core(here, gate_grad, out_grad))
    came_later = hold(came_later, other_sum.away, *down_sum.outs)
    summed_later = scan_grads(owned, came_later)
    later = swap(summed_later)
    if fanout > 1:
        later = to_heads(later, fanout)
    other_sum.take(by_core(here, out_grad, gate_grad))
    later = meet(hold(later, other_sum.part), down_sum)
    down_apart = scatter_owners(down_sum.part.reshape(-1, width // 2))
    other_x, other_y = other_sum.two(width // 2)
    other_x.go("x", later)
    other_y.go("y", later)
    later = hold(later, *other_x.outs, *other_y.outs)
    state = (query_low, key_low, value_low, w, u, a, fresh, kept, heads_grad, cols, rows)
    mixed_a, beta_a, taps_a = delta_backward(
        0, *state, later, q_mixed, qg_pre, query_taps, kv_mixed, kv_pre, kv_taps, heads
    )
    mixed_a = meet(mixed_a, other_x, other_y)
    other_x.go("y")
    other_y.go("x")
    a_sum = Reduce(here)
    cut = [number * head_dim for number in head_parts(heads)]
    theirs, ours = shares(mixed_a, 0, 3 * cut[0])
    a_sum.swap(contract(normed_ext, theirs, 0, 0))
    a_sum.take(contract(normed_ext, ours, 0, 0))
    later = meet(hold(later, a_sum.part), other_x, other_y)
    other_sum.join(other_x, other_y)
    a_x, a_y = a_sum.two((a_sum.part.shape[-1] // lanes + 1) // 2 * lanes)
    a_x.go("x", later)
    a_y.go("y", later)
    other_sum.go("w", later)
    later = hold(later, *a_x.outs, *a_y.outs, *other_sum.outs)
    mixed_b, beta_b, taps_b = delta_backward(
        1, *state, later, q_mixed, qg_pre, query_taps, kv_mixed, kv_pre, kv_taps, heads
    )
    mixed_b = hold(meet(mixed_b, other_sum, a_x, a_y), pair_apart)
    a_x.go("y")
    a_y.go("x")
    b_sum = Reduce(here)
    theirs, ours = shares(mixed_b, 0, 3 * cut[1])
    b_sum.swap(contract(normed_ext, theirs, 0, 0))
    taps_b, beta_b = hold((taps_b, beta_b), b_sum.away)

    def by_kind(first_heads, other_heads):
        pieces = []
        for i in range(3):
            for array, wide in zip((first_heads, other_heads), cut):
                pieces.append(array[:, i * wide : (i + 1) * wide])
        return jnp.concatenate(pieces, axis=1)

    betapre_low = (beta_a + beta_b).astype(BF)
    taps_grad = by_kind(taps_a, taps_b)
    parts = (
        outgain_grad.reshape(here.nf, -1),
        jnp.swapaxes(taps_grad.reshape(taps_count, here.nf, -1), 0, 1).reshape(here.nf, -1),
    )
    flat = jnp.concatenate(parts, axis=1)
    flat = jnp.pad(flat, ((0, 0), (0, columns * shard_rows - flat.shape[1])))
    extra = jnp.pad(flat.reshape(width, columns), ((0, 0), (heads, lanes - heads - columns)))
    small_sum = Reduce(here)
    small_sum.begin(contract(normed_low, hold(betapre_low, mixed_b), 0, 0) + extra)
    small_sum.both()
    b_sum.take(contract(normed_ext, ours, 0, 0))
    small_sum.end()
    mixed_b = hold(mixed_b, b_sum.part, small_sum.part)
    b_sum.go("x")
    small_sum.go("x")
    wide_grad = (
        contract(mixed_a[:, cut[0] :], kv_full[:, : 2 * cut[0]], 1, 1)
        + contract(mixed_b[:, cut[1] :], kv_full[:, 2 * cut[0] :], 1, 1)
        + contract(mixed_a[:, : cut[0]], qg_full[:, : cut[0]], 1, 1)
        + contract(mixed_b[:, : cut[1]], qg_full[:, cut[0] : width], 1, 1)
    )
    rim_grad = from_behind(wide_grad[row_count:].astype(BF), -1).astype(F32)
    normed_grad = (
        wide_grad[:row_count]
        + jnp.pad(rim_grad, ((row_count - rim, 0), (0, 0)))
        + contract(betapre_low, extra_full, 1, 1)
        + contract(gatepre_low, qg_full[:, width:], 1, 1)
    )
    normed_grad = meet(normed_grad, b_sum, a_x, a_y, small_sum)
    other_sum.go("v", normed_grad)
    a_sum.join(a_x, a_y)
    b_sum.go("y")
    small_sum.go("y")
    pair_sum.begin_x(pair_apart, normed_grad)
    a_sum.go("w")
    (input_back,) = jax.vjp(partial(rms_norm, gain=attn_scale), residual)[1](normed_grad)
    input_grad = meet(
        (middle_grad + input_back).astype(BF), b_sum, a_sum, other_sum, small_sum, pair_sum
    )
    b_sum.go("w", input_grad)
    a_sum.go("v", input_grad)
    small_sum.go("w", input_grad)
    def gain_grad(gain, pairs):
        total = sum(jnp.sum(weight.astype(F32) * grad, axis=1) for weight, grad in pairs)
        return total / gain.astype(F32)

    other = here.send(pair_sum.part, "c")
    hidgate_total = by_core(here, pair_sum.part, other).astype(F32)
    hidup_total = by_core(here, other, pair_sum.part).astype(F32)
    ffngain_total = gain_grad(ffn_gain, ((ffn_gate, hidgate_total), (ffn_up, hidup_total)))
    hidgate_total, hidup_total, ffngain_total = meet(
        (hidgate_total, hidup_total, ffngain_total), b_sum, a_sum, small_sum
    )
    b_sum.go("v", a_sum.part)
    small_sum.go("v", a_sum.part)
    held = meet(a_sum.part, b_sum, small_sum)
    both = Reduce(here)
    both.part = jnp.concatenate([b_sum.part, held, other_sum.part, small_sum.part], axis=1)
    both.split = True
    both.rows()
    down_sum.part = hold(down_apart, held)
    down_sum.rows()
    down_total = join_way(here, down_sum.part, "c", 1).astype(F32)
    whole = both.other()
    ends = [0]
    for one in (b_sum, a_sum, other_sum, small_sum):
        ends.append(ends[-1] + one.part.shape[1])

    def joined(start, end):
        mine, theirs = both.part[:, start:end], whole[:, start:end]
        return by_core(here, mine, theirs), by_core(here, theirs, mine)

    b_both, a_both, other_both = [joined(*pair) for pair in zip(ends[:3], ends[1:4])]
    outproj_total, gate_total = [part.astype(F32) for part in other_both]
    qkv_total = by_kind(jnp.concatenate(a_both, axis=1), jnp.concatenate(b_both, axis=1)).astype(F32)
    extra = both.part[:, ends[3] :].astype(F32)
    beta_total = extra[:, :heads]

    attngain_total = gain_grad(
        attn_gain, ((qkv_weight, qkv_total), (beta_weight, beta_total), (gate_weight, gate_total))
    )
    flat = extra[:, heads : heads + columns].reshape(-1)
    cut, at = [], 0
    for part in parts:
        cut.append(flat[at : at + part.shape[1]])
        at += part.shape[1]
    return (
        output,
        input_grad,
        attngain_total,
        qkv_total,
        beta_total,
        gate_total,
        cut[1].reshape(conv_taps.shape),
        cut[0],
        outproj_total,
        ffngain_total,
        hidgate_total,
        hidup_total,
        down_total,
    )


def solution(mesh):
    placed = (
        P(("rep", "fsdp"), None),
        P(("rep", "fsdp")),
        P("fsdp"),
        P("fsdp", None),
        P("fsdp", None),
        P("fsdp", None),
        P(None, "fsdp"),
        P("fsdp"),
        P("fsdp", None),
        P("fsdp"),
        P("fsdp", None),
        P("fsdp", None),
        P("fsdp", None),
        P(("rep", "fsdp"), None),
    )
    return jax.shard_map(
        on_device,
        mesh=mesh,
        in_specs=placed,
        out_specs=(
            P(("rep", "fsdp"), None),
            P(("rep", "fsdp"), None),
            P("fsdp"),
            P("fsdp", None),
            P("fsdp", None),
            P("fsdp", None),
            P(None, "fsdp"),
            P("fsdp"),
            P("fsdp", None),
            P("fsdp"),
            P("fsdp", None),
            P("fsdp", None),
            P("fsdp", None),
        ),
        check_vma=False,
    )
```
